512 devices in a mesh: row: 16 (over z_hi, y, core), col: 32 (over z_lo, x).
Axes of the slice: x: 4, y: 4, z: 16 (z_hi: 2, z_lo: 8; z = z_hi * 8 + z_lo), core: 2. Of those that a mesh axis runs over, the one named last changes fastest.
Arguments:
- amplitudes: bfloat16 [8192, 4096], P('row', 'col'), may hold values from -6 to 6
- packed_tiles: bfloat16 [16, 512, 128, 128], P('row', 'col'), may hold values from -0.09375 to 0.09375
- tile_ids: int32 [16, 512], P('row', 'col'), may hold values from 0 to 511, as said below
- residual_in: float32 [8192, 32768], P('row', 'col'), may hold values from -6 to 6
Outputs:
- ladder: float32 [8192, 32768], P('row', 'col')
The draws below stay inside these ranges and needn't reach their ends.
Inputs may be any that keep to these rules, and one draw needn't show every extreme that they name: `tile_ids`: in each grid row the ids are a permutation of 0 to 511; no device holds more than 1 ids of one value of id // 16, and some device holds exactly 1.
All inputs are finite; a program needn't handle non-finite values.
Results may differ from the reference program's by a relative error of at most 0.0003.
Values may be sent and summed in bfloat16 or wider, within the bound.
A program may use at most 64 MiB of HBM per device.

```python
import jax
import jax.numpy as jnp

TILE = 128
KT_DEV = 2
QT_DEV = 8
TILES_DEV = 16
KDIM = 4096
QDIM = 32768
PAIRS = 8192
N_ROW = 16
N_COL = 32


def draw_tile_ids(key, part):
    total = N_COL * TILES_DEV

    def one_row(row_key):
        key_perm, key_pos, key_mix = jax.random.split(row_key, 3)
        source_perm = jax.random.permutation(key_perm, N_COL)
        dest_col = jnp.repeat(jnp.arange(N_COL), TILES_DEV)
        serial = jnp.tile(jnp.arange(TILES_DEV), N_COL)
        local_pos = jax.vmap(lambda sub_key: jax.random.permutation(sub_key, TILES_DEV))(jax.random.split(key_pos, N_COL)).reshape(-1)
        source = source_perm[(dest_col + serial) % N_COL]
        identity = dest_col * TILES_DEV + local_pos
        shuffle = jax.random.permutation(key_mix, total)
        scores = source * total + shuffle
        ordering = jnp.argsort(scores, stable=True)
        return identity[ordering]
    return jax.vmap(one_row)(jax.random.split(key, N_ROW)).astype(jnp.int32)


def shard_levels(own_key, extent, pieces, smallest, top_value):
    level = 1.0
    for dim, parts in pieces:
        draws = jax.random.uniform(jax.random.fold_in(jax.random.fold_in(own_key, 6), dim), (parts,), jnp.float32, smallest / len(pieces), top_value / len(pieces))
        level = level * jnp.repeat(jnp.exp(draws), extent[dim] // parts).reshape((-1,) + (1,) * (len(extent) - 1 - dim))
    return level


def noise(rng, extent, spread, bound, shards=(), held_as=jnp.bfloat16):
    loudness = shard_levels(rng, extent, shards, -0.22, 0.18) if shards else 1.0
    result = jax.random.normal(rng, extent, jnp.float32) * spread * loudness
    return jnp.minimum(jnp.maximum(result, -bound), bound).astype(held_as)


def setup_inputs(seed: int = 0) -> dict:
    arg_keys = jax.random.split(jax.random.key(seed), 5)
    amplitudes = noise(arg_keys[0], (PAIRS, KDIM), 1.0, 6.0, ((0, 16), (1, 32)))
    packed_tiles = noise(arg_keys[1], (N_ROW, N_COL * TILES_DEV, TILE, TILE), KDIM ** -0.5, 0.09375, ((0, 16), (1, 32)))
    tile_ids = draw_tile_ids(jax.random.fold_in(arg_keys[4], 71), 0)
    residual_in = noise(arg_keys[3], (PAIRS, QDIM), 1.0, 6.0, ((0, 16), (1, 32)), jnp.float32)
    return dict(amplitudes=amplitudes, packed_tiles=packed_tiles, tile_ids=tile_ids, residual_in=residual_in)


def reference(amplitudes, packed_tiles, tile_ids, residual_in):
    ordering = jnp.argsort(tile_ids, axis=1)
    arranged = jnp.take_along_axis(packed_tiles, ordering[:, :, None, None], axis=1)
    arranged = arranged.reshape(N_ROW, N_COL, KT_DEV, QT_DEV, TILE, TILE)
    arranged = arranged.transpose(0, 2, 4, 1, 3, 5).reshape(KDIM, QDIM)
    product = jnp.dot(amplitudes, arranged, preferred_element_type=jnp.float32)
    return residual_in + product
```

```python
import jax
import jax.numpy as jnp
from jax import lax
from jax.sharding import Mesh
from jax.sharding import PartitionSpec as P

ROW_AXES = ("z_hi", "y", "core")
COL_AXES = ("z_lo", "x")
ROW_SPLIT = (2, 4, 2)
COL_SPLIT = (8, 4)


def body(amplitudes, packed_tiles, tile_ids, residual_in):
    per_device = packed_tiles.shape[1]
    tile = packed_tiles.shape[2]
    col_count = COL_SPLIT[0] * COL_SPLIT[1]
    own_ids = tile_ids[0]
    target_col = own_ids // per_device
    position = own_ids % per_device
    chooser = (jnp.arange(col_count)[:, None] == target_col[None, :]).astype(jnp.bfloat16)
    tag_rows = jnp.broadcast_to(
        (position + 1).astype(jnp.bfloat16)[:, None, None], (per_device, 16, tile)
    )
    tagged = jnp.concatenate([packed_tiles[0], tag_rows], axis=1)
    outgoing = jnp.einsum("sl,lij->sij", chooser, tagged, preferred_element_type=jnp.float32)
    outgoing = outgoing.astype(jnp.bfloat16)
    incoming = lax.all_to_all(outgoing, COL_AXES, split_axis=0, concat_axis=0, tiled=True)
    tags = incoming[:, tile, 0].astype(jnp.float32)
    unpack = (
        (jnp.arange(per_device, dtype=jnp.float32)[:, None] + 1.0) == tags[None, :]
    ).astype(jnp.bfloat16)
    unpacked = jnp.einsum(
        "ps,sij->pij", unpack, incoming[:, :tile, :], preferred_element_type=jnp.float32
    ).astype(jnp.bfloat16)
    kt = 2
    qt = per_device // kt
    block = unpacked.reshape(kt, qt, tile, tile).transpose(0, 2, 1, 3).reshape(kt, tile, qt * tile)
    g = lax.all_gather(block, "z_hi")
    g = lax.all_gather(g, "y")
    g = lax.all_gather(g, "core")
    a = lax.all_gather(amplitudes, "z_lo")
    a = lax.all_gather(a, "x")
    a = a.reshape(2, 2, 2, 4, a.shape[2], a.shape[3])
    product = jnp.einsum("ckhypj,cyhkjn->pn", a, g, preferred_element_type=jnp.float32)
    return residual_in + product


def solution(mesh):
    devices = mesh.devices.reshape(ROW_SPLIT + COL_SPLIT)
    fine = Mesh(devices, ROW_AXES + COL_AXES)
    row, col = ROW_AXES, COL_AXES
    in_specs = (P(row, col), P(row, col, None, None), P(row, col), P(row, col))
    out_specs = P(row, col)
    return jax.shard_map(body, mesh=fine, in_specs=in_specs, out_specs=out_specs, check_vma=False)
```

```python
import functools

import jax
import jax.numpy as jnp
from jax import lax
from jax.experimental import pallas as pl
from jax.experimental.pallas import tpu as pltpu
from jax.sharding import Mesh
from jax.sharding import PartitionSpec as P

ROW_AXES = ("z_hi", "y", "core")
COL_AXES = ("z_lo", "x")
ROW_SPLIT = (2, 4, 2)
COL_SPLIT = (8, 4)
MESH = pl.DeviceIdType.MESH


def gather_kernel(axis, n, x_ref, o_ref, send_sem, recv_sem, local_sem):
    me = lax.axis_index(axis)
    barrier = pltpu.get_barrier_semaphore()
    for j in range(1, n):
        peer = lax.rem(me + j, n)
        pl.semaphore_signal(barrier, inc=1, device_id={axis: peer}, device_id_type=MESH)
    pl.semaphore_wait(barrier, n - 1)
    local = pltpu.make_async_copy(x_ref, o_ref.at[me], local_sem)
    local.start()
    copies = []
    for j in range(1, n):
        peer = lax.rem(me + j, n)
        copy = pltpu.make_async_remote_copy(
            src_ref=x_ref,
            dst_ref=o_ref.at[me],
            send_sem=send_sem.at[j],
            recv_sem=recv_sem.at[j],
            device_id={axis: peer},
            device_id_type=MESH,
        )
        copy.start()
        copies.append(copy)
    local.wait()
    for copy in copies:
        copy.wait()


def gather(x, axis, n, cid):
    nbytes = x.size * x.dtype.itemsize
    return pl.pallas_call(
        functools.partial(gather_kernel, axis, n),
        out_shape=jax.ShapeDtypeStruct((n,) + x.shape, x.dtype),
        in_specs=[pl.BlockSpec(memory_space=pl.ANY)],
        out_specs=pl.BlockSpec(memory_space=pl.ANY),
        scratch_shapes=[
            pltpu.SemaphoreType.DMA((n,)),
            pltpu.SemaphoreType.DMA((n,)),
            pltpu.SemaphoreType.DMA(()),
        ],
        compiler_params=pltpu.CompilerParams(collective_id=cid, has_side_effects=True),
        cost_estimate=pl.CostEstimate(flops=0, transcendentals=0, bytes_accessed=2 * n * nbytes),
        name=f"gather_{axis}",
    )(x)


def body(amplitudes, packed_tiles, tile_ids, residual_in):
    per_device = packed_tiles.shape[1]
    tile = packed_tiles.shape[2]
    col_count = COL_SPLIT[0] * COL_SPLIT[1]
    own_ids = tile_ids[0]
    target_col = own_ids // per_device
    position = own_ids % per_device
    chooser = (jnp.arange(col_count)[:, None] == target_col[None, :]).astype(jnp.bfloat16)
    tag_rows = jnp.broadcast_to(
        (position + 1).astype(jnp.bfloat16)[:, None, None], (per_device, 16, tile)
    )
    tagged = jnp.concatenate([packed_tiles[0], tag_rows], axis=1)
    outgoing = jnp.einsum("sl,lij->sij", chooser, tagged, preferred_element_type=jnp.float32)
    outgoing = outgoing.astype(jnp.bfloat16)
    incoming = lax.all_to_all(outgoing, COL_AXES, split_axis=0, concat_axis=0, tiled=True)
    tags = incoming[:, tile, 0].astype(jnp.float32)
    unpack = (
        (jnp.arange(per_device, dtype=jnp.float32)[:, None] + 1.0) == tags[None, :]
    ).astype(jnp.bfloat16)
    unpacked = jnp.einsum(
        "ps,sij->pij", unpack, incoming[:, :tile, :], preferred_element_type=jnp.float32
    ).astype(jnp.bfloat16)
    kt = 2
    qt = per_device // kt
    block = unpacked.reshape(kt, qt, tile, tile).transpose(0, 2, 1, 3).reshape(kt, tile, qt * tile)
    g = gather(block, "z_hi", ROW_SPLIT[0], 0)
    g = gather(g, "y", ROW_SPLIT[1], 1)
    g = gather(g, "core", ROW_SPLIT[2], 2)
    a = gather(amplitudes, "z_lo", COL_SPLIT[0], 3)
    a = gather(a, "x", COL_SPLIT[1], 4)
    a = a.reshape(2, 2, 2, 4, a.shape[2], a.shape[3])
    product = jnp.einsum("ckhypj,cyhkjn->pn", a, g, preferred_element_type=jnp.float32)
    return residual_in + product


def solution(mesh):
    devices = mesh.devices.reshape(ROW_SPLIT + COL_SPLIT)
    fine = Mesh(devices, ROW_AXES + COL_AXES)
    row, col = ROW_AXES, COL_AXES
    in_specs = (P(row, col), P(row, col, None, None), P(row, col), P(row, col))
    out_specs = P(row, col)
    return jax.shard_map(body, mesh=fine, in_specs=in_specs, out_specs=out_specs, check_vma=False)
```

```python
import functools

import jax
import jax.numpy as jnp
from jax import lax
from jax.experimental import pallas as pl
from jax.experimental.pallas import tpu as pltpu
from jax.sharding import Mesh
from jax.sharding import PartitionSpec as P

ROW_AXES = ("z_hi", "y", "core")
COL_AXES = ("z_lo", "x")
ROW_SPLIT = (2, 4, 2)
COL_SPLIT = (8, 4)
MESH = pl.DeviceIdType.MESH


def gather_kernel(axis, n, x_ref, o_ref, send_sem, recv_sem):
    me = lax.axis_index(axis)
    barrier = pltpu.get_barrier_semaphore()
    for j in range(1, n):
        peer = lax.rem(me + j, n)
        pl.semaphore_signal(barrier, inc=1, device_id={axis: peer}, device_id_type=MESH)
    pl.semaphore_wait(barrier, n - 1)
    copies = []
    for j in range(1, n):
        peer = lax.rem(me + j, n)
        copy = pltpu.make_async_remote_copy(
            src_ref=x_ref,
            dst_ref=o_ref.at[me],
            send_sem=send_sem.at[j],
            recv_sem=recv_sem.at[j],
            device_id={axis: peer},
            device_id_type=MESH,
        )
        copy.start()
        copies.append(copy)
    for copy in copies:
        copy.wait()


def gather(x, axis, n, cid):
    nbytes = x.size * x.dtype.itemsize
    out = pl.pallas_call(
        functools.partial(gather_kernel, axis, n),
        out_shape=jax.ShapeDtypeStruct((n,) + x.shape, x.dtype),
        in_specs=[pl.BlockSpec(memory_space=pl.ANY)],
        out_specs=pl.BlockSpec(memory_space=pl.ANY),
        scratch_shapes=[
            pltpu.SemaphoreType.DMA((n,)),
            pltpu.SemaphoreType.DMA((n,)),
        ],
        compiler_params=pltpu.CompilerParams(collective_id=cid, has_side_effects=True),
        cost_estimate=pl.CostEstimate(flops=0, transcendentals=0, bytes_accessed=2 * n * nbytes),
        name=f"gather_{axis}",
    )(x)
    return lax.dynamic_update_slice_in_dim(out, x[None], lax.axis_index(axis), axis=0)


def body(amplitudes, packed_tiles, tile_ids, residual_in):
    per_device = packed_tiles.shape[1]
    tile = packed_tiles.shape[2]
    col_count = COL_SPLIT[0] * COL_SPLIT[1]
    own_ids = tile_ids[0]
    target_col = own_ids // per_device
    position = own_ids % per_device
    chooser = (jnp.arange(col_count)[:, None] == target_col[None, :]).astype(jnp.bfloat16)
    tag_rows = jnp.broadcast_to(
        (position + 1).astype(jnp.bfloat16)[:, None, None], (per_device, 16, tile)
    )
    tagged = jnp.concatenate([packed_tiles[0], tag_rows], axis=1)
    outgoing = jnp.einsum("sl,lij->sij", chooser, tagged, preferred_element_type=jnp.float32)
    outgoing = outgoing.astype(jnp.bfloat16)
    incoming = lax.all_to_all(outgoing, COL_AXES, split_axis=0, concat_axis=0, tiled=True)
    tags = incoming[:, tile, 0].astype(jnp.float32)
    unpack = (
        (jnp.arange(per_device, dtype=jnp.float32)[:, None] + 1.0) == tags[None, :]
    ).astype(jnp.bfloat16)
    unpacked = jnp.einsum(
        "ps,sij->pij", unpack, incoming[:, :tile, :], preferred_element_type=jnp.float32
    ).astype(jnp.bfloat16)
    kt = 2
    qt = per_device // kt
    block = unpacked.reshape(kt, qt, tile, tile).transpose(0, 2, 1, 3).reshape(kt, tile, qt * tile)
    g = gather(block, "z_hi", ROW_SPLIT[0], 0)
    g = gather(g, "y", ROW_SPLIT[1], 1)
    g = gather(g, "core", ROW_SPLIT[2], 2)
    a = gather(amplitudes, "z_lo", COL_SPLIT[0], 3)
    a = gather(a, "x", COL_SPLIT[1], 4)
    a = a.reshape(2, 2, 2, 4, a.shape[2], a.shape[3])
    product = jnp.einsum("ckhypj,cyhkjn->pn", a, g, preferred_element_type=jnp.float32)
    return residual_in + product


def solution(mesh):
    devices = mesh.devices.reshape(ROW_SPLIT + COL_SPLIT)
    fine = Mesh(devices, ROW_AXES + COL_AXES)
    row, col = ROW_AXES, COL_AXES
    in_specs = (P(row, col), P(row, col, None, None), P(row, col), P(row, col))
    out_specs = P(row, col)
    return jax.shard_map(body, mesh=fine, in_specs=in_specs, out_specs=out_specs, check_vma=False)
```

```python
import functools

import jax
import jax.numpy as jnp
from jax import lax
from jax.experimental import pallas as pl
from jax.experimental.pallas import tpu as pltpu
from jax.sharding import Mesh
from jax.sharding import PartitionSpec as P

ROW_AXES = ("z_hi", "y", "core")
COL_AXES = ("z_lo", "x")
ROW_SPLIT = (2, 4, 2)
COL_SPLIT = (8, 4)
MESH = pl.DeviceIdType.MESH


def gather_kernel(groups, *refs):
    count = len(groups)
    x_refs, o_refs = refs[:count], refs[count:2 * count]
    send_sem, recv_sem = refs[2 * count:]
    barrier = pltpu.get_barrier_semaphore()
    for axis, n in groups:
        me = lax.axis_index(axis)
        for j in range(1, n):
            peer = lax.rem(me + j, n)
            pl.semaphore_signal(barrier, inc=1, device_id={axis: peer}, device_id_type=MESH)
    pl.semaphore_wait(barrier, sum(n - 1 for _, n in groups))
    copies = []
    slot = 0
    order = [(g, j) for j in range(1, max(n for _, n in groups)) for g in range(count) if j < groups[g][1]]
    for g, j in order:
        axis, n = groups[g]
        me = lax.axis_index(axis)
        peer = lax.rem(me + j, n)
        copy = pltpu.make_async_remote_copy(
            src_ref=x_refs[g],
            dst_ref=o_refs[g].at[me],
            send_sem=send_sem.at[slot],
            recv_sem=recv_sem.at[slot],
            device_id={axis: peer},
            device_id_type=MESH,
        )
        copy.start()
        copies.append(copy)
        slot += 1
    for copy in copies:
        copy.wait()


def gather(xs, groups, cid):
    xs, groups = list(xs), list(groups)
    slots = sum(n - 1 for _, n in groups)
    nbytes = sum(2 * n * x.size * x.dtype.itemsize for x, (_, n) in zip(xs, groups))
    outs = pl.pallas_call(
        functools.partial(gather_kernel, groups),
        out_shape=[jax.ShapeDtypeStruct((n,) + x.shape, x.dtype) for x, (_, n) in zip(xs, groups)],
        in_specs=[pl.BlockSpec(memory_space=pl.ANY)] * len(xs),
        out_specs=[pl.BlockSpec(memory_space=pl.ANY)] * len(xs),
        scratch_shapes=[pltpu.SemaphoreType.DMA((slots,)), pltpu.SemaphoreType.DMA((slots,))],
        compiler_params=pltpu.CompilerParams(collective_id=cid, has_side_effects=True),
        cost_estimate=pl.CostEstimate(flops=0, transcendentals=0, bytes_accessed=nbytes),
        name="gather_" + "_".join(axis for axis, _ in groups),
    )(*xs)
    return [
        lax.dynamic_update_slice_in_dim(out, x[None], lax.axis_index(axis), axis=0)
        for out, x, (axis, _) in zip(outs, xs, groups)
    ]


def body(amplitudes, packed_tiles, tile_ids, residual_in):
    per_device = packed_tiles.shape[1]
    tile = packed_tiles.shape[2]
    col_count = COL_SPLIT[0] * COL_SPLIT[1]
    own_ids = tile_ids[0]
    target_col = own_ids // per_device
    position = own_ids % per_device
    chooser = (jnp.arange(col_count)[:, None] == target_col[None, :]).astype(jnp.bfloat16)
    tag_rows = jnp.broadcast_to(
        (position + 1).astype(jnp.bfloat16)[:, None, None], (per_device, 16, tile)
    )
    tagged = jnp.concatenate([packed_tiles[0], tag_rows], axis=1)
    outgoing = jnp.einsum("sl,lij->sij", chooser, tagged, preferred_element_type=jnp.float32)
    outgoing = outgoing.astype(jnp.bfloat16)
    incoming = lax.all_to_all(outgoing, COL_AXES, split_axis=0, concat_axis=0, tiled=True)
    tags = incoming[:, tile, 0].astype(jnp.float32)
    unpack = (
        (jnp.arange(per_device, dtype=jnp.float32)[:, None] + 1.0) == tags[None, :]
    ).astype(jnp.bfloat16)
    unpacked = jnp.einsum(
        "ps,sij->pij", unpack, incoming[:, :tile, :], preferred_element_type=jnp.float32
    ).astype(jnp.bfloat16)
    kt = 2
    qt = per_device // kt
    block = unpacked.reshape(kt, qt, tile, tile).transpose(0, 2, 1, 3).reshape(kt, tile, qt * tile)
    (a,) = gather([amplitudes], [("z_lo", COL_SPLIT[0])], 3)
    (g,) = gather([block], [("z_hi", ROW_SPLIT[0])], 0)
    a, g = gather([a, g], [("x", COL_SPLIT[1]), ("y", ROW_SPLIT[1])], 1)
    (g,) = gather([g], [("core", ROW_SPLIT[2])], 2)
    a = a.reshape(2, 2, 2, 4, a.shape[2], a.shape[3])
    product = jnp.einsum("ckhypj,cyhkjn->pn", a, g, preferred_element_type=jnp.float32)
    return residual_in + product


def solution(mesh):
    devices = mesh.devices.reshape(ROW_SPLIT + COL_SPLIT)
    fine = Mesh(devices, ROW_AXES + COL_AXES)
    row, col = ROW_AXES, COL_AXES
    in_specs = (P(row, col), P(row, col, None, None), P(row, col), P(row, col))
    out_specs = P(row, col)
    return jax.shard_map(body, mesh=fine, in_specs=in_specs, out_specs=out_specs, check_vma=False)
```

```python
import functools
import math

import jax
import jax.numpy as jnp
from jax import lax
from jax.experimental import pallas as pl
from jax.experimental.pallas import tpu as pltpu
from jax.sharding import Mesh
from jax.sharding import PartitionSpec as P

ROW_AXES = ("z_hi", "y", "core")
COL_AXES = ("z_lo", "x")
ROW_SPLIT = (2, 4, 2)
COL_SPLIT = (8, 4)
MESH = pl.DeviceIdType.MESH


def _index(axes, sizes):
    index = 0
    for axis, size in zip(axes, sizes):
        index = index * size + lax.axis_index(axis)
    return index


def _device(axes, sizes, flat):
    coords = {}
    for axis, size in reversed(list(zip(axes, sizes))):
        coords[axis] = lax.rem(flat, size)
        flat = flat // size
    return coords


def exchange_kernel(groups, *refs):
    count = len(groups)
    x_refs, o_refs = refs[:count], refs[count:2 * count]
    send_sem, recv_sem = refs[2 * count:]
    barrier = pltpu.get_barrier_semaphore()
    total = 0
    for _, axes, sizes in groups:
        n = math.prod(sizes)
        me = _index(axes, sizes)
        for j in range(1, n):
            peer = _device(axes, sizes, lax.rem(me + j, n))
            pl.semaphore_signal(barrier, inc=1, device_id=peer, device_id_type=MESH)
        total += n - 1
    pl.semaphore_wait(barrier, total)
    copies = []
    slot = 0
    longest = max(math.prod(sizes) for _, _, sizes in groups)
    for j in range(1, longest):
        for g, (kind, axes, sizes) in enumerate(groups):
            n = math.prod(sizes)
            if j >= n:
                continue
            me = _index(axes, sizes)
            flat = lax.rem(me + j, n)
            src = x_refs[g] if kind == "gather" else x_refs[g].at[flat]
            copy = pltpu.make_async_remote_copy(
                src_ref=src,
                dst_ref=o_refs[g].at[me],
                send_sem=send_sem.at[slot],
                recv_sem=recv_sem.at[slot],
                device_id=_device(axes, sizes, flat),
                device_id_type=MESH,
            )
            copy.start()
            copies.append(copy)
            slot += 1
    for copy in copies:
        copy.wait()


def exchange(xs, groups, cid):
    xs, groups = list(xs), list(groups)
    slots = sum(math.prod(sizes) - 1 for _, _, sizes in groups)
    shapes = []
    for x, (kind, _, sizes) in zip(xs, groups):
        shapes.append((math.prod(sizes),) + x.shape if kind == "gather" else x.shape)
    nbytes = sum(2 * math.prod(shape) * x.dtype.itemsize for x, shape in zip(xs, shapes))
    outs = pl.pallas_call(
        functools.partial(exchange_kernel, groups),
        out_shape=[jax.ShapeDtypeStruct(shape, x.dtype) for x, shape in zip(xs, shapes)],
        in_specs=[pl.BlockSpec(memory_space=pl.ANY)] * len(xs),
        out_specs=[pl.BlockSpec(memory_space=pl.ANY)] * len(xs),
        scratch_shapes=[pltpu.SemaphoreType.DMA((slots,)), pltpu.SemaphoreType.DMA((slots,))],
        compiler_params=pltpu.CompilerParams(collective_id=cid, has_side_effects=True),
        cost_estimate=pl.CostEstimate(flops=0, transcendentals=0, bytes_accessed=nbytes),
        name="exchange_" + "_".join("".join(axes) for _, axes, _ in groups),
    )(*xs)
    results = []
    for out, x, (kind, axes, sizes) in zip(outs, xs, groups):
        me = _index(axes, sizes)
        own = x[None] if kind == "gather" else lax.dynamic_slice_in_dim(x, me, 1, axis=0)
        results.append(lax.dynamic_update_slice_in_dim(out, own, me, axis=0))
    return results


def gather(xs, groups, cid):
    return exchange(xs, [("gather", (axis,), (n,)) for axis, n in groups], cid)


def body(amplitudes, packed_tiles, tile_ids, residual_in):
    per_device = packed_tiles.shape[1]
    tile = packed_tiles.shape[2]
    col_count = COL_SPLIT[0] * COL_SPLIT[1]
    own_ids = tile_ids[0]
    target_col = own_ids // per_device
    position = own_ids % per_device
    chooser = (jnp.arange(col_count)[:, None] == target_col[None, :]).astype(jnp.bfloat16)
    tag_rows = jnp.broadcast_to(
        (position + 1).astype(jnp.bfloat16)[:, None, None], (per_device, 16, tile)
    )
    tagged = jnp.concatenate([packed_tiles[0], tag_rows], axis=1)
    outgoing = jnp.einsum("sl,lij->sij", chooser, tagged, preferred_element_type=jnp.float32)
    outgoing = outgoing.astype(jnp.bfloat16)
    incoming, a = exchange(
        [outgoing, amplitudes],
        [("a2a", COL_AXES, COL_SPLIT), ("gather", ("z_lo",), (COL_SPLIT[0],))],
        3,
    )
    tags = incoming[:, tile, 0].astype(jnp.float32)
    unpack = (
        (jnp.arange(per_device, dtype=jnp.float32)[:, None] + 1.0) == tags[None, :]
    ).astype(jnp.bfloat16)
    unpacked = jnp.einsum(
        "ps,sij->pij", unpack, incoming[:, :tile, :], preferred_element_type=jnp.float32
    ).astype(jnp.bfloat16)
    kt = 2
    qt = per_device // kt
    block = unpacked.reshape(kt, qt, tile, tile).transpose(0, 2, 1, 3).reshape(kt, tile, qt * tile)
    (g,) = gather([block], [("z_hi", ROW_SPLIT[0])], 0)
    a, g = gather([a, g], [("x", COL_SPLIT[1]), ("y", ROW_SPLIT[1])], 1)
    (g,) = gather([g], [("core", ROW_SPLIT[2])], 2)
    a = a.reshape(2, 2, 2, 4, a.shape[2], a.shape[3])
    product = jnp.einsum("ckhypj,cyhkjn->pn", a, g, preferred_element_type=jnp.float32)
    return residual_in + product


def solution(mesh):
    devices = mesh.devices.reshape(ROW_SPLIT + COL_SPLIT)
    fine = Mesh(devices, ROW_AXES + COL_AXES)
    row, col = ROW_AXES, COL_AXES
    in_specs = (P(row, col), P(row, col, None, None), P(row, col), P(row, col))
    out_specs = P(row, col)
    return jax.shard_map(body, mesh=fine, in_specs=in_specs, out_specs=out_specs, check_vma=False)
```

```python
import functools
import math

import jax
import jax.numpy as jnp
from jax import lax
from jax.experimental import pallas as pl
from jax.experimental.pallas import tpu as pltpu
from jax.sharding import Mesh
from jax.sharding import PartitionSpec as P

ROW_AXES = ("z_hi", "y", "core")
COL_AXES = ("z_lo", "x")
ROW_SPLIT = (2, 4, 2)
COL_SPLIT = (8, 4)
MESH = pl.DeviceIdType.MESH


def _index(axes, sizes):
    index = 0
    for axis, size in zip(axes, sizes):
        index = index * size + lax.axis_index(axis)
    return index


def _device(axes, sizes, flat):
    coords = {}
    for axis, size in reversed(list(zip(axes, sizes))):
        coords[axis] = lax.rem(flat, size)
        flat = flat // size
    return coords


def exchange_kernel(groups, *refs):
    count = len(groups)
    x_refs, o_refs = refs[:count], refs[count:2 * count]
    send_sem, recv_sem, line_send, line_recv = refs[2 * count:]
    barrier = pltpu.get_barrier_semaphore()
    total = 0
    for kind, axes, sizes in groups:
        n = math.prod(sizes)
        if kind == "line":
            axis = axes[0]
            i = lax.axis_index(axis)

            @pl.when(i > 0)
            def _():
                pl.semaphore_signal(barrier, inc=1, device_id={axis: i - 1}, device_id_type=MESH)

            @pl.when(i < n - 1)
            def _():
                pl.semaphore_signal(barrier, inc=1, device_id={axis: i + 1}, device_id_type=MESH)

            total = total + (i > 0).astype(jnp.int32) + (i < n - 1).astype(jnp.int32)
            continue
        me = _index(axes, sizes)
        for j in range(1, n):
            peer = _device(axes, sizes, lax.rem(me + j, n))
            pl.semaphore_signal(barrier, inc=1, device_id=peer, device_id_type=MESH)
        total = total + (n - 1)
    pl.semaphore_wait(barrier, total)
    copies = []
    slot = 0
    direct = [(g, grp) for g, grp in enumerate(groups) if grp[0] != "line"]
    longest = max([math.prod(sizes) for _, (_, _, sizes) in direct], default=1)
    for j in range(1, longest):
        for g, (kind, axes, sizes) in direct:
            n = math.prod(sizes)
            if j >= n:
                continue
            me = _index(axes, sizes)
            flat = lax.rem(me + j, n)
            src = x_refs[g] if kind == "gather" else x_refs[g].at[flat]
            copy = pltpu.make_async_remote_copy(
                src_ref=src,
                dst_ref=o_refs[g].at[me],
                send_sem=send_sem.at[slot],
                recv_sem=recv_sem.at[slot],
                device_id=_device(axes, sizes, flat),
                device_id_type=MESH,
            )
            copy.start()
            copies.append(copy)
            slot += 1
    for g, (kind, axes, sizes) in enumerate(groups):
        if kind == "line":
            _line_ring(axes[0], sizes[0], x_refs[g], o_refs[g], line_send, line_recv)
    for copy in copies:
        copy.wait()


def _line_ring(axis, n, x_ref, o_ref, send_sem, recv_sem):
    i = lax.axis_index(axis)

    def hop(step, direction):
        if direction == 0:
            origin, target, alive = i - step + 1, i + 1, (i + 1 <= n - 1) & (i - step + 1 >= 0)
        else:
            origin, target, alive = i + step - 1, i - 1, (i >= 1) & (i + step - 1 <= n - 1)
        origin = jnp.clip(origin, 0, n - 1)
        src = x_ref if step == 1 else o_ref.at[origin]
        copy = pltpu.make_async_remote_copy(
            src_ref=src,
            dst_ref=o_ref.at[origin],
            send_sem=send_sem.at[direction, step - 1],
            recv_sem=recv_sem.at[direction, step - 1],
            device_id={axis: jnp.clip(target, 0, n - 1)},
            device_id_type=MESH,
        )
        return copy, alive

    def arrival(step, direction):
        origin = i - step if direction == 0 else i + step
        alive = (origin >= 0) & (origin <= n - 1)
        copy = pltpu.make_async_copy(
            x_ref, o_ref.at[jnp.clip(origin, 0, n - 1)], recv_sem.at[direction, step - 1]
        )
        return copy, alive

    sent = []
    for step in range(1, n):
        for direction in (0, 1):
            copy, alive = hop(step, direction)
            pl.when(alive)(copy.start)
            sent.append((copy, alive))
        for direction in (0, 1):
            copy, alive = arrival(step, direction)
            pl.when(alive)(copy.wait)
    for copy, alive in sent:
        pl.when(alive)(copy.wait_send)


def exchange(xs, groups, cid):
    xs, groups = list(xs), list(groups)
    slots = max(1, sum(math.prod(sizes) - 1 for kind, _, sizes in groups if kind != "line"))
    line = max([sizes[0] for kind, _, sizes in groups if kind == "line"], default=2)
    shapes = []
    for x, (kind, _, sizes) in zip(xs, groups):
        shapes.append(x.shape if kind == "a2a" else (math.prod(sizes),) + x.shape)
    nbytes = sum(2 * math.prod(shape) * x.dtype.itemsize for x, shape in zip(xs, shapes))
    outs = pl.pallas_call(
        functools.partial(exchange_kernel, groups),
        out_shape=[jax.ShapeDtypeStruct(shape, x.dtype) for x, shape in zip(xs, shapes)],
        in_specs=[pl.BlockSpec(memory_space=pl.ANY)] * len(xs),
        out_specs=[pl.BlockSpec(memory_space=pl.ANY)] * len(xs),
        scratch_shapes=[
            pltpu.SemaphoreType.DMA((slots,)),
            pltpu.SemaphoreType.DMA((slots,)),
            pltpu.SemaphoreType.DMA((2, line - 1)),
            pltpu.SemaphoreType.DMA((2, line - 1)),
        ],
        compiler_params=pltpu.CompilerParams(collective_id=cid, has_side_effects=True),
        cost_estimate=pl.CostEstimate(flops=0, transcendentals=0, bytes_accessed=nbytes),
        name="exchange_" + "_".join("".join(axes) for _, axes, _ in groups),
    )(*xs)
    results = []
    for out, x, (kind, axes, sizes) in zip(outs, xs, groups):
        me = _index(axes, sizes)
        own = lax.dynamic_slice_in_dim(x, me, 1, axis=0) if kind == "a2a" else x[None]
        results.append(lax.dynamic_update_slice_in_dim(out, own, me, axis=0))
    return results


def gather(xs, groups, cid):
    return exchange(xs, [("gather", (axis,), (n,)) for axis, n in groups], cid)


def body(amplitudes, packed_tiles, tile_ids, residual_in):
    per_device = packed_tiles.shape[1]
    tile = packed_tiles.shape[2]
    col_count = COL_SPLIT[0] * COL_SPLIT[1]
    own_ids = tile_ids[0]
    target_col = own_ids // per_device
    position = own_ids % per_device
    chooser = (jnp.arange(col_count)[:, None] == target_col[None, :]).astype(jnp.bfloat16)
    tag_rows = jnp.broadcast_to(
        (position + 1).astype(jnp.bfloat16)[:, None, None], (per_device, 16, tile)
    )
    tagged = jnp.concatenate([packed_tiles[0], tag_rows], axis=1)
    outgoing = jnp.einsum("sl,lij->sij", chooser, tagged, preferred_element_type=jnp.float32)
    outgoing = outgoing.astype(jnp.bfloat16)
    incoming, a = exchange(
        [outgoing, amplitudes],
        [("a2a", COL_AXES, COL_SPLIT), ("line", ("z_lo",), (COL_SPLIT[0],))],
        3,
    )
    tags = incoming[:, tile, 0].astype(jnp.float32)
    unpack = (
        (jnp.arange(per_device, dtype=jnp.float32)[:, None] + 1.0) == tags[None, :]
    ).astype(jnp.bfloat16)
    unpacked = jnp.einsum(
        "ps,sij->pij", unpack, incoming[:, :tile, :], preferred_element_type=jnp.float32
    ).astype(jnp.bfloat16)
    kt = 2
    qt = per_device // kt
    block = unpacked.reshape(kt, qt, tile, tile).transpose(0, 2, 1, 3).reshape(kt, tile, qt * tile)
    (g,) = gather([block], [("z_hi", ROW_SPLIT[0])], 0)
    a, g = gather([a, g], [("x", COL_SPLIT[1]), ("y", ROW_SPLIT[1])], 1)
    (g,) = gather([g], [("core", ROW_SPLIT[2])], 2)
    a = a.reshape(2, 2, 2, 4, a.shape[2], a.shape[3])
    product = jnp.einsum("ckhypj,cyhkjn->pn", a, g, preferred_element_type=jnp.float32)
    return residual_in + product


def solution(mesh):
    devices = mesh.devices.reshape(ROW_SPLIT + COL_SPLIT)
    fine = Mesh(devices, ROW_AXES + COL_AXES)
    row, col = ROW_AXES, COL_AXES
    in_specs = (P(row, col), P(row, col, None, None), P(row, col), P(row, col))
    out_specs = P(row, col)
    return jax.shard_map(body, mesh=fine, in_specs=in_specs, out_specs=out_specs, check_vma=False)
```

```python
import functools
import math

import jax
import jax.numpy as jnp
from jax import lax
from jax.experimental import pallas as pl
from jax.experimental.pallas import tpu as pltpu
from jax.sharding import Mesh
from jax.sharding import PartitionSpec as P

ROW_AXES = ("z_hi", "y", "core")
COL_AXES = ("z_lo", "x")
ROW_SPLIT = (2, 4, 2)
COL_SPLIT = (8, 4)
MESH = pl.DeviceIdType.MESH


def _index(axes, sizes):
    index = 0
    for axis, size in zip(axes, sizes):
        index = index * size + lax.axis_index(axis)
    return index


def _device(axes, sizes, flat):
    coords = {}
    for axis, size in reversed(list(zip(axes, sizes))):
        coords[axis] = lax.rem(flat, size)
        flat = flat // size
    return coords


def exchange_kernel(groups, *refs):
    count = len(groups)
    x_refs, o_refs = refs[:count], refs[count:2 * count]
    send_sem, recv_sem, line_send, line_recv = refs[2 * count:]
    barrier = pltpu.get_barrier_semaphore()
    total = 0
    for kind, axes, sizes in groups:
        n = math.prod(sizes)
        if kind == "line":
            axis = axes[0]
            i = lax.axis_index(axis)

            @pl.when(i > 0)
            def _():
                pl.semaphore_signal(barrier, inc=1, device_id={axis: i - 1}, device_id_type=MESH)

            @pl.when(i < n - 1)
            def _():
                pl.semaphore_signal(barrier, inc=1, device_id={axis: i + 1}, device_id_type=MESH)

            total = total + (i > 0).astype(jnp.int32) + (i < n - 1).astype(jnp.int32)
            continue
        me = _index(axes, sizes)
        for j in range(1, n):
            peer = _device(axes, sizes, lax.rem(me + j, n))
            pl.semaphore_signal(barrier, inc=1, device_id=peer, device_id_type=MESH)
        total = total + (n - 1)
    pl.semaphore_wait(barrier, total)
    copies = []
    slot = 0
    direct = [(g, grp) for g, grp in enumerate(groups) if grp[0] != "line"]
    longest = max([math.prod(sizes) for _, (_, _, sizes) in direct], default=1)
    for j in range(1, longest):
        for g, (kind, axes, sizes) in direct:
            n = math.prod(sizes)
            if j >= n:
                continue
            me = _index(axes, sizes)
            flat = lax.rem(me + j, n)
            src = x_refs[g] if kind == "gather" else x_refs[g].at[flat]
            copy = pltpu.make_async_remote_copy(
                src_ref=src,
                dst_ref=o_refs[g].at[me],
                send_sem=send_sem.at[slot],
                recv_sem=recv_sem.at[slot],
                device_id=_device(axes, sizes, flat),
                device_id_type=MESH,
            )
            copy.start()
            copies.append(copy)
            slot += 1
    for g, (kind, axes, sizes) in enumerate(groups):
        if kind == "line":
            _line_ring(axes[0], sizes[0], x_refs[g], o_refs[g], line_send, line_recv)
    for copy in copies:
        copy.wait()


def _line_ring(axis, n, x_ref, o_ref, send_sem, recv_sem):
    i = lax.axis_index(axis)

    def hop(step, direction):
        if direction == 0:
            origin, target, alive = i - step + 1, i + 1, (i + 1 <= n - 1) & (i - step + 1 >= 0)
        else:
            origin, target, alive = i + step - 1, i - 1, (i >= 1) & (i + step - 1 <= n - 1)
        origin = jnp.clip(origin, 0, n - 1)
        src = x_ref if step == 1 else o_ref.at[origin]
        copy = pltpu.make_async_remote_copy(
            src_ref=src,
            dst_ref=o_ref.at[origin],
            send_sem=send_sem.at[direction, step - 1],
            recv_sem=recv_sem.at[direction, step - 1],
            device_id={axis: jnp.clip(target, 0, n - 1)},
            device_id_type=MESH,
        )
        return copy, alive

    def arrival(step, direction):
        origin = i - step if direction == 0 else i + step
        alive = (origin >= 0) & (origin <= n - 1)
        copy = pltpu.make_async_copy(
            x_ref, o_ref.at[jnp.clip(origin, 0, n - 1)], recv_sem.at[direction, step - 1]
        )
        return copy, alive

    sent = []
    for step in range(1, n):
        for direction in (0, 1):
            copy, alive = hop(step, direction)
            pl.when(alive)(copy.start)
            sent.append((copy, alive))
        for direction in (0, 1):
            copy, alive = arrival(step, direction)
            pl.when(alive)(copy.wait)
    for copy, alive in sent:
        pl.when(alive)(copy.wait_send)


def exchange(xs, groups, cid):
    xs, groups = list(xs), list(groups)
    slots = max(1, sum(math.prod(sizes) - 1 for kind, _, sizes in groups if kind != "line"))
    line = max([sizes[0] for kind, _, sizes in groups if kind == "line"], default=2)
    shapes = []
    for x, (kind, _, sizes) in zip(xs, groups):
        shapes.append(x.shape if kind == "a2a" else (math.prod(sizes),) + x.shape)
    nbytes = sum(2 * math.prod(shape) * x.dtype.itemsize for x, shape in zip(xs, shapes))
    outs = pl.pallas_call(
        functools.partial(exchange_kernel, groups),
        out_shape=[jax.ShapeDtypeStruct(shape, x.dtype) for x, shape in zip(xs, shapes)],
        in_specs=[pl.BlockSpec(memory_space=pl.ANY)] * len(xs),
        out_specs=[pl.BlockSpec(memory_space=pl.ANY)] * len(xs),
        scratch_shapes=[
            pltpu.SemaphoreType.DMA((slots,)),
            pltpu.SemaphoreType.DMA((slots,)),
            pltpu.SemaphoreType.DMA((2, line - 1)),
            pltpu.SemaphoreType.DMA((2, line - 1)),
        ],
        compiler_params=pltpu.CompilerParams(collective_id=cid, has_side_effects=True),
        cost_estimate=pl.CostEstimate(flops=0, transcendentals=0, bytes_accessed=nbytes),
        name="exchange_" + "_".join("".join(axes) for _, axes, _ in groups),
    )(*xs)
    results = []
    for out, x, (kind, axes, sizes) in zip(outs, xs, groups):
        me = _index(axes, sizes)
        own = lax.dynamic_slice_in_dim(x, me, 1, axis=0) if kind == "a2a" else x[None]
        results.append(lax.dynamic_update_slice_in_dim(out, own, me, axis=0))
    return results


def gather(xs, groups, cid):
    return exchange(xs, [("gather", (axis,), (n,)) for axis, n in groups], cid)


def row_kernel(a_ref, b_ref, ao_ref, g_ref, a_send, a_recv, z_send, z_recv, y_send, y_recv, c_send, c_recv):
    nx, ny = COL_SPLIT[1], ROW_SPLIT[1]
    h, y, c = lax.axis_index("z_hi"), lax.axis_index("y"), lax.axis_index("core")
    xi = lax.axis_index("x")
    peers = [{"z_hi": 1 - h}, {"core": 1 - c}]
    peers += [{"y": lax.rem(y + j, ny)} for j in range(1, ny)]
    peers += [{"x": lax.rem(xi + j, nx)} for j in range(1, nx)]
    barrier = pltpu.get_barrier_semaphore()
    for peer in peers:
        pl.semaphore_signal(barrier, inc=1, device_id=peer, device_id_type=MESH)
    pl.semaphore_wait(barrier, len(peers))
    sent = []

    def send(src, dst, ssem, rsem, peer):
        copy = pltpu.make_async_remote_copy(
            src_ref=src, dst_ref=dst, send_sem=ssem, recv_sem=rsem, device_id=peer, device_id_type=MESH
        )
        copy.start()
        sent.append(copy)

    def arrive(dst, rsem, like):
        pltpu.make_async_copy(like, dst, rsem).wait()

    for j in range(1, nx):
        send(a_ref, ao_ref.at[xi], a_send.at[j - 1], a_recv.at[j - 1], {"x": lax.rem(xi + j, nx)})
    send(b_ref, g_ref.at[c, y, h], z_send.at[0], z_recv.at[0], {"z_hi": 1 - h})
    for j in range(1, ny):
        send(b_ref, g_ref.at[c, y, h], y_send.at[j - 1, 0], y_recv.at[j - 1, 0], {"y": lax.rem(y + j, ny)})
    send(b_ref, g_ref.at[c, y, h], c_send.at[y, h], c_recv.at[y, h], {"core": 1 - c})
    arrive(g_ref.at[c, y, 1 - h], z_recv.at[0], b_ref)
    for j in range(1, ny):
        src = g_ref.at[c, y, 1 - h]
        send(src, src, y_send.at[j - 1, 1], y_recv.at[j - 1, 1], {"y": lax.rem(y + j, ny)})
    send(g_ref.at[c, y, 1 - h], g_ref.at[c, y, 1 - h], c_send.at[y, 1 - h], c_recv.at[y, 1 - h], {"core": 1 - c})
    for j in range(1, ny):
        origin = lax.rem(y - j + ny, ny)
        for k, hh in ((0, h), (1, 1 - h)):
            block = g_ref.at[c, origin, hh]
            arrive(block, y_recv.at[j - 1, k], b_ref)
            send(block, block, c_send.at[origin, hh], c_recv.at[origin, hh], {"core": 1 - c})
    for yy in range(ny):
        for hh in range(ROW_SPLIT[0]):
            arrive(g_ref.at[1 - c, yy, hh], c_recv.at[yy, hh], b_ref)
    for j in range(1, nx):
        arrive(ao_ref.at[lax.rem(xi - j + nx, nx)], a_recv.at[j - 1], a_ref)
    for copy in sent:
        copy.wait_send()


def row_exchange(a, b):
    nx = COL_SPLIT[1]
    nh, ny, nc = ROW_SPLIT
    a_out = (nx,) + a.shape
    b_out = (nc, ny, nh) + b.shape
    nbytes = 2 * (math.prod(a_out) + math.prod(b_out)) * a.dtype.itemsize
    ao, g = pl.pallas_call(
        row_kernel,
        out_shape=[jax.ShapeDtypeStruct(a_out, a.dtype), jax.ShapeDtypeStruct(b_out, b.dtype)],
        in_specs=[pl.BlockSpec(memory_space=pl.ANY)] * 2,
        out_specs=[pl.BlockSpec(memory_space=pl.ANY)] * 2,
        scratch_shapes=[
            pltpu.SemaphoreType.DMA((nx - 1,)),
            pltpu.SemaphoreType.DMA((nx - 1,)),
            pltpu.SemaphoreType.DMA((1,)),
            pltpu.SemaphoreType.DMA((1,)),
            pltpu.SemaphoreType.DMA((ny - 1, 2)),
            pltpu.SemaphoreType.DMA((ny - 1, 2)),
            pltpu.SemaphoreType.DMA((ny, nh)),
            pltpu.SemaphoreType.DMA((ny, nh)),
        ],
        compiler_params=pltpu.CompilerParams(collective_id=7, has_side_effects=True),
        cost_estimate=pl.CostEstimate(flops=0, transcendentals=0, bytes_accessed=nbytes),
        name="row_exchange",
    )(a, b)
    xi = lax.axis_index("x")
    h, y, c = lax.axis_index("z_hi"), lax.axis_index("y"), lax.axis_index("core")
    ao = lax.dynamic_update_slice_in_dim(ao, a[None], xi, axis=0)
    g = lax.dynamic_update_slice(g, b[None, None, None], (c, y, h) + (0,) * b.ndim)
    return ao, g


def body(amplitudes, packed_tiles, tile_ids, residual_in):
    per_device = packed_tiles.shape[1]
    tile = packed_tiles.shape[2]
    col_count = COL_SPLIT[0] * COL_SPLIT[1]
    own_ids = tile_ids[0]
    target_col = own_ids // per_device
    position = own_ids % per_device
    chooser = (jnp.arange(col_count)[:, None] == target_col[None, :]).astype(jnp.bfloat16)
    tag_rows = jnp.broadcast_to(
        (position + 1).astype(jnp.bfloat16)[:, None, None], (per_device, 16, tile)
    )
    tagged = jnp.concatenate([packed_tiles[0], tag_rows], axis=1)
    outgoing = jnp.einsum("sl,lij->sij", chooser, tagged, preferred_element_type=jnp.float32)
    outgoing = outgoing.astype(jnp.bfloat16)
    incoming, a = exchange(
        [outgoing, amplitudes],
        [("a2a", COL_AXES, COL_SPLIT), ("line", ("z_lo",), (COL_SPLIT[0],))],
        3,
    )
    tags = incoming[:, tile, 0].astype(jnp.float32)
    unpack = (
        (jnp.arange(per_device, dtype=jnp.float32)[:, None] + 1.0) == tags[None, :]
    ).astype(jnp.bfloat16)
    unpacked = jnp.einsum(
        "ps,sij->pij", unpack, incoming[:, :tile, :], preferred_element_type=jnp.float32
    ).astype(jnp.bfloat16)
    kt = 2
    qt = per_device // kt
    block = unpacked.reshape(kt, qt, tile, tile).transpose(0, 2, 1, 3).reshape(kt, tile, qt * tile)
    a, g = row_exchange(a, block)
    a = a.reshape(2, 2, 2, 4, a.shape[2], a.shape[3])
    product = jnp.einsum("ckhypj,cyhkjn->pn", a, g, preferred_element_type=jnp.float32)
    return residual_in + product


def solution(mesh):
    devices = mesh.devices.reshape(ROW_SPLIT + COL_SPLIT)
    fine = Mesh(devices, ROW_AXES + COL_AXES)
    row, col = ROW_AXES, COL_AXES
    in_specs = (P(row, col), P(row, col, None, None), P(row, col), P(row, col))
    out_specs = P(row, col)
    return jax.shard_map(body, mesh=fine, in_specs=in_specs, out_specs=out_specs, check_vma=False)
```

```python
import functools
import math

import jax
import jax.numpy as jnp
from jax import lax
from jax.experimental import pallas as pl
from jax.experimental.pallas import tpu as pltpu
from jax.sharding import Mesh
from jax.sharding import PartitionSpec as P

ROW_AXES = ("z_hi", "y", "core")
COL_AXES = ("z_lo", "x")
ROW_SPLIT = (2, 4, 2)
COL_SPLIT = (8, 4)
MESH = pl.DeviceIdType.MESH


def _index(axes, sizes):
    index = 0
    for axis, size in zip(axes, sizes):
        index = index * size + lax.axis_index(axis)
    return index


def _device(axes, sizes, flat):
    coords = {}
    for axis, size in reversed(list(zip(axes, sizes))):
        coords[axis] = lax.rem(flat, size)
        flat = flat // size
    return coords


def exchange_kernel(groups, *refs):
    count = len(groups)
    x_refs, o_refs = refs[:count], refs[count:2 * count]
    send_sem, recv_sem, line_send, line_recv = refs[2 * count:]
    barrier = pltpu.get_barrier_semaphore()
    total = 0
    for kind, axes, sizes in groups:
        n = math.prod(sizes)
        if kind == "line":
            axis = axes[0]
            i = lax.axis_index(axis)

            @pl.when(i > 0)
            def _():
                pl.semaphore_signal(barrier, inc=1, device_id={axis: i - 1}, device_id_type=MESH)

            @pl.when(i < n - 1)
            def _():
                pl.semaphore_signal(barrier, inc=1, device_id={axis: i + 1}, device_id_type=MESH)

            total = total + (i > 0).astype(jnp.int32) + (i < n - 1).astype(jnp.int32)
            continue
        me = _index(axes, sizes)
        for j in range(1, n):
            peer = _device(axes, sizes, lax.rem(me + j, n))
            pl.semaphore_signal(barrier, inc=1, device_id=peer, device_id_type=MESH)
        total = total + (n - 1)
    pl.semaphore_wait(barrier, total)
    copies = []
    slot = 0
    direct = [(g, grp) for g, grp in enumerate(groups) if grp[0] != "line"]
    longest = max([math.prod(sizes) for _, (_, _, sizes) in direct], default=1)
    for j in range(1, longest):
        for g, (kind, axes, sizes) in direct:
            n = math.prod(sizes)
            if j >= n:
                continue
            me = _index(axes, sizes)
            flat = lax.rem(me + j, n)
            src = x_refs[g] if kind == "gather" else x_refs[g].at[flat]
            copy = pltpu.make_async_remote_copy(
                src_ref=src,
                dst_ref=o_refs[g].at[me],
                send_sem=send_sem.at[slot],
                recv_sem=recv_sem.at[slot],
                device_id=_device(axes, sizes, flat),
                device_id_type=MESH,
            )
            copy.start()
            copies.append(copy)
            slot += 1
    for g, (kind, axes, sizes) in enumerate(groups):
        if kind == "line":
            _line_ring(axes[0], sizes[0], x_refs[g], o_refs[g], line_send, line_recv)
    for copy in copies:
        copy.wait()


def _line_ring(axis, n, x_ref, o_ref, send_sem, recv_sem):
    i = lax.axis_index(axis)

    def hop(step, direction):
        if direction == 0:
            origin, target, alive = i - step + 1, i + 1, (i + 1 <= n - 1) & (i - step + 1 >= 0)
        else:
            origin, target, alive = i + step - 1, i - 1, (i >= 1) & (i + step - 1 <= n - 1)
        origin = jnp.clip(origin, 0, n - 1)
        src = x_ref if step == 1 else o_ref.at[origin]
        copy = pltpu.make_async_remote_copy(
            src_ref=src,
            dst_ref=o_ref.at[origin],
            send_sem=send_sem.at[direction, step - 1],
            recv_sem=recv_sem.at[direction, step - 1],
            device_id={axis: jnp.clip(target, 0, n - 1)},
            device_id_type=MESH,
        )
        return copy, alive

    def arrival(step, direction):
        origin = i - step if direction == 0 else i + step
        alive = (origin >= 0) & (origin <= n - 1)
        copy = pltpu.make_async_copy(
            x_ref, o_ref.at[jnp.clip(origin, 0, n - 1)], recv_sem.at[direction, step - 1]
        )
        return copy, alive

    sent = []
    for step in range(1, n):
        for direction in (0, 1):
            copy, alive = hop(step, direction)
            pl.when(alive)(copy.start)
            sent.append((copy, alive))
        for direction in (0, 1):
            copy, alive = arrival(step, direction)
            pl.when(alive)(copy.wait)
    for copy, alive in sent:
        pl.when(alive)(copy.wait_send)


def exchange(xs, groups, cid):
    xs, groups = list(xs), list(groups)
    slots = max(1, sum(math.prod(sizes) - 1 for kind, _, sizes in groups if kind != "line"))
    line = max([sizes[0] for kind, _, sizes in groups if kind == "line"], default=2)
    shapes = []
    for x, (kind, _, sizes) in zip(xs, groups):
        shapes.append(x.shape if kind == "a2a" else (math.prod(sizes),) + x.shape)
    nbytes = sum(2 * math.prod(shape) * x.dtype.itemsize for x, shape in zip(xs, shapes))
    outs = pl.pallas_call(
        functools.partial(exchange_kernel, groups),
        out_shape=[jax.ShapeDtypeStruct(shape, x.dtype) for x, shape in zip(xs, shapes)],
        in_specs=[pl.BlockSpec(memory_space=pl.ANY)] * len(xs),
        out_specs=[pl.BlockSpec(memory_space=pl.ANY)] * len(xs),
        scratch_shapes=[
            pltpu.SemaphoreType.DMA((slots,)),
            pltpu.SemaphoreType.DMA((slots,)),
            pltpu.SemaphoreType.DMA((2, line - 1)),
            pltpu.SemaphoreType.DMA((2, line - 1)),
        ],
        compiler_params=pltpu.CompilerParams(collective_id=cid, has_side_effects=True),
        cost_estimate=pl.CostEstimate(flops=0, transcendentals=0, bytes_accessed=nbytes),
        name="exchange_" + "_".join("".join(axes) for _, axes, _ in groups),
    )(*xs)
    results = []
    for out, x, (kind, axes, sizes) in zip(outs, xs, groups):
        me = _index(axes, sizes)
        own = lax.dynamic_slice_in_dim(x, me, 1, axis=0) if kind == "a2a" else x[None]
        results.append(lax.dynamic_update_slice_in_dim(out, own, me, axis=0))
    return results


def gather(xs, groups, cid):
    return exchange(xs, [("gather", (axis,), (n,)) for axis, n in groups], cid)


def row_kernel(a_ref, b_ref, ao_ref, g_ref, *sems):
    xd_send, xd_recv, xr_send, xr_recv, z_send, z_recv, yd_send, yd_recv, yr_send, yr_recv, c_send, c_recv = sems
    nx, ny = COL_SPLIT[1], ROW_SPLIT[1]
    h, y, c = lax.axis_index("z_hi"), lax.axis_index("y"), lax.axis_index("core")
    xi = lax.axis_index("x")
    up_x, dn_x, far_x = lax.rem(xi + 1, nx), lax.rem(xi + nx - 1, nx), lax.rem(xi + 2, nx)
    up_y, dn_y, far_y = lax.rem(y + 1, ny), lax.rem(y + ny - 1, ny), lax.rem(y + 2, ny)
    core, zpeer = {"core": 1 - c}, {"z_hi": 1 - h}
    peers = [zpeer, core, {"y": up_y}, {"y": dn_y}, {"x": up_x}, {"x": dn_x}]
    barrier = pltpu.get_barrier_semaphore()
    for peer in peers:
        pl.semaphore_signal(barrier, inc=1, device_id=peer, device_id_type=MESH)
    pl.semaphore_wait(barrier, len(peers))
    sent = []
    half_a = a_ref.shape[0] // 2
    a_half = (pl.ds(0, half_a), pl.ds(half_a, half_a))

    def send(src, dst, ssem, rsem, peer):
        copy = pltpu.make_async_remote_copy(
            src_ref=src, dst_ref=dst, send_sem=ssem, recv_sem=rsem, device_id=peer, device_id_type=MESH
        )
        copy.start()
        sent.append(copy)

    def arrive(dst, rsem, like):
        pltpu.make_async_copy(like, dst, rsem).wait()

    def to_core(yy, hh):
        for half in range(2):
            block = g_ref.at[c, yy, hh, half]
            send(block, block, c_send.at[yy, hh, half], c_recv.at[yy, hh, half], core)

    send(a_ref, ao_ref.at[xi], xd_send.at[0], xd_recv.at[0], {"x": up_x})
    send(a_ref, ao_ref.at[xi], xd_send.at[1], xd_recv.at[1], {"x": dn_x})
    send(b_ref, g_ref.at[c, y, h], z_send.at[0], z_recv.at[0], zpeer)
    send(b_ref, g_ref.at[c, y, h], yd_send.at[0, 0], yd_recv.at[0, 0], {"y": up_y})
    send(b_ref, g_ref.at[c, y, h], yd_send.at[1, 0], yd_recv.at[1, 0], {"y": dn_y})
    for half in range(2):
        send(b_ref.at[half], g_ref.at[c, y, h, half], c_send.at[y, h, half], c_recv.at[y, h, half], core)
    arrive(ao_ref.at[dn_x], xd_recv.at[0], a_ref)
    src = ao_ref.at[dn_x, a_half[0]]
    send(src, src, xr_send.at[0], xr_recv.at[0], {"x": up_x})
    arrive(ao_ref.at[up_x], xd_recv.at[1], a_ref)
    src = ao_ref.at[up_x, a_half[1]]
    send(src, src, xr_send.at[1], xr_recv.at[1], {"x": dn_x})
    arrive(g_ref.at[c, y, 1 - h], z_recv.at[0], b_ref)
    src = g_ref.at[c, y, 1 - h]
    send(src, src, yd_send.at[0, 1], yd_recv.at[0, 1], {"y": up_y})
    send(src, src, yd_send.at[1, 1], yd_recv.at[1, 1], {"y": dn_y})
    to_core(y, 1 - h)
    for direction, origin, target in ((0, dn_y, up_y), (1, up_y, dn_y)):
        for k, hh in ((0, h), (1, 1 - h)):
            arrive(g_ref.at[c, origin, hh], yd_recv.at[direction, k], b_ref)
            src = g_ref.at[c, origin, hh, direction]
            send(src, src, yr_send.at[direction, k], yr_recv.at[direction, k], {"y": target})
            to_core(origin, hh)
    for k, hh in ((0, h), (1, 1 - h)):
        for direction in range(2):
            arrive(g_ref.at[c, far_y, hh, direction], yr_recv.at[direction, k], b_ref.at[0])
        to_core(far_y, hh)
    arrive(ao_ref.at[far_x, a_half[0]], xr_recv.at[0], a_ref.at[a_half[0]])
    arrive(ao_ref.at[far_x, a_half[1]], xr_recv.at[1], a_ref.at[a_half[1]])
    for yy in range(ny):
        for hh in range(ROW_SPLIT[0]):
            for half in range(2):
                arrive(g_ref.at[1 - c, yy, hh, half], c_recv.at[yy, hh, half], b_ref.at[0])
    for copy in sent:
        copy.wait_send()


def row_exchange(a, b):
    nx = COL_SPLIT[1]
    nh, ny, nc = ROW_SPLIT
    a_out = (nx,) + a.shape
    b_out = (nc, ny, nh) + b.shape
    nbytes = 2 * (math.prod(a_out) + math.prod(b_out)) * a.dtype.itemsize
    sem_shapes = [(2,), (2,), (1,), (2, 2), (2, 2), (ny, nh, 2)]
    ao, g = pl.pallas_call(
        row_kernel,
        out_shape=[jax.ShapeDtypeStruct(a_out, a.dtype), jax.ShapeDtypeStruct(b_out, b.dtype)],
        in_specs=[pl.BlockSpec(memory_space=pl.ANY)] * 2,
        out_specs=[pl.BlockSpec(memory_space=pl.ANY)] * 2,
        scratch_shapes=[pltpu.SemaphoreType.DMA(shape) for shape in sem_shapes for _ in range(2)],
        compiler_params=pltpu.CompilerParams(collective_id=7, has_side_effects=True),
        cost_estimate=pl.CostEstimate(flops=0, transcendentals=0, bytes_accessed=nbytes),
        name="row_exchange",
    )(a, b)
    xi = lax.axis_index("x")
    h, y, c = lax.axis_index("z_hi"), lax.axis_index("y"), lax.axis_index("core")
    ao = lax.dynamic_update_slice_in_dim(ao, a[None], xi, axis=0)
    g = lax.dynamic_update_slice(g, b[None, None, None], (c, y, h) + (0,) * b.ndim)
    return ao, g


def body(amplitudes, packed_tiles, tile_ids, residual_in):
    per_device = packed_tiles.shape[1]
    tile = packed_tiles.shape[2]
    col_count = COL_SPLIT[0] * COL_SPLIT[1]
    own_ids = tile_ids[0]
    target_col = own_ids // per_device
    position = own_ids % per_device
    chooser = (jnp.arange(col_count)[:, None] == target_col[None, :]).astype(jnp.bfloat16)
    tag_rows = jnp.broadcast_to(
        (position + 1).astype(jnp.bfloat16)[:, None, None], (per_device, 16, tile)
    )
    tagged = jnp.concatenate([packed_tiles[0], tag_rows], axis=1)
    outgoing = jnp.einsum("sl,lij->sij", chooser, tagged, preferred_element_type=jnp.float32)
    outgoing = outgoing.astype(jnp.bfloat16)
    incoming, a = exchange(
        [outgoing, amplitudes],
        [("a2a", COL_AXES, COL_SPLIT), ("line", ("z_lo",), (COL_SPLIT[0],))],
        3,
    )
    tags = incoming[:, tile, 0].astype(jnp.float32)
    unpack = (
        (jnp.arange(per_device, dtype=jnp.float32)[:, None] + 1.0) == tags[None, :]
    ).astype(jnp.bfloat16)
    unpacked = jnp.einsum(
        "ps,sij->pij", unpack, incoming[:, :tile, :], preferred_element_type=jnp.float32
    ).astype(jnp.bfloat16)
    kt = 2
    qt = per_device // kt
    block = unpacked.reshape(kt, qt, tile, tile).transpose(0, 2, 1, 3).reshape(kt, tile, qt * tile)
    a, g = row_exchange(a, block)
    a = a.reshape(2, 2, 2, 4, a.shape[2], a.shape[3])
    product = jnp.einsum("ckhypj,cyhkjn->pn", a, g, preferred_element_type=jnp.float32)
    return residual_in + product


def solution(mesh):
    devices = mesh.devices.reshape(ROW_SPLIT + COL_SPLIT)
    fine = Mesh(devices, ROW_AXES + COL_AXES)
    row, col = ROW_AXES, COL_AXES
    in_specs = (P(row, col), P(row, col, None, None), P(row, col), P(row, col))
    out_specs = P(row, col)
    return jax.shard_map(body, mesh=fine, in_specs=in_specs, out_specs=out_specs, check_vma=False)
```

```python
import functools
import math

import jax
import jax.numpy as jnp
from jax import lax
from jax.experimental import pallas as pl
from jax.experimental.pallas import tpu as pltpu
from jax.sharding import Mesh
from jax.sharding import PartitionSpec as P

ROW_AXES = ("z_hi", "y", "core")
COL_AXES = ("z_lo", "x")
ROW_SPLIT = (2, 4, 2)
COL_SPLIT = (8, 4)
MESH = pl.DeviceIdType.MESH


def _index(axes, sizes):
    index = 0
    for axis, size in zip(axes, sizes):
        index = index * size + lax.axis_index(axis)
    return index


def _device(axes, sizes, flat):
    coords = {}
    for axis, size in reversed(list(zip(axes, sizes))):
        coords[axis] = lax.rem(flat, size)
        flat = flat // size
    return coords


def exchange_kernel(groups, *refs):
    count = len(groups)
    x_refs, o_refs = refs[:count], refs[count:2 * count]
    send_sem, recv_sem, line_send, line_recv = refs[2 * count:]
    barrier = pltpu.get_barrier_semaphore()
    total = 0
    for kind, axes, sizes in groups:
        n = math.prod(sizes)
        if kind == "line":
            axis = axes[0]
            i = lax.axis_index(axis)

            @pl.when(i > 0)
            def _():
                pl.semaphore_signal(barrier, inc=1, device_id={axis: i - 1}, device_id_type=MESH)

            @pl.when(i < n - 1)
            def _():
                pl.semaphore_signal(barrier, inc=1, device_id={axis: i + 1}, device_id_type=MESH)

            total = total + (i > 0).astype(jnp.int32) + (i < n - 1).astype(jnp.int32)
            continue
        me = _index(axes, sizes)
        for j in range(1, n):
            peer = _device(axes, sizes, lax.rem(me + j, n))
            pl.semaphore_signal(barrier, inc=1, device_id=peer, device_id_type=MESH)
        total = total + (n - 1)
    pl.semaphore_wait(barrier, total)
    copies = []
    slot = 0
    direct = [(g, grp) for g, grp in enumerate(groups) if grp[0] != "line"]
    longest = max([math.prod(sizes) for _, (_, _, sizes) in direct], default=1)
    for j in range(1, longest):
        for g, (kind, axes, sizes) in direct:
            n = math.prod(sizes)
            if j >= n:
                continue
            me = _index(axes, sizes)
            flat = lax.rem(me + j, n)
            src = x_refs[g] if kind == "gather" else x_refs[g].at[flat]
            copy = pltpu.make_async_remote_copy(
                src_ref=src,
                dst_ref=o_refs[g].at[me],
                send_sem=send_sem.at[slot],
                recv_sem=recv_sem.at[slot],
                device_id=_device(axes, sizes, flat),
                device_id_type=MESH,
            )
            copy.start()
            copies.append(copy)
            slot += 1
    for g, (kind, axes, sizes) in enumerate(groups):
        if kind == "line":
            _line_ring(axes[0], sizes[0], x_refs[g], o_refs[g], line_send, line_recv)
    for copy in copies:
        copy.wait()


def _line_ring(axis, n, x_ref, o_ref, send_sem, recv_sem):
    i = lax.axis_index(axis)

    def hop(step, direction):
        if direction == 0:
            origin, target, alive = i - step + 1, i + 1, (i + 1 <= n - 1) & (i - step + 1 >= 0)
        else:
            origin, target, alive = i + step - 1, i - 1, (i >= 1) & (i + step - 1 <= n - 1)
        origin = jnp.clip(origin, 0, n - 1)
        src = x_ref if step == 1 else o_ref.at[origin]
        copy = pltpu.make_async_remote_copy(
            src_ref=src,
            dst_ref=o_ref.at[origin],
            send_sem=send_sem.at[direction, step - 1],
            recv_sem=recv_sem.at[direction, step - 1],
            device_id={axis: jnp.clip(target, 0, n - 1)},
            device_id_type=MESH,
        )
        return copy, alive

    def arrival(step, direction):
        origin = i - step if direction == 0 else i + step
        alive = (origin >= 0) & (origin <= n - 1)
        copy = pltpu.make_async_copy(
            x_ref, o_ref.at[jnp.clip(origin, 0, n - 1)], recv_sem.at[direction, step - 1]
        )
        return copy, alive

    sent = []
    for step in range(1, n):
        for direction in (0, 1):
            copy, alive = hop(step, direction)
            pl.when(alive)(copy.start)
            sent.append((copy, alive))
        for direction in (0, 1):
            copy, alive = arrival(step, direction)
            pl.when(alive)(copy.wait)
    for copy, alive in sent:
        pl.when(alive)(copy.wait_send)


def exchange(xs, groups, cid):
    xs, groups = list(xs), list(groups)
    slots = max(1, sum(math.prod(sizes) - 1 for kind, _, sizes in groups if kind != "line"))
    line = max([sizes[0] for kind, _, sizes in groups if kind == "line"], default=2)
    shapes = []
    for x, (kind, _, sizes) in zip(xs, groups):
        shapes.append(x.shape if kind == "a2a" else (math.prod(sizes),) + x.shape)
    nbytes = sum(2 * math.prod(shape) * x.dtype.itemsize for x, shape in zip(xs, shapes))
    outs = pl.pallas_call(
        functools.partial(exchange_kernel, groups),
        out_shape=[jax.ShapeDtypeStruct(shape, x.dtype) for x, shape in zip(xs, shapes)],
        in_specs=[pl.BlockSpec(memory_space=pl.ANY)] * len(xs),
        out_specs=[pl.BlockSpec(memory_space=pl.ANY)] * len(xs),
        scratch_shapes=[
            pltpu.SemaphoreType.DMA((slots,)),
            pltpu.SemaphoreType.DMA((slots,)),
            pltpu.SemaphoreType.DMA((2, line - 1)),
            pltpu.SemaphoreType.DMA((2, line - 1)),
        ],
        compiler_params=pltpu.CompilerParams(collective_id=cid, has_side_effects=True),
        cost_estimate=pl.CostEstimate(flops=0, transcendentals=0, bytes_accessed=nbytes),
        name="exchange_" + "_".join("".join(axes) for _, axes, _ in groups),
    )(*xs)
    results = []
    for out, x, (kind, axes, sizes) in zip(outs, xs, groups):
        me = _index(axes, sizes)
        own = lax.dynamic_slice_in_dim(x, me, 1, axis=0) if kind == "a2a" else x[None]
        results.append(lax.dynamic_update_slice_in_dim(out, own, me, axis=0))
    return results


def gather(xs, groups, cid):
    return exchange(xs, [("gather", (axis,), (n,)) for axis, n in groups], cid)


def row_kernel(a_ref, b_ref, ao_ref, g_ref, *sems):
    xd_send, xd_recv, xr_send, xr_recv, z_send, z_recv, yd_send, yd_recv, yr_send, yr_recv, c_send, c_recv = sems
    nx, ny = COL_SPLIT[1], ROW_SPLIT[1]
    h, y, c = lax.axis_index("z_hi"), lax.axis_index("y"), lax.axis_index("core")
    xi = lax.axis_index("x")
    up_x, dn_x, far_x = lax.rem(xi + 1, nx), lax.rem(xi + nx - 1, nx), lax.rem(xi + 2, nx)
    up_y, dn_y, far_y = lax.rem(y + 1, ny), lax.rem(y + ny - 1, ny), lax.rem(y + 2, ny)
    core, zpeer = {"core": 1 - c}, {"z_hi": 1 - h}
    peers = [zpeer, core, {"y": up_y}, {"y": dn_y}, {"x": up_x}, {"x": dn_x}]
    barrier = pltpu.get_barrier_semaphore()
    for peer in peers:
        pl.semaphore_signal(barrier, inc=1, device_id=peer, device_id_type=MESH)
    pl.semaphore_wait(barrier, len(peers))
    sent = []
    half_a = a_ref.shape[0] // 2
    a_half = (pl.ds(0, half_a), pl.ds(half_a, half_a))

    def send(src, dst, ssem, rsem, peer):
        copy = pltpu.make_async_remote_copy(
            src_ref=src, dst_ref=dst, send_sem=ssem, recv_sem=rsem, device_id=peer, device_id_type=MESH
        )
        copy.start()
        sent.append(copy)

    def arrive(dst, rsem, like):
        pltpu.make_async_copy(like, dst, rsem).wait()

    def to_core(yy, hh):
        for half in range(2):
            block = g_ref.at[c, yy, hh, half]
            send(block, block, c_send.at[yy, hh, half], c_recv.at[yy, hh, half], core)

    send(a_ref, ao_ref.at[xi], xd_send.at[0], xd_recv.at[0], {"x": up_x})
    send(a_ref, ao_ref.at[xi], xd_send.at[1], xd_recv.at[1], {"x": dn_x})
    send(b_ref, g_ref.at[c, y, h], z_send.at[0], z_recv.at[0], zpeer)
    send(b_ref, g_ref.at[c, y, h], yd_send.at[0, 0], yd_recv.at[0, 0], {"y": up_y})
    send(b_ref, g_ref.at[c, y, h], yd_send.at[1, 0], yd_recv.at[1, 0], {"y": dn_y})
    for half in range(2):
        send(b_ref.at[half], g_ref.at[c, y, h, half], c_send.at[y, h, half], c_recv.at[y, h, half], core)
    arrive(ao_ref.at[dn_x], xd_recv.at[0], a_ref)
    src = ao_ref.at[dn_x, a_half[0]]
    send(src, src, xr_send.at[0], xr_recv.at[0], {"x": up_x})
    arrive(ao_ref.at[up_x], xd_recv.at[1], a_ref)
    src = ao_ref.at[up_x, a_half[1]]
    send(src, src, xr_send.at[1], xr_recv.at[1], {"x": dn_x})
    arrive(g_ref.at[c, y, 1 - h], z_recv.at[0], b_ref)
    src = g_ref.at[c, y, 1 - h]
    send(src, src, yd_send.at[0, 1], yd_recv.at[0, 1], {"y": up_y})
    send(src, src, yd_send.at[1, 1], yd_recv.at[1, 1], {"y": dn_y})
    to_core(y, 1 - h)
    for direction, origin, target in ((0, dn_y, up_y), (1, up_y, dn_y)):
        for k, hh in ((0, h), (1, 1 - h)):
            arrive(g_ref.at[c, origin, hh], yd_recv.at[direction, k], b_ref)
            src = g_ref.at[c, origin, hh, direction]
            send(src, src, yr_send.at[direction, k], yr_recv.at[direction, k], {"y": target})
            to_core(origin, hh)
    for k, hh in ((0, h), (1, 1 - h)):
        for direction in range(2):
            arrive(g_ref.at[c, far_y, hh, direction], yr_recv.at[direction, k], b_ref.at[0])
        to_core(far_y, hh)
    arrive(ao_ref.at[far_x, a_half[0]], xr_recv.at[0], a_ref.at[a_half[0]])
    arrive(ao_ref.at[far_x, a_half[1]], xr_recv.at[1], a_ref.at[a_half[1]])
    for yy in range(ny):
        for hh in range(ROW_SPLIT[0]):
            for half in range(2):
                arrive(g_ref.at[1 - c, yy, hh, half], c_recv.at[yy, hh, half], b_ref.at[0])
    for copy in sent:
        copy.wait_send()


def row_exchange(a, b):
    nx = COL_SPLIT[1]
    nh, ny, nc = ROW_SPLIT
    a_out = (nx,) + a.shape
    b_out = (nc, ny, nh) + b.shape
    nbytes = 2 * (math.prod(a_out) + math.prod(b_out)) * a.dtype.itemsize
    sem_shapes = [(2,), (2,), (1,), (2, 2), (2, 2), (ny, nh, 2)]
    ao, g = pl.pallas_call(
        row_kernel,
        out_shape=[jax.ShapeDtypeStruct(a_out, a.dtype), jax.ShapeDtypeStruct(b_out, b.dtype)],
        in_specs=[pl.BlockSpec(memory_space=pl.ANY)] * 2,
        out_specs=[pl.BlockSpec(memory_space=pl.ANY)] * 2,
        scratch_shapes=[pltpu.SemaphoreType.DMA(shape) for shape in sem_shapes for _ in range(2)],
        compiler_params=pltpu.CompilerParams(collective_id=7, has_side_effects=True),
        cost_estimate=pl.CostEstimate(flops=0, transcendentals=0, bytes_accessed=nbytes),
        name="row_exchange",
    )(a, b)
    xi = lax.axis_index("x")
    h, y, c = lax.axis_index("z_hi"), lax.axis_index("y"), lax.axis_index("core")
    ao = lax.dynamic_update_slice_in_dim(ao, a[None], xi, axis=0)
    g = lax.dynamic_update_slice(g, b[None, None, None], (c, y, h) + (0,) * b.ndim)
    return ao, g


def body(amplitudes, packed_tiles, tile_ids, residual_in):
    per_device = packed_tiles.shape[1]
    tile = packed_tiles.shape[2]
    col_count = COL_SPLIT[0] * COL_SPLIT[1]
    own_ids = tile_ids[0]
    target_col = own_ids // per_device
    chooser = (jnp.arange(col_count)[:, None] == target_col[None, :]).astype(jnp.bfloat16)
    outgoing = jnp.einsum("sl,lij->sij", chooser, packed_tiles[0], preferred_element_type=jnp.float32)
    outgoing = outgoing.astype(jnp.bfloat16)
    incoming, a, all_ids = exchange(
        [outgoing, amplitudes, tile_ids],
        [("a2a", COL_AXES, COL_SPLIT), ("line", ("z_lo",), (COL_SPLIT[0],)), ("gather", COL_AXES, COL_SPLIT)],
        3,
    )
    me = _index(COL_AXES, COL_SPLIT)
    all_ids = all_ids.reshape(col_count, per_device)
    mine = (all_ids // per_device) == me
    tags = jnp.sum(jnp.where(mine, all_ids % per_device + 1, 0), axis=1)
    unpack = (jnp.arange(per_device)[:, None] + 1 == tags[None, :]).astype(jnp.bfloat16)
    unpacked = jnp.einsum(
        "ps,sij->pij", unpack, incoming, preferred_element_type=jnp.float32
    ).astype(jnp.bfloat16)
    kt = 2
    qt = per_device // kt
    block = unpacked.reshape(kt, qt, tile, tile).transpose(0, 2, 1, 3).reshape(kt, tile, qt * tile)
    a, g = row_exchange(a, block)
    a = a.reshape(2, 2, 2, 4, a.shape[2], a.shape[3])
    product = jnp.einsum("ckhypj,cyhkjn->pn", a, g, preferred_element_type=jnp.float32)
    return residual_in + product


def solution(mesh):
    devices = mesh.devices.reshape(ROW_SPLIT + COL_SPLIT)
    fine = Mesh(devices, ROW_AXES + COL_AXES)
    row, col = ROW_AXES, COL_AXES
    in_specs = (P(row, col), P(row, col, None, None), P(row, col), P(row, col))
    out_specs = P(row, col)
    return jax.shard_map(body, mesh=fine, in_specs=in_specs, out_specs=out_specs, check_vma=False)
```

```python
import functools
import math

import jax
import jax.numpy as jnp
from jax import lax
from jax.experimental import pallas as pl
from jax.experimental.pallas import tpu as pltpu
from jax.sharding import Mesh
from jax.sharding import PartitionSpec as P

ROW_AXES = ("z_hi", "y", "core")
COL_AXES = ("z_lo", "x")
ROW_SPLIT = (2, 4, 2)
COL_SPLIT = (8, 4)
MESH = pl.DeviceIdType.MESH


def _index(axes, sizes):
    index = 0
    for axis, size in zip(axes, sizes):
        index = index * size + lax.axis_index(axis)
    return index


def _device(axes, sizes, flat):
    coords = {}
    for axis, size in reversed(list(zip(axes, sizes))):
        coords[axis] = lax.rem(flat, size)
        flat = flat // size
    return coords


def exchange_kernel(groups, *refs):
    count = len(groups)
    x_refs, o_refs = refs[:count], refs[count:2 * count]
    send_sem, recv_sem, line_send, line_recv = refs[2 * count:]
    barrier = pltpu.get_barrier_semaphore()
    total = 0
    for kind, axes, sizes in groups:
        n = math.prod(sizes)
        if kind == "line":
            axis = axes[0]
            i = lax.axis_index(axis)

            @pl.when(i > 0)
            def _():
                pl.semaphore_signal(barrier, inc=1, device_id={axis: i - 1}, device_id_type=MESH)

            @pl.when(i < n - 1)
            def _():
                pl.semaphore_signal(barrier, inc=1, device_id={axis: i + 1}, device_id_type=MESH)

            total = total + (i > 0).astype(jnp.int32) + (i < n - 1).astype(jnp.int32)
            continue
        me = _index(axes, sizes)
        for j in range(1, n):
            peer = _device(axes, sizes, lax.rem(me + j, n))
            pl.semaphore_signal(barrier, inc=1, device_id=peer, device_id_type=MESH)
        total = total + (n - 1)
    pl.semaphore_wait(barrier, total)
    copies = []
    slot = 0
    direct = [(g, grp) for g, grp in enumerate(groups) if grp[0] != "line"]
    longest = max([math.prod(sizes) for _, (_, _, sizes) in direct], default=1)
    for j in range(1, longest):
        for g, (kind, axes, sizes) in direct:
            n = math.prod(sizes)
            if j >= n:
                continue
            me = _index(axes, sizes)
            flat = lax.rem(me + j, n)
            src = x_refs[g] if kind == "gather" else x_refs[g].at[flat]
            copy = pltpu.make_async_remote_copy(
                src_ref=src,
                dst_ref=o_refs[g].at[me],
                send_sem=send_sem.at[slot],
                recv_sem=recv_sem.at[slot],
                device_id=_device(axes, sizes, flat),
                device_id_type=MESH,
            )
            copy.start()
            copies.append(copy)
            slot += 1
    for g, (kind, axes, sizes) in enumerate(groups):
        if kind == "line":
            _line_ring(axes[0], sizes[0], x_refs[g], o_refs[g], line_send, line_recv)
    for copy in copies:
        copy.wait()


def _line_ring(axis, n, x_ref, o_ref, send_sem, recv_sem):
    i = lax.axis_index(axis)

    def hop(step, direction):
        if direction == 0:
            origin, target, alive = i - step + 1, i + 1, (i + 1 <= n - 1) & (i - step + 1 >= 0)
        else:
            origin, target, alive = i + step - 1, i - 1, (i >= 1) & (i + step - 1 <= n - 1)
        origin = jnp.clip(origin, 0, n - 1)
        src = x_ref if step == 1 else o_ref.at[origin]
        copy = pltpu.make_async_remote_copy(
            src_ref=src,
            dst_ref=o_ref.at[origin],
            send_sem=send_sem.at[direction, step - 1],
            recv_sem=recv_sem.at[direction, step - 1],
            device_id={axis: jnp.clip(target, 0, n - 1)},
            device_id_type=MESH,
        )
        return copy, alive

    def arrival(step, direction):
        origin = i - step if direction == 0 else i + step
        alive = (origin >= 0) & (origin <= n - 1)
        copy = pltpu.make_async_copy(
            x_ref, o_ref.at[jnp.clip(origin, 0, n - 1)], recv_sem.at[direction, step - 1]
        )
        return copy, alive

    sent = []
    for step in range(1, n):
        for direction in (0, 1):
            copy, alive = hop(step, direction)
            pl.when(alive)(copy.start)
            sent.append((copy, alive))
        for direction in (0, 1):
            copy, alive = arrival(step, direction)
            pl.when(alive)(copy.wait)
    for copy, alive in sent:
        pl.when(alive)(copy.wait_send)


def exchange(xs, groups, cid):
    xs, groups = list(xs), list(groups)
    slots = max(1, sum(math.prod(sizes) - 1 for kind, _, sizes in groups if kind != "line"))
    line = max([sizes[0] for kind, _, sizes in groups if kind == "line"], default=2)
    shapes = []
    for x, (kind, _, sizes) in zip(xs, groups):
        shapes.append(x.shape if kind == "a2a" else (math.prod(sizes),) + x.shape)
    nbytes = sum(2 * math.prod(shape) * x.dtype.itemsize for x, shape in zip(xs, shapes))
    outs = pl.pallas_call(
        functools.partial(exchange_kernel, groups),
        out_shape=[jax.ShapeDtypeStruct(shape, x.dtype) for x, shape in zip(xs, shapes)],
        in_specs=[pl.BlockSpec(memory_space=pl.ANY)] * len(xs),
        out_specs=[pl.BlockSpec(memory_space=pl.ANY)] * len(xs),
        scratch_shapes=[
            pltpu.SemaphoreType.DMA((slots,)),
            pltpu.SemaphoreType.DMA((slots,)),
            pltpu.SemaphoreType.DMA((2, line - 1)),
            pltpu.SemaphoreType.DMA((2, line - 1)),
        ],
        compiler_params=pltpu.CompilerParams(collective_id=cid, has_side_effects=True),
        cost_estimate=pl.CostEstimate(flops=0, transcendentals=0, bytes_accessed=nbytes),
        name="exchange_" + "_".join("".join(axes) for _, axes, _ in groups),
    )(*xs)
    results = []
    for out, x, (kind, axes, sizes) in zip(outs, xs, groups):
        me = _index(axes, sizes)
        own = lax.dynamic_slice_in_dim(x, me, 1, axis=0) if kind == "a2a" else x[None]
        results.append(lax.dynamic_update_slice_in_dim(out, own, me, axis=0))
    return results


def gather(xs, groups, cid):
    return exchange(xs, [("gather", (axis,), (n,)) for axis, n in groups], cid)


def row_kernel(a_ref, b_ref, ao_ref, g_ref, relay_ref, *sems):
    xd_send, xd_recv, xr_send, xr_recv, z_send, z_recv, yd_send, yd_recv, yr_send, yr_recv, c_send, c_recv = sems
    nx, ny = COL_SPLIT[1], ROW_SPLIT[1]
    h, y, c = lax.axis_index("z_hi"), lax.axis_index("y"), lax.axis_index("core")
    xi = lax.axis_index("x")
    up_x, dn_x, far_x = lax.rem(xi + 1, nx), lax.rem(xi + nx - 1, nx), lax.rem(xi + 2, nx)
    up_y, dn_y, far_y = lax.rem(y + 1, ny), lax.rem(y + ny - 1, ny), lax.rem(y + 2, ny)
    core = {"core": 1 - c}
    zl, nzl = lax.axis_index("z_lo"), COL_SPLIT[0]
    quarter = nzl // 2
    low = zl < quarter
    up_h = jnp.where(low, h, 1 - h)
    dn_h = jnp.where(low, 1 - h, h)
    up_z = {"z_hi": up_h, "z_lo": jnp.where(low, zl + quarter, zl - quarter)}
    dn_z = {"z_hi": dn_h, "z_lo": jnp.where(low, zl + quarter, zl - quarter)}
    peers = [up_z, dn_z, core, {"y": up_y}, {"y": dn_y}, {"x": up_x}, {"x": dn_x}]
    barrier = pltpu.get_barrier_semaphore()
    for peer in peers:
        pl.semaphore_signal(barrier, inc=1, device_id=peer, device_id_type=MESH)
    pl.semaphore_wait(barrier, len(peers))
    sent = []
    half_a = a_ref.shape[0] // 2
    a_half = (pl.ds(0, half_a), pl.ds(half_a, half_a))

    def send(src, dst, ssem, rsem, peer):
        copy = pltpu.make_async_remote_copy(
            src_ref=src, dst_ref=dst, send_sem=ssem, recv_sem=rsem, device_id=peer, device_id_type=MESH
        )
        copy.start()
        sent.append(copy)

    def arrive(dst, rsem, like):
        pltpu.make_async_copy(like, dst, rsem).wait()

    def to_core(yy, hh):
        for half in range(2):
            block = g_ref.at[c, yy, hh, half]
            send(block, block, c_send.at[yy, hh, half], c_recv.at[yy, hh, half], core)

    send(a_ref, ao_ref.at[xi], xd_send.at[0], xd_recv.at[0], {"x": up_x})
    send(a_ref, ao_ref.at[xi], xd_send.at[1], xd_recv.at[1], {"x": dn_x})
    send(b_ref.at[0], relay_ref.at[0], z_send.at[0], z_recv.at[0], up_z)
    send(b_ref.at[1], relay_ref.at[1], z_send.at[1], z_recv.at[1], dn_z)
    send(b_ref, g_ref.at[c, y, h], yd_send.at[0, 0], yd_recv.at[0, 0], {"y": up_y})
    send(b_ref, g_ref.at[c, y, h], yd_send.at[1, 0], yd_recv.at[1, 0], {"y": dn_y})
    for half in range(2):
        send(b_ref.at[half], g_ref.at[c, y, h, half], c_send.at[y, h, half], c_recv.at[y, h, half], core)
    arrive(ao_ref.at[dn_x], xd_recv.at[0], a_ref)
    src = ao_ref.at[dn_x, a_half[0]]
    send(src, src, xr_send.at[0], xr_recv.at[0], {"x": up_x})
    arrive(ao_ref.at[up_x], xd_recv.at[1], a_ref)
    src = ao_ref.at[up_x, a_half[1]]
    send(src, src, xr_send.at[1], xr_recv.at[1], {"x": dn_x})
    arrive(relay_ref.at[0], z_recv.at[0], b_ref.at[0])
    send(relay_ref.at[0], g_ref.at[c, y, 1 - up_h, 0], z_send.at[2], z_recv.at[2], up_z)
    arrive(relay_ref.at[1], z_recv.at[1], b_ref.at[1])
    send(relay_ref.at[1], g_ref.at[c, y, 1 - dn_h, 1], z_send.at[3], z_recv.at[3], dn_z)
    arrive(g_ref.at[c, y, 1 - h, 0], z_recv.at[2], b_ref.at[0])
    arrive(g_ref.at[c, y, 1 - h, 1], z_recv.at[3], b_ref.at[1])
    src = g_ref.at[c, y, 1 - h]
    send(src, src, yd_send.at[0, 1], yd_recv.at[0, 1], {"y": up_y})
    send(src, src, yd_send.at[1, 1], yd_recv.at[1, 1], {"y": dn_y})
    to_core(y, 1 - h)
    for direction, origin, target in ((0, dn_y, up_y), (1, up_y, dn_y)):
        for k, hh in ((0, h), (1, 1 - h)):
            arrive(g_ref.at[c, origin, hh], yd_recv.at[direction, k], b_ref)
            src = g_ref.at[c, origin, hh, direction]
            send(src, src, yr_send.at[direction, k], yr_recv.at[direction, k], {"y": target})
            to_core(origin, hh)
    for k, hh in ((0, h), (1, 1 - h)):
        for direction in range(2):
            arrive(g_ref.at[c, far_y, hh, direction], yr_recv.at[direction, k], b_ref.at[0])
        to_core(far_y, hh)
    arrive(ao_ref.at[far_x, a_half[0]], xr_recv.at[0], a_ref.at[a_half[0]])
    arrive(ao_ref.at[far_x, a_half[1]], xr_recv.at[1], a_ref.at[a_half[1]])
    for yy in range(ny):
        for hh in range(ROW_SPLIT[0]):
            for half in range(2):
                arrive(g_ref.at[1 - c, yy, hh, half], c_recv.at[yy, hh, half], b_ref.at[0])
    for copy in sent:
        copy.wait_send()


def row_exchange(a, b):
    nx = COL_SPLIT[1]
    nh, ny, nc = ROW_SPLIT
    a_out = (nx,) + a.shape
    b_out = (nc, ny, nh) + b.shape
    nbytes = 2 * (math.prod(a_out) + math.prod(b_out)) * a.dtype.itemsize
    sem_shapes = [(2,), (2,), (4,), (2, 2), (2, 2), (ny, nh, 2)]
    ao, g, _ = pl.pallas_call(
        row_kernel,
        out_shape=[
            jax.ShapeDtypeStruct(a_out, a.dtype),
            jax.ShapeDtypeStruct(b_out, b.dtype),
            jax.ShapeDtypeStruct(b.shape, b.dtype),
        ],
        in_specs=[pl.BlockSpec(memory_space=pl.ANY)] * 2,
        out_specs=[pl.BlockSpec(memory_space=pl.ANY)] * 3,
        scratch_shapes=[pltpu.SemaphoreType.DMA(shape) for shape in sem_shapes for _ in range(2)],
        compiler_params=pltpu.CompilerParams(collective_id=7, has_side_effects=True),
        cost_estimate=pl.CostEstimate(flops=0, transcendentals=0, bytes_accessed=nbytes),
        name="row_exchange",
    )(a, b)
    xi = lax.axis_index("x")
    h, y, c = lax.axis_index("z_hi"), lax.axis_index("y"), lax.axis_index("core")
    ao = lax.dynamic_update_slice_in_dim(ao, a[None], xi, axis=0)
    g = lax.dynamic_update_slice(g, b[None, None, None], (c, y, h) + (0,) * b.ndim)
    return ao, g


def body(amplitudes, packed_tiles, tile_ids, residual_in):
    per_device = packed_tiles.shape[1]
    tile = packed_tiles.shape[2]
    col_count = COL_SPLIT[0] * COL_SPLIT[1]
    own_ids = tile_ids[0]
    target_col = own_ids // per_device
    chooser = (jnp.arange(col_count)[:, None] == target_col[None, :]).astype(jnp.bfloat16)
    outgoing = jnp.einsum("sl,lij->sij", chooser, packed_tiles[0], preferred_element_type=jnp.float32)
    outgoing = outgoing.astype(jnp.bfloat16)
    incoming, a, all_ids = exchange(
        [outgoing, amplitudes, tile_ids],
        [("a2a", COL_AXES, COL_SPLIT), ("line", ("z_lo",), (COL_SPLIT[0],)), ("gather", COL_AXES, COL_SPLIT)],
        3,
    )
    me = _index(COL_AXES, COL_SPLIT)
    all_ids = all_ids.reshape(col_count, per_device)
    mine = (all_ids // per_device) == me
    tags = jnp.sum(jnp.where(mine, all_ids % per_device + 1, 0), axis=1)
    unpack = (jnp.arange(per_device)[:, None] + 1 == tags[None, :]).astype(jnp.bfloat16)
    unpacked = jnp.einsum(
        "ps,sij->pij", unpack, incoming, preferred_element_type=jnp.float32
    ).astype(jnp.bfloat16)
    kt = 2
    qt = per_device // kt
    block = unpacked.reshape(kt, qt, tile, tile).transpose(0, 2, 1, 3).reshape(kt, tile, qt * tile)
    a, g = row_exchange(a, block)
    a = a.reshape(2, 2, 2, 4, a.shape[2], a.shape[3])
    product = jnp.einsum("ckhypj,cyhkjn->pn", a, g, preferred_element_type=jnp.float32)
    return residual_in + product


def solution(mesh):
    devices = mesh.devices.reshape(ROW_SPLIT + COL_SPLIT)
    fine = Mesh(devices, ROW_AXES + COL_AXES)
    row, col = ROW_AXES, COL_AXES
    in_specs = (P(row, col), P(row, col, None, None), P(row, col), P(row, col))
    out_specs = P(row, col)
    return jax.shard_map(body, mesh=fine, in_specs=in_specs, out_specs=out_specs, check_vma=False)
```

```python
import functools
import math

import jax
import jax.numpy as jnp
from jax import lax
from jax.experimental import pallas as pl
from jax.experimental.pallas import tpu as pltpu
from jax.sharding import Mesh
from jax.sharding import PartitionSpec as P

ROW_AXES = ("z_hi", "y", "core")
COL_AXES = ("z_lo", "x")
ROW_SPLIT = (2, 4, 2)
COL_SPLIT = (8, 4)
MESH = pl.DeviceIdType.MESH


def _index(axes, sizes):
    index = 0
    for axis, size in zip(axes, sizes):
        index = index * size + lax.axis_index(axis)
    return index


def _device(axes, sizes, flat):
    coords = {}
    for axis, size in reversed(list(zip(axes, sizes))):
        coords[axis] = lax.rem(flat, size)
        flat = flat // size
    return coords


def exchange_kernel(groups, *refs):
    count = len(groups)
    x_refs, o_refs = refs[:count], refs[count:2 * count]
    send_sem, recv_sem, line_send, line_recv, local_sem = refs[2 * count:]
    own = []
    for g, (kind, axes, sizes) in enumerate(groups):
        me = _index(axes, sizes)
        src = x_refs[g].at[me] if kind == "a2a" else x_refs[g]
        copy = pltpu.make_async_copy(src, o_refs[g].at[me], local_sem.at[g])
        copy.start()
        own.append(copy)
    barrier = pltpu.get_barrier_semaphore()
    total = 0
    for kind, axes, sizes in groups:
        n = math.prod(sizes)
        if kind == "line":
            axis = axes[0]
            i = lax.axis_index(axis)

            @pl.when(i > 0)
            def _():
                pl.semaphore_signal(barrier, inc=1, device_id={axis: i - 1}, device_id_type=MESH)

            @pl.when(i < n - 1)
            def _():
                pl.semaphore_signal(barrier, inc=1, device_id={axis: i + 1}, device_id_type=MESH)

            total = total + (i > 0).astype(jnp.int32) + (i < n - 1).astype(jnp.int32)
            continue
        me = _index(axes, sizes)
        for j in range(1, n):
            peer = _device(axes, sizes, lax.rem(me + j, n))
            pl.semaphore_signal(barrier, inc=1, device_id=peer, device_id_type=MESH)
        total = total + (n - 1)
    pl.semaphore_wait(barrier, total)
    copies = []
    slot = 0
    direct = [(g, grp) for g, grp in enumerate(groups) if grp[0] != "line"]
    longest = max([math.prod(sizes) for _, (_, _, sizes) in direct], default=1)
    for j in range(1, longest):
        for g, (kind, axes, sizes) in direct:
            n = math.prod(sizes)
            if j >= n:
                continue
            me = _index(axes, sizes)
            flat = lax.rem(me + j, n)
            src = x_refs[g] if kind == "gather" else x_refs[g].at[flat]
            copy = pltpu.make_async_remote_copy(
                src_ref=src,
                dst_ref=o_refs[g].at[me],
                send_sem=send_sem.at[slot],
                recv_sem=recv_sem.at[slot],
                device_id=_device(axes, sizes, flat),
                device_id_type=MESH,
            )
            copy.start()
            copies.append(copy)
            slot += 1
    for g, (kind, axes, sizes) in enumerate(groups):
        if kind == "line":
            _line_ring(axes[0], sizes[0], x_refs[g], o_refs[g], line_send, line_recv)
    for copy in copies + own:
        copy.wait()


def _line_ring(axis, n, x_ref, o_ref, send_sem, recv_sem):
    i = lax.axis_index(axis)

    def hop(step, direction):
        if direction == 0:
            origin, target, alive = i - step + 1, i + 1, (i + 1 <= n - 1) & (i - step + 1 >= 0)
        else:
            origin, target, alive = i + step - 1, i - 1, (i >= 1) & (i + step - 1 <= n - 1)
        origin = jnp.clip(origin, 0, n - 1)
        src = x_ref if step == 1 else o_ref.at[origin]
        copy = pltpu.make_async_remote_copy(
            src_ref=src,
            dst_ref=o_ref.at[origin],
            send_sem=send_sem.at[direction, step - 1],
            recv_sem=recv_sem.at[direction, step - 1],
            device_id={axis: jnp.clip(target, 0, n - 1)},
            device_id_type=MESH,
        )
        return copy, alive

    def arrival(step, direction):
        origin = i - step if direction == 0 else i + step
        alive = (origin >= 0) & (origin <= n - 1)
        copy = pltpu.make_async_copy(
            x_ref, o_ref.at[jnp.clip(origin, 0, n - 1)], recv_sem.at[direction, step - 1]
        )
        return copy, alive

    sent = []
    for step in range(1, n):
        for direction in (0, 1):
            copy, alive = hop(step, direction)
            pl.when(alive)(copy.start)
            sent.append((copy, alive))
        for direction in (0, 1):
            copy, alive = arrival(step, direction)
            pl.when(alive)(copy.wait)
    for copy, alive in sent:
        pl.when(alive)(copy.wait_send)


def exchange(xs, groups, cid):
    xs, groups = list(xs), list(groups)
    slots = max(1, sum(math.prod(sizes) - 1 for kind, _, sizes in groups if kind != "line"))
    line = max([sizes[0] for kind, _, sizes in groups if kind == "line"], default=2)
    shapes = []
    for x, (kind, _, sizes) in zip(xs, groups):
        shapes.append(x.shape if kind == "a2a" else (math.prod(sizes),) + x.shape)
    nbytes = sum(2 * math.prod(shape) * x.dtype.itemsize for x, shape in zip(xs, shapes))
    outs = pl.pallas_call(
        functools.partial(exchange_kernel, groups),
        out_shape=[jax.ShapeDtypeStruct(shape, x.dtype) for x, shape in zip(xs, shapes)],
        in_specs=[pl.BlockSpec(memory_space=pl.ANY)] * len(xs),
        out_specs=[pl.BlockSpec(memory_space=pl.ANY)] * len(xs),
        scratch_shapes=[
            pltpu.SemaphoreType.DMA((slots,)),
            pltpu.SemaphoreType.DMA((slots,)),
            pltpu.SemaphoreType.DMA((2, line - 1)),
            pltpu.SemaphoreType.DMA((2, line - 1)),
            pltpu.SemaphoreType.DMA((len(xs),)),
        ],
        compiler_params=pltpu.CompilerParams(collective_id=cid, has_side_effects=True),
        cost_estimate=pl.CostEstimate(flops=0, transcendentals=0, bytes_accessed=nbytes),
        name="exchange_" + "_".join("".join(axes) for _, axes, _ in groups),
    )(*xs)
    return list(outs)


def gather(xs, groups, cid):
    return exchange(xs, [("gather", (axis,), (n,)) for axis, n in groups], cid)


def row_kernel(a_ref, b_ref, ao_ref, g_ref, *sems):
    xd_send, xd_recv, xr_send, xr_recv, z_send, z_recv, yd_send, yd_recv, yr_send, yr_recv, c_send, c_recv = sems[:12]
    local_sem = sems[12]
    nx, ny = COL_SPLIT[1], ROW_SPLIT[1]
    h, y, c = lax.axis_index("z_hi"), lax.axis_index("y"), lax.axis_index("core")
    xi = lax.axis_index("x")
    up_x, dn_x, far_x = lax.rem(xi + 1, nx), lax.rem(xi + nx - 1, nx), lax.rem(xi + 2, nx)
    up_y, dn_y, far_y = lax.rem(y + 1, ny), lax.rem(y + ny - 1, ny), lax.rem(y + 2, ny)
    core, zpeer = {"core": 1 - c}, {"z_hi": 1 - h}
    peers = [zpeer, core, {"y": up_y}, {"y": dn_y}, {"x": up_x}, {"x": dn_x}]
    barrier = pltpu.get_barrier_semaphore()
    for peer in peers:
        pl.semaphore_signal(barrier, inc=1, device_id=peer, device_id_type=MESH)
    pl.semaphore_wait(barrier, len(peers))
    own = [
        pltpu.make_async_copy(a_ref, ao_ref.at[xi], local_sem.at[0]),
        pltpu.make_async_copy(b_ref, g_ref.at[c, y, h], local_sem.at[1]),
    ]
    for copy in own:
        copy.start()
    sent = []
    half_a = a_ref.shape[0] // 2
    a_half = (pl.ds(0, half_a), pl.ds(half_a, half_a))

    def send(src, dst, ssem, rsem, peer):
        copy = pltpu.make_async_remote_copy(
            src_ref=src, dst_ref=dst, send_sem=ssem, recv_sem=rsem, device_id=peer, device_id_type=MESH
        )
        copy.start()
        sent.append(copy)

    def arrive(dst, rsem, like):
        pltpu.make_async_copy(like, dst, rsem).wait()

    def to_core(yy, hh):
        for half in range(2):
            block = g_ref.at[c, yy, hh, half]
            send(block, block, c_send.at[yy, hh, half], c_recv.at[yy, hh, half], core)

    send(a_ref, ao_ref.at[xi], xd_send.at[0], xd_recv.at[0], {"x": up_x})
    send(a_ref, ao_ref.at[xi], xd_send.at[1], xd_recv.at[1], {"x": dn_x})
    send(b_ref, g_ref.at[c, y, h], z_send.at[0], z_recv.at[0], zpeer)
    send(b_ref, g_ref.at[c, y, h], yd_send.at[0, 0], yd_recv.at[0, 0], {"y": up_y})
    send(b_ref, g_ref.at[c, y, h], yd_send.at[1, 0], yd_recv.at[1, 0], {"y": dn_y})
    for half in range(2):
        send(b_ref.at[half], g_ref.at[c, y, h, half], c_send.at[y, h, half], c_recv.at[y, h, half], core)
    arrive(ao_ref.at[dn_x], xd_recv.at[0], a_ref)
    src = ao_ref.at[dn_x, a_half[0]]
    send(src, src, xr_send.at[0], xr_recv.at[0], {"x": up_x})
    arrive(ao_ref.at[up_x], xd_recv.at[1], a_ref)
    src = ao_ref.at[up_x, a_half[1]]
    send(src, src, xr_send.at[1], xr_recv.at[1], {"x": dn_x})
    arrive(g_ref.at[c, y, 1 - h], z_recv.at[0], b_ref)
    src = g_ref.at[c, y, 1 - h]
    send(src, src, yd_send.at[0, 1], yd_recv.at[0, 1], {"y": up_y})
    send(src, src, yd_send.at[1, 1], yd_recv.at[1, 1], {"y": dn_y})
    to_core(y, 1 - h)
    for direction, origin, target in ((0, dn_y, up_y), (1, up_y, dn_y)):
        for k, hh in ((0, h), (1, 1 - h)):
            arrive(g_ref.at[c, origin, hh], yd_recv.at[direction, k], b_ref)
            src = g_ref.at[c, origin, hh, direction]
            send(src, src, yr_send.at[direction, k], yr_recv.at[direction, k], {"y": target})
            to_core(origin, hh)
    for k, hh in ((0, h), (1, 1 - h)):
        for direction in range(2):
            arrive(g_ref.at[c, far_y, hh, direction], yr_recv.at[direction, k], b_ref.at[0])
        to_core(far_y, hh)
    arrive(ao_ref.at[far_x, a_half[0]], xr_recv.at[0], a_ref.at[a_half[0]])
    arrive(ao_ref.at[far_x, a_half[1]], xr_recv.at[1], a_ref.at[a_half[1]])
    for yy in range(ny):
        for hh in range(ROW_SPLIT[0]):
            for half in range(2):
                arrive(g_ref.at[1 - c, yy, hh, half], c_recv.at[yy, hh, half], b_ref.at[0])
    for copy in sent:
        copy.wait_send()
    for copy in own:
        copy.wait()


def row_exchange(a, b):
    nx = COL_SPLIT[1]
    nh, ny, nc = ROW_SPLIT
    a_out = (nx,) + a.shape
    b_out = (nc, ny, nh) + b.shape
    nbytes = 2 * (math.prod(a_out) + math.prod(b_out)) * a.dtype.itemsize
    sem_shapes = [(2,), (2,), (1,), (2, 2), (2, 2), (ny, nh, 2)]
    ao, g = pl.pallas_call(
        row_kernel,
        out_shape=[jax.ShapeDtypeStruct(a_out, a.dtype), jax.ShapeDtypeStruct(b_out, b.dtype)],
        in_specs=[pl.BlockSpec(memory_space=pl.ANY)] * 2,
        out_specs=[pl.BlockSpec(memory_space=pl.ANY)] * 2,
        scratch_shapes=[pltpu.SemaphoreType.DMA(shape) for shape in sem_shapes for _ in range(2)]
        + [pltpu.SemaphoreType.DMA((2,))],
        compiler_params=pltpu.CompilerParams(collective_id=7, has_side_effects=True),
        cost_estimate=pl.CostEstimate(flops=0, transcendentals=0, bytes_accessed=nbytes),
        name="row_exchange",
    )(a, b)
    return ao, g


def body(amplitudes, packed_tiles, tile_ids, residual_in):
    per_device = packed_tiles.shape[1]
    tile = packed_tiles.shape[2]
    col_count = COL_SPLIT[0] * COL_SPLIT[1]
    own_ids = tile_ids[0]
    target_col = own_ids // per_device
    chooser = (jnp.arange(col_count)[:, None] == target_col[None, :]).astype(jnp.bfloat16)
    outgoing = jnp.einsum("sl,lij->sij", chooser, packed_tiles[0], preferred_element_type=jnp.float32)
    outgoing = outgoing.astype(jnp.bfloat16)
    incoming, a, all_ids = exchange(
        [outgoing, amplitudes, tile_ids],
        [("a2a", COL_AXES, COL_SPLIT), ("line", ("z_lo",), (COL_SPLIT[0],)), ("gather", COL_AXES, COL_SPLIT)],
        3,
    )
    me = _index(COL_AXES, COL_SPLIT)
    all_ids = all_ids.reshape(col_count, per_device)
    mine = (all_ids // per_device) == me
    tags = jnp.sum(jnp.where(mine, all_ids % per_device + 1, 0), axis=1)
    unpack = (jnp.arange(per_device)[:, None] + 1 == tags[None, :]).astype(jnp.bfloat16)
    unpacked = jnp.einsum(
        "ps,sij->pij", unpack, incoming, preferred_element_type=jnp.float32
    ).astype(jnp.bfloat16)
    kt = 2
    qt = per_device // kt
    block = unpacked.reshape(kt, qt, tile, tile).transpose(0, 2, 1, 3).reshape(kt, tile, qt * tile)
    a, g = row_exchange(a, block)
    a = a.reshape(2, 2, 2, 4, a.shape[2], a.shape[3])
    product = jnp.einsum("ckhypj,cyhkjn->pn", a, g, preferred_element_type=jnp.float32)
    return residual_in + product


def solution(mesh):
    devices = mesh.devices.reshape(ROW_SPLIT + COL_SPLIT)
    fine = Mesh(devices, ROW_AXES + COL_AXES)
    row, col = ROW_AXES, COL_AXES
    in_specs = (P(row, col), P(row, col, None, None), P(row, col), P(row, col))
    out_specs = P(row, col)
    return jax.shard_map(body, mesh=fine, in_specs=in_specs, out_specs=out_specs, check_vma=False)
```

```python
import functools
import math

import jax
import jax.numpy as jnp
from jax import lax
from jax.experimental import pallas as pl
from jax.experimental.pallas import tpu as pltpu
from jax.sharding import Mesh
from jax.sharding import PartitionSpec as P

ROW_AXES = ("z_hi", "y", "core")
COL_AXES = ("z_lo", "x")
ROW_SPLIT = (2, 4, 2)
COL_SPLIT = (8, 4)
MESH = pl.DeviceIdType.MESH


def _index(axes, sizes):
    index = 0
    for axis, size in zip(axes, sizes):
        index = index * size + lax.axis_index(axis)
    return index


def _device(axes, sizes, flat):
    coords = {}
    for axis, size in reversed(list(zip(axes, sizes))):
        coords[axis] = lax.rem(flat, size)
        flat = flat // size
    return coords


def exchange_kernel(groups, *refs):
    count = len(groups)
    x_refs, o_refs = refs[:count], refs[count:2 * count]
    send_sem, recv_sem, line_send, line_recv, local_sem = refs[2 * count:]
    own = []
    for g, (kind, axes, sizes) in enumerate(groups):
        me = _index(axes, sizes)
        src = x_refs[g].at[me] if kind == "a2a" else x_refs[g]
        copy = pltpu.make_async_copy(src, o_refs[g].at[me], local_sem.at[g])
        copy.start()
        own.append(copy)
    barrier = pltpu.get_barrier_semaphore()
    total = 0
    for kind, axes, sizes in groups:
        n = math.prod(sizes)
        if kind == "line":
            axis = axes[0]
            i = lax.axis_index(axis)

            @pl.when(i > 0)
            def _():
                pl.semaphore_signal(barrier, inc=1, device_id={axis: i - 1}, device_id_type=MESH)

            @pl.when(i < n - 1)
            def _():
                pl.semaphore_signal(barrier, inc=1, device_id={axis: i + 1}, device_id_type=MESH)

            total = total + (i > 0).astype(jnp.int32) + (i < n - 1).astype(jnp.int32)
            continue
        me = _index(axes, sizes)
        for j in range(1, n):
            peer = _device(axes, sizes, lax.rem(me + j, n))
            pl.semaphore_signal(barrier, inc=1, device_id=peer, device_id_type=MESH)
        total = total + (n - 1)
    pl.semaphore_wait(barrier, total)
    copies = []
    slot = 0
    direct = [(g, grp) for g, grp in enumerate(groups) if grp[0] != "line"]
    longest = max([math.prod(sizes) for _, (_, _, sizes) in direct], default=1)
    starts = []
    for j in range(1, longest):
        for g, (kind, axes, sizes) in direct:
            n = math.prod(sizes)
            if j >= n:
                continue
            me = _index(axes, sizes)
            flat = lax.rem(me + j, n)
            src = x_refs[g] if kind == "gather" else x_refs[g].at[flat]
            copy = pltpu.make_async_remote_copy(
                src_ref=src,
                dst_ref=o_refs[g].at[me],
                send_sem=send_sem.at[slot],
                recv_sem=recv_sem.at[slot],
                device_id=_device(axes, sizes, flat),
                device_id_type=MESH,
            )
            starts.append(copy.start)
            copies.append(copy)
            slot += 1
    lines = [(g, grp) for g, grp in enumerate(groups) if grp[0] == "line"]
    if lines:
        g, (_, axes, sizes) = lines[0]
        steps = sizes[0] - 1
        per = -(-len(starts) // steps)
        batches = [starts[k * per:(k + 1) * per] for k in range(steps)]
        _line_ring(axes[0], sizes[0], x_refs[g], o_refs[g], line_send, line_recv, batches)
    else:
        for start in starts:
            start()
    for copy in copies + own:
        copy.wait()


def _line_ring(axis, n, x_ref, o_ref, send_sem, recv_sem, batches):
    i = lax.axis_index(axis)

    def hop(step, direction):
        if direction == 0:
            origin, target, alive = i - step + 1, i + 1, (i + 1 <= n - 1) & (i - step + 1 >= 0)
        else:
            origin, target, alive = i + step - 1, i - 1, (i >= 1) & (i + step - 1 <= n - 1)
        origin = jnp.clip(origin, 0, n - 1)
        src = x_ref if step == 1 else o_ref.at[origin]
        copy = pltpu.make_async_remote_copy(
            src_ref=src,
            dst_ref=o_ref.at[origin],
            send_sem=send_sem.at[direction, step - 1],
            recv_sem=recv_sem.at[direction, step - 1],
            device_id={axis: jnp.clip(target, 0, n - 1)},
            device_id_type=MESH,
        )
        return copy, alive

    def arrival(step, direction):
        origin = i - step if direction == 0 else i + step
        alive = (origin >= 0) & (origin <= n - 1)
        copy = pltpu.make_async_copy(
            x_ref, o_ref.at[jnp.clip(origin, 0, n - 1)], recv_sem.at[direction, step - 1]
        )
        return copy, alive

    sent = []
    for step in range(1, n):
        for direction in (0, 1):
            copy, alive = hop(step, direction)
            pl.when(alive)(copy.start)
            sent.append((copy, alive))
        for start in batches[step - 1]:
            start()
        for direction in (0, 1):
            copy, alive = arrival(step, direction)
            pl.when(alive)(copy.wait)
    for copy, alive in sent:
        pl.when(alive)(copy.wait_send)


def exchange(xs, groups, cid):
    xs, groups = list(xs), list(groups)
    slots = max(1, sum(math.prod(sizes) - 1 for kind, _, sizes in groups if kind != "line"))
    line = max([sizes[0] for kind, _, sizes in groups if kind == "line"], default=2)
    shapes = []
    for x, (kind, _, sizes) in zip(xs, groups):
        shapes.append(x.shape if kind == "a2a" else (math.prod(sizes),) + x.shape)
    nbytes = sum(2 * math.prod(shape) * x.dtype.itemsize for x, shape in zip(xs, shapes))
    outs = pl.pallas_call(
        functools.partial(exchange_kernel, groups),
        out_shape=[jax.ShapeDtypeStruct(shape, x.dtype) for x, shape in zip(xs, shapes)],
        in_specs=[pl.BlockSpec(memory_space=pl.ANY)] * len(xs),
        out_specs=[pl.BlockSpec(memory_space=pl.ANY)] * len(xs),
        scratch_shapes=[
            pltpu.SemaphoreType.DMA((slots,)),
            pltpu.SemaphoreType.DMA((slots,)),
            pltpu.SemaphoreType.DMA((2, line - 1)),
            pltpu.SemaphoreType.DMA((2, line - 1)),
            pltpu.SemaphoreType.DMA((len(xs),)),
        ],
        compiler_params=pltpu.CompilerParams(collective_id=cid, has_side_effects=True),
        cost_estimate=pl.CostEstimate(flops=0, transcendentals=0, bytes_accessed=nbytes),
        name="exchange_" + "_".join("".join(axes) for _, axes, _ in groups),
    )(*xs)
    return list(outs)


def gather(xs, groups, cid):
    return exchange(xs, [("gather", (axis,), (n,)) for axis, n in groups], cid)


def row_kernel(a_ref, b_ref, ao_ref, g_ref, *sems):
    xd_send, xd_recv, xr_send, xr_recv, z_send, z_recv, yd_send, yd_recv, yr_send, yr_recv, c_send, c_recv = sems[:12]
    local_sem = sems[12]
    nx, ny = COL_SPLIT[1], ROW_SPLIT[1]
    h, y, c = lax.axis_index("z_hi"), lax.axis_index("y"), lax.axis_index("core")
    xi = lax.axis_index("x")
    up_x, dn_x, far_x = lax.rem(xi + 1, nx), lax.rem(xi + nx - 1, nx), lax.rem(xi + 2, nx)
    up_y, dn_y, far_y = lax.rem(y + 1, ny), lax.rem(y + ny - 1, ny), lax.rem(y + 2, ny)
    core, zpeer = {"core": 1 - c}, {"z_hi": 1 - h}
    peers = [zpeer, core, {"y": up_y}, {"y": dn_y}, {"x": up_x}, {"x": dn_x}]
    barrier = pltpu.get_barrier_semaphore()
    for peer in peers:
        pl.semaphore_signal(barrier, inc=1, device_id=peer, device_id_type=MESH)
    pl.semaphore_wait(barrier, len(peers))
    own = [
        pltpu.make_async_copy(a_ref, ao_ref.at[xi], local_sem.at[0]),
        pltpu.make_async_copy(b_ref, g_ref.at[c, y, h], local_sem.at[1]),
    ]
    for copy in own:
        copy.start()
    sent = []
    half_a = a_ref.shape[0] // 2
    a_half = (pl.ds(0, half_a), pl.ds(half_a, half_a))

    def send(src, dst, ssem, rsem, peer):
        copy = pltpu.make_async_remote_copy(
            src_ref=src, dst_ref=dst, send_sem=ssem, recv_sem=rsem, device_id=peer, device_id_type=MESH
        )
        copy.start()
        sent.append(copy)

    def arrive(dst, rsem, like):
        pltpu.make_async_copy(like, dst, rsem).wait()

    def to_core(yy, hh):
        for half in range(2):
            block = g_ref.at[c, yy, hh, half]
            send(block, block, c_send.at[yy, hh, half], c_recv.at[yy, hh, half], core)

    send(a_ref, ao_ref.at[xi], xd_send.at[0], xd_recv.at[0], {"x": up_x})
    send(a_ref, ao_ref.at[xi], xd_send.at[1], xd_recv.at[1], {"x": dn_x})
    send(b_ref, g_ref.at[c, y, h], z_send.at[0], z_recv.at[0], zpeer)
    send(b_ref, g_ref.at[c, y, h], yd_send.at[0, 0], yd_recv.at[0, 0], {"y": up_y})
    send(b_ref, g_ref.at[c, y, h], yd_send.at[1, 0], yd_recv.at[1, 0], {"y": dn_y})
    for half in range(2):
        send(b_ref.at[half], g_ref.at[c, y, h, half], c_send.at[y, h, half], c_recv.at[y, h, half], core)
    arrive(ao_ref.at[dn_x], xd_recv.at[0], a_ref)
    src = ao_ref.at[dn_x, a_half[0]]
    send(src, src, xr_send.at[0], xr_recv.at[0], {"x": up_x})
    arrive(ao_ref.at[up_x], xd_recv.at[1], a_ref)
    src = ao_ref.at[up_x, a_half[1]]
    send(src, src, xr_send.at[1], xr_recv.at[1], {"x": dn_x})
    arrive(g_ref.at[c, y, 1 - h], z_recv.at[0], b_ref)
    src = g_ref.at[c, y, 1 - h]
    send(src, src, yd_send.at[0, 1], yd_recv.at[0, 1], {"y": up_y})
    send(src, src, yd_send.at[1, 1], yd_recv.at[1, 1], {"y": dn_y})
    to_core(y, 1 - h)
    for direction, origin, target in ((0, dn_y, up_y), (1, up_y, dn_y)):
        for k, hh in ((0, h), (1, 1 - h)):
            arrive(g_ref.at[c, origin, hh], yd_recv.at[direction, k], b_ref)
            src = g_ref.at[c, origin, hh, direction]
            send(src, src, yr_send.at[direction, k], yr_recv.at[direction, k], {"y": target})
            to_core(origin, hh)
    for k, hh in ((0, h), (1, 1 - h)):
        for direction in range(2):
            arrive(g_ref.at[c, far_y, hh, direction], yr_recv.at[direction, k], b_ref.at[0])
        to_core(far_y, hh)
    arrive(ao_ref.at[far_x, a_half[0]], xr_recv.at[0], a_ref.at[a_half[0]])
    arrive(ao_ref.at[far_x, a_half[1]], xr_recv.at[1], a_ref.at[a_half[1]])
    for yy in range(ny):
        for hh in range(ROW_SPLIT[0]):
            for half in range(2):
                arrive(g_ref.at[1 - c, yy, hh, half], c_recv.at[yy, hh, half], b_ref.at[0])
    for copy in sent:
        copy.wait_send()
    for copy in own:
        copy.wait()


def row_exchange(a, b):
    nx = COL_SPLIT[1]
    nh, ny, nc = ROW_SPLIT
    a_out = (nx,) + a.shape
    b_out = (nc, ny, nh) + b.shape
    nbytes = 2 * (math.prod(a_out) + math.prod(b_out)) * a.dtype.itemsize
    sem_shapes = [(2,), (2,), (1,), (2, 2), (2, 2), (ny, nh, 2)]
    ao, g = pl.pallas_call(
        row_kernel,
        out_shape=[jax.ShapeDtypeStruct(a_out, a.dtype), jax.ShapeDtypeStruct(b_out, b.dtype)],
        in_specs=[pl.BlockSpec(memory_space=pl.ANY)] * 2,
        out_specs=[pl.BlockSpec(memory_space=pl.ANY)] * 2,
        scratch_shapes=[pltpu.SemaphoreType.DMA(shape) for shape in sem_shapes for _ in range(2)]
        + [pltpu.SemaphoreType.DMA((2,))],
        compiler_params=pltpu.CompilerParams(collective_id=7, has_side_effects=True),
        cost_estimate=pl.CostEstimate(flops=0, transcendentals=0, bytes_accessed=nbytes),
        name="row_exchange",
    )(a, b)
    return ao, g


def body(amplitudes, packed_tiles, tile_ids, residual_in):
    per_device = packed_tiles.shape[1]
    tile = packed_tiles.shape[2]
    col_count = COL_SPLIT[0] * COL_SPLIT[1]
    own_ids = tile_ids[0]
    target_col = own_ids // per_device
    chooser = (jnp.arange(col_count)[:, None] == target_col[None, :]).astype(jnp.bfloat16)
    outgoing = jnp.einsum("sl,lij->sij", chooser, packed_tiles[0], preferred_element_type=jnp.float32)
    outgoing = outgoing.astype(jnp.bfloat16)
    incoming, a, all_ids = exchange(
        [outgoing, amplitudes, tile_ids],
        [("a2a", COL_AXES, COL_SPLIT), ("line", ("z_lo",), (COL_SPLIT[0],)), ("gather", COL_AXES, COL_SPLIT)],
        3,
    )
    me = _index(COL_AXES, COL_SPLIT)
    all_ids = all_ids.reshape(col_count, per_device)
    mine = (all_ids // per_device) == me
    tags = jnp.sum(jnp.where(mine, all_ids % per_device + 1, 0), axis=1)
    unpack = (jnp.arange(per_device)[:, None] + 1 == tags[None, :]).astype(jnp.bfloat16)
    unpacked = jnp.einsum(
        "ps,sij->pij", unpack, incoming, preferred_element_type=jnp.float32
    ).astype(jnp.bfloat16)
    kt = 2
    qt = per_device // kt
    block = unpacked.reshape(kt, qt, tile, tile).transpose(0, 2, 1, 3).reshape(kt, tile, qt * tile)
    a, g = row_exchange(a, block)
    a = a.reshape(2, 2, 2, 4, a.shape[2], a.shape[3])
    product = jnp.einsum("ckhypj,cyhkjn->pn", a, g, preferred_element_type=jnp.float32)
    return residual_in + product


def solution(mesh):
    devices = mesh.devices.reshape(ROW_SPLIT + COL_SPLIT)
    fine = Mesh(devices, ROW_AXES + COL_AXES)
    row, col = ROW_AXES, COL_AXES
    in_specs = (P(row, col), P(row, col, None, None), P(row, col), P(row, col))
    out_specs = P(row, col)
    return jax.shard_map(body, mesh=fine, in_specs=in_specs, out_specs=out_specs, check_vma=False)
```

```python
import functools
import math

import jax
import jax.numpy as jnp
from jax import lax
from jax.experimental import pallas as pl
from jax.experimental.pallas import tpu as pltpu
from jax.sharding import Mesh
from jax.sharding import PartitionSpec as P

ROW_AXES = ("z_hi", "y", "core")
COL_AXES = ("z_lo", "x")
ROW_SPLIT = (2, 4, 2)
COL_SPLIT = (8, 4)
MESH = pl.DeviceIdType.MESH


def _index(axes, sizes):
    index = 0
    for axis, size in zip(axes, sizes):
        index = index * size + lax.axis_index(axis)
    return index


def _device(axes, sizes, flat):
    coords = {}
    for axis, size in reversed(list(zip(axes, sizes))):
        coords[axis] = lax.rem(flat, size)
        flat = flat // size
    return coords


def exchange_kernel(groups, *refs):
    count = len(groups)
    x_refs, o_refs = refs[:count], refs[count:2 * count]
    send_sem, recv_sem, line_send, line_recv, local_sem = refs[2 * count:]
    own = []
    for g, (kind, axes, sizes) in enumerate(groups):
        me = _index(axes, sizes)
        src = x_refs[g].at[me] if kind == "a2a" else x_refs[g]
        copy = pltpu.make_async_copy(src, o_refs[g].at[me], local_sem.at[g])
        copy.start()
        own.append(copy)
    barrier = pltpu.get_barrier_semaphore()
    total = 0
    for kind, axes, sizes in groups:
        n = math.prod(sizes)
        if kind == "line":
            axis = axes[0]
            i = lax.axis_index(axis)

            @pl.when(i > 0)
            def _():
                pl.semaphore_signal(barrier, inc=1, device_id={axis: i - 1}, device_id_type=MESH)

            @pl.when(i < n - 1)
            def _():
                pl.semaphore_signal(barrier, inc=1, device_id={axis: i + 1}, device_id_type=MESH)

            total = total + (i > 0).astype(jnp.int32) + (i < n - 1).astype(jnp.int32)
            continue
        me = _index(axes, sizes)
        for j in range(1, n):
            peer = _device(axes, sizes, lax.rem(me + j, n))
            pl.semaphore_signal(barrier, inc=1, device_id=peer, device_id_type=MESH)
        total = total + (n - 1)
    pl.semaphore_wait(barrier, total)
    copies = []
    slot = 0
    direct = [(g, grp) for g, grp in enumerate(groups) if grp[0] != "line"]
    longest = max([math.prod(sizes) for _, (_, _, sizes) in direct], default=1)
    for j in range(1, longest):
        for g, (kind, axes, sizes) in direct:
            n = math.prod(sizes)
            if j >= n:
                continue
            me = _index(axes, sizes)
            flat = lax.rem(me + j, n)
            src = x_refs[g] if kind == "gather" else x_refs[g].at[flat]
            copy = pltpu.make_async_remote_copy(
                src_ref=src,
                dst_ref=o_refs[g].at[me],
                send_sem=send_sem.at[slot],
                recv_sem=recv_sem.at[slot],
                device_id=_device(axes, sizes, flat),
                device_id_type=MESH,
            )
            copy.start()
            copies.append(copy)
            slot += 1
    for g, (kind, axes, sizes) in enumerate(groups):
        if kind == "line":
            _line_ring(axes[0], sizes[0], x_refs[g], o_refs[g], line_send, line_recv)
    for copy in copies + own:
        copy.wait()


def _line_ring(axis, n, x_ref, o_ref, send_sem, recv_sem):
    i = lax.axis_index(axis)

    def hop(step, direction):
        if direction == 0:
            origin, target, alive = i - step + 1, i + 1, (i + 1 <= n - 1) & (i - step + 1 >= 0)
        else:
            origin, target, alive = i + step - 1, i - 1, (i >= 1) & (i + step - 1 <= n - 1)
        origin = jnp.clip(origin, 0, n - 1)
        src = x_ref if step == 1 else o_ref.at[origin]
        copy = pltpu.make_async_remote_copy(
            src_ref=src,
            dst_ref=o_ref.at[origin],
            send_sem=send_sem.at[direction, step - 1],
            recv_sem=recv_sem.at[direction, step - 1],
            device_id={axis: jnp.clip(target, 0, n - 1)},
            device_id_type=MESH,
        )
        return copy, alive

    def arrival(step, direction):
        origin = i - step if direction == 0 else i + step
        alive = (origin >= 0) & (origin <= n - 1)
        copy = pltpu.make_async_copy(
            x_ref, o_ref.at[jnp.clip(origin, 0, n - 1)], recv_sem.at[direction, step - 1]
        )
        return copy, alive

    sent = []
    for step in range(1, n):
        for direction in (0, 1):
            copy, alive = hop(step, direction)
            pl.when(alive)(copy.start)
            sent.append((copy, alive))
        for direction in (0, 1):
            copy, alive = arrival(step, direction)
            pl.when(alive)(copy.wait)
    for copy, alive in sent:
        pl.when(alive)(copy.wait_send)


def exchange(xs, groups, cid):
    xs, groups = list(xs), list(groups)
    slots = max(1, sum(math.prod(sizes) - 1 for kind, _, sizes in groups if kind != "line"))
    line = max([sizes[0] for kind, _, sizes in groups if kind == "line"], default=2)
    shapes = []
    for x, (kind, _, sizes) in zip(xs, groups):
        shapes.append(x.shape if kind == "a2a" else (math.prod(sizes),) + x.shape)
    nbytes = sum(2 * math.prod(shape) * x.dtype.itemsize for x, shape in zip(xs, shapes))
    outs = pl.pallas_call(
        functools.partial(exchange_kernel, groups),
        out_shape=[jax.ShapeDtypeStruct(shape, x.dtype) for x, shape in zip(xs, shapes)],
        in_specs=[pl.BlockSpec(memory_space=pl.ANY)] * len(xs),
        out_specs=[pl.BlockSpec(memory_space=pl.ANY)] * len(xs),
        scratch_shapes=[
            pltpu.SemaphoreType.DMA((slots,)),
            pltpu.SemaphoreType.DMA((slots,)),
            pltpu.SemaphoreType.DMA((2, line - 1)),
            pltpu.SemaphoreType.DMA((2, line - 1)),
            pltpu.SemaphoreType.DMA((len(xs),)),
        ],
        compiler_params=pltpu.CompilerParams(collective_id=cid, has_side_effects=True),
        cost_estimate=pl.CostEstimate(flops=0, transcendentals=0, bytes_accessed=nbytes),
        name="exchange_" + "_".join("".join(axes) for _, axes, _ in groups),
    )(*xs)
    return list(outs)


def gather(xs, groups, cid):
    return exchange(xs, [("gather", (axis,), (n,)) for axis, n in groups], cid)


def row_kernel(a_ref, b_ref, ao_ref, g_ref, *sems):
    xd_send, xd_recv, xr_send, xr_recv, z_send, z_recv, yd_send, yd_recv, yr_send, yr_recv, c_send, c_recv = sems[:12]
    local_sem = sems[12]
    nx, ny = COL_SPLIT[1], ROW_SPLIT[1]
    h, y, c = lax.axis_index("z_hi"), lax.axis_index("y"), lax.axis_index("core")
    xi = lax.axis_index("x")
    up_x, dn_x, far_x = lax.rem(xi + 1, nx), lax.rem(xi + nx - 1, nx), lax.rem(xi + 2, nx)
    up_y, dn_y, far_y = lax.rem(y + 1, ny), lax.rem(y + ny - 1, ny), lax.rem(y + 2, ny)
    core, zpeer = {"core": 1 - c}, {"z_hi": 1 - h}
    peers = [zpeer, core, {"y": up_y}, {"y": dn_y}, {"x": up_x}, {"x": dn_x}]
    barrier = pltpu.get_barrier_semaphore()
    for peer in peers:
        pl.semaphore_signal(barrier, inc=1, device_id=peer, device_id_type=MESH)
    pl.semaphore_wait(barrier, len(peers))
    own = [
        pltpu.make_async_copy(a_ref, ao_ref.at[xi], local_sem.at[0]),
        pltpu.make_async_copy(b_ref, g_ref.at[c, y, h], local_sem.at[1]),
    ]
    for copy in own:
        copy.start()
    sent = []
    half_a = a_ref.shape[0] // 2
    a_half = (pl.ds(0, half_a), pl.ds(half_a, half_a))

    def send(src, dst, ssem, rsem, peer):
        copy = pltpu.make_async_remote_copy(
            src_ref=src, dst_ref=dst, send_sem=ssem, recv_sem=rsem, device_id=peer, device_id_type=MESH
        )
        copy.start()
        sent.append(copy)

    def arrive(dst, rsem, like):
        pltpu.make_async_copy(like, dst, rsem).wait()

    def to_core(yy, hh):
        for half in range(2):
            block = g_ref.at[c, yy, hh, half]
            send(block, block, c_send.at[yy, hh, half], c_recv.at[yy, hh, half], core)

    send(a_ref, ao_ref.at[xi], xd_send.at[0], xd_recv.at[0], {"x": up_x})
    send(a_ref, ao_ref.at[xi], xd_send.at[1], xd_recv.at[1], {"x": dn_x})
    for half in range(2):
        send(b_ref.at[half], g_ref.at[c, y, h, half], z_send.at[half], z_recv.at[half], zpeer)
    send(b_ref, g_ref.at[c, y, h], yd_send.at[0, 0], yd_recv.at[0, 0], {"y": up_y})
    send(b_ref, g_ref.at[c, y, h], yd_send.at[1, 0], yd_recv.at[1, 0], {"y": dn_y})
    for half in range(2):
        send(b_ref.at[half], g_ref.at[c, y, h, half], c_send.at[y, h, half], c_recv.at[y, h, half], core)
    arrive(ao_ref.at[dn_x], xd_recv.at[0], a_ref)
    src = ao_ref.at[dn_x, a_half[0]]
    send(src, src, xr_send.at[0], xr_recv.at[0], {"x": up_x})
    arrive(ao_ref.at[up_x], xd_recv.at[1], a_ref)
    src = ao_ref.at[up_x, a_half[1]]
    send(src, src, xr_send.at[1], xr_recv.at[1], {"x": dn_x})
    for half in range(2):
        src = g_ref.at[c, y, 1 - h, half]
        arrive(src, z_recv.at[half], b_ref.at[half])
        send(src, src, yd_send.at[0, 1 + half], yd_recv.at[0, 1], {"y": up_y})
        send(src, src, yd_send.at[1, 1 + half], yd_recv.at[1, 1], {"y": dn_y})
        send(src, src, c_send.at[y, 1 - h, half], c_recv.at[y, 1 - h, half], core)
    for direction, origin, target in ((0, dn_y, up_y), (1, up_y, dn_y)):
        for k, hh in ((0, h), (1, 1 - h)):
            arrive(g_ref.at[c, origin, hh], yd_recv.at[direction, k], b_ref)
            src = g_ref.at[c, origin, hh, direction]
            send(src, src, yr_send.at[direction, k], yr_recv.at[direction, k], {"y": target})
            to_core(origin, hh)
    for k, hh in ((0, h), (1, 1 - h)):
        for direction in range(2):
            arrive(g_ref.at[c, far_y, hh, direction], yr_recv.at[direction, k], b_ref.at[0])
        to_core(far_y, hh)
    arrive(ao_ref.at[far_x, a_half[0]], xr_recv.at[0], a_ref.at[a_half[0]])
    arrive(ao_ref.at[far_x, a_half[1]], xr_recv.at[1], a_ref.at[a_half[1]])
    for yy in range(ny):
        for hh in range(ROW_SPLIT[0]):
            for half in range(2):
                arrive(g_ref.at[1 - c, yy, hh, half], c_recv.at[yy, hh, half], b_ref.at[0])
    for copy in sent:
        copy.wait_send()
    for copy in own:
        copy.wait()


def row_exchange(a, b):
    nx = COL_SPLIT[1]
    nh, ny, nc = ROW_SPLIT
    a_out = (nx,) + a.shape
    b_out = (nc, ny, nh) + b.shape
    nbytes = 2 * (math.prod(a_out) + math.prod(b_out)) * a.dtype.itemsize
    sem_shapes = [(2,), (2,), (2,), (2, 3), (2, 2), (ny, nh, 2)]
    ao, g = pl.pallas_call(
        row_kernel,
        out_shape=[jax.ShapeDtypeStruct(a_out, a.dtype), jax.ShapeDtypeStruct(b_out, b.dtype)],
        in_specs=[pl.BlockSpec(memory_space=pl.ANY)] * 2,
        out_specs=[pl.BlockSpec(memory_space=pl.ANY)] * 2,
        scratch_shapes=[pltpu.SemaphoreType.DMA(shape) for shape in sem_shapes for _ in range(2)]
        + [pltpu.SemaphoreType.DMA((2,))],
        compiler_params=pltpu.CompilerParams(collective_id=7, has_side_effects=True),
        cost_estimate=pl.CostEstimate(flops=0, transcendentals=0, bytes_accessed=nbytes),
        name="row_exchange",
    )(a, b)
    return ao, g


def body(amplitudes, packed_tiles, tile_ids, residual_in):
    per_device = packed_tiles.shape[1]
    tile = packed_tiles.shape[2]
    col_count = COL_SPLIT[0] * COL_SPLIT[1]
    own_ids = tile_ids[0]
    target_col = own_ids // per_device
    chooser = (jnp.arange(col_count)[:, None] == target_col[None, :]).astype(jnp.bfloat16)
    outgoing = jnp.einsum("sl,lij->sij", chooser, packed_tiles[0], preferred_element_type=jnp.float32)
    outgoing = outgoing.astype(jnp.bfloat16)
    incoming, a, all_ids = exchange(
        [outgoing, amplitudes, tile_ids],
        [("a2a", COL_AXES, COL_SPLIT), ("line", ("z_lo",), (COL_SPLIT[0],)), ("gather", COL_AXES, COL_SPLIT)],
        3,
    )
    me = _index(COL_AXES, COL_SPLIT)
    all_ids = all_ids.reshape(col_count, per_device)
    mine = (all_ids // per_device) == me
    tags = jnp.sum(jnp.where(mine, all_ids % per_device + 1, 0), axis=1)
    unpack = (jnp.arange(per_device)[:, None] + 1 == tags[None, :]).astype(jnp.bfloat16)
    unpacked = jnp.einsum(
        "ps,sij->pij", unpack, incoming, preferred_element_type=jnp.float32
    ).astype(jnp.bfloat16)
    kt = 2
    qt = per_device // kt
    block = unpacked.reshape(kt, qt, tile, tile).transpose(0, 2, 1, 3).reshape(kt, tile, qt * tile)
    a, g = row_exchange(a, block)
    a = a.reshape(2, 2, 2, 4, a.shape[2], a.shape[3])
    product = jnp.einsum("ckhypj,cyhkjn->pn", a, g, preferred_element_type=jnp.float32)
    return residual_in + product


def solution(mesh):
    devices = mesh.devices.reshape(ROW_SPLIT + COL_SPLIT)
    fine = Mesh(devices, ROW_AXES + COL_AXES)
    row, col = ROW_AXES, COL_AXES
    in_specs = (P(row, col), P(row, col, None, None), P(row, col), P(row, col))
    out_specs = P(row, col)
    return jax.shard_map(body, mesh=fine, in_specs=in_specs, out_specs=out_specs, check_vma=False)
```

```python
import functools
import math

import jax
import jax.numpy as jnp
from jax import lax
from jax.experimental import pallas as pl
from jax.experimental.pallas import tpu as pltpu
from jax.sharding import Mesh
from jax.sharding import PartitionSpec as P

ROW_AXES = ("z_hi", "y", "core")
COL_AXES = ("z_lo", "x")
ROW_SPLIT = (2, 4, 2)
COL_SPLIT = (8, 4)
MESH = pl.DeviceIdType.MESH


def _index(axes, sizes):
    index = 0
    for axis, size in zip(axes, sizes):
        index = index * size + lax.axis_index(axis)
    return index


def _device(axes, sizes, flat):
    coords = {}
    for axis, size in reversed(list(zip(axes, sizes))):
        coords[axis] = lax.rem(flat, size)
        flat = flat // size
    return coords


def exchange_kernel(groups, *refs):
    count = len(groups)
    x_refs, o_refs = refs[:count], refs[count:2 * count]
    send_sem, recv_sem, line_send, line_recv, local_sem = refs[2 * count:]
    own = []
    for g, (kind, axes, sizes) in enumerate(groups):
        me = _index(axes, sizes)
        src = x_refs[g].at[me] if kind == "a2a" else x_refs[g]
        copy = pltpu.make_async_copy(src, o_refs[g].at[me], local_sem.at[g])
        copy.start()
        own.append(copy)
    barrier = pltpu.get_barrier_semaphore()
    total = 0
    for kind, axes, sizes in groups:
        n = math.prod(sizes)
        if kind == "line":
            axis = axes[0]
            i = lax.axis_index(axis)

            @pl.when(i > 0)
            def _():
                pl.semaphore_signal(barrier, inc=1, device_id={axis: i - 1}, device_id_type=MESH)

            @pl.when(i < n - 1)
            def _():
                pl.semaphore_signal(barrier, inc=1, device_id={axis: i + 1}, device_id_type=MESH)

            total = total + (i > 0).astype(jnp.int32) + (i < n - 1).astype(jnp.int32)
            continue
        me = _index(axes, sizes)
        for j in range(1, n):
            peer = _device(axes, sizes, lax.rem(me + j, n))
            pl.semaphore_signal(barrier, inc=1, device_id=peer, device_id_type=MESH)
        total = total + (n - 1)
    pl.semaphore_wait(barrier, total)
    copies = []
    slot = 0
    direct = [(g, grp) for g, grp in enumerate(groups) if grp[0] != "line"]
    longest = max([math.prod(sizes) for _, (_, _, sizes) in direct], default=1)
    for j in range(1, longest):
        for g, (kind, axes, sizes) in direct:
            n = math.prod(sizes)
            if j >= n:
                continue
            me = _index(axes, sizes)
            flat = lax.rem(me + j, n)
            src = x_refs[g] if kind == "gather" else x_refs[g].at[flat]
            copy = pltpu.make_async_remote_copy(
                src_ref=src,
                dst_ref=o_refs[g].at[me],
                send_sem=send_sem.at[slot],
                recv_sem=recv_sem.at[slot],
                device_id=_device(axes, sizes, flat),
                device_id_type=MESH,
            )
            copy.start()
            copies.append(copy)
            slot += 1
    for g, (kind, axes, sizes) in enumerate(groups):
        if kind == "line":
            _line_ring(axes[0], sizes[0], x_refs[g], o_refs[g], line_send, line_recv)
    for copy in copies + own:
        copy.wait()


def _line_ring(axis, n, x_ref, o_ref, send_sem, recv_sem):
    i = lax.axis_index(axis)

    def hop(step, direction):
        if direction == 0:
            origin, target, alive = i - step + 1, i + 1, (i + 1 <= n - 1) & (i - step + 1 >= 0)
        else:
            origin, target, alive = i + step - 1, i - 1, (i >= 1) & (i + step - 1 <= n - 1)
        origin = jnp.clip(origin, 0, n - 1)
        src = x_ref if step == 1 else o_ref.at[origin]
        copy = pltpu.make_async_remote_copy(
            src_ref=src,
            dst_ref=o_ref.at[origin],
            send_sem=send_sem.at[direction, step - 1],
            recv_sem=recv_sem.at[direction, step - 1],
            device_id={axis: jnp.clip(target, 0, n - 1)},
            device_id_type=MESH,
        )
        return copy, alive

    def arrival(step, direction):
        origin = i - step if direction == 0 else i + step
        alive = (origin >= 0) & (origin <= n - 1)
        copy = pltpu.make_async_copy(
            x_ref, o_ref.at[jnp.clip(origin, 0, n - 1)], recv_sem.at[direction, step - 1]
        )
        return copy, alive

    sent = []
    for step in range(1, n):
        for direction in (0, 1):
            copy, alive = hop(step, direction)
            pl.when(alive)(copy.start)
            sent.append((copy, alive))
        for direction in (0, 1):
            copy, alive = arrival(step, direction)
            pl.when(alive)(copy.wait)
    for copy, alive in sent:
        pl.when(alive)(copy.wait_send)


def exchange(xs, groups, cid):
    xs, groups = list(xs), list(groups)
    slots = max(1, sum(math.prod(sizes) - 1 for kind, _, sizes in groups if kind != "line"))
    line = max([sizes[0] for kind, _, sizes in groups if kind == "line"], default=2)
    shapes = []
    for x, (kind, _, sizes) in zip(xs, groups):
        shapes.append(x.shape if kind == "a2a" else (math.prod(sizes),) + x.shape)
    nbytes = sum(2 * math.prod(shape) * x.dtype.itemsize for x, shape in zip(xs, shapes))
    outs = pl.pallas_call(
        functools.partial(exchange_kernel, groups),
        out_shape=[jax.ShapeDtypeStruct(shape, x.dtype) for x, shape in zip(xs, shapes)],
        in_specs=[pl.BlockSpec(memory_space=pl.ANY)] * len(xs),
        out_specs=[pl.BlockSpec(memory_space=pl.ANY)] * len(xs),
        scratch_shapes=[
            pltpu.SemaphoreType.DMA((slots,)),
            pltpu.SemaphoreType.DMA((slots,)),
            pltpu.SemaphoreType.DMA((2, line - 1)),
            pltpu.SemaphoreType.DMA((2, line - 1)),
            pltpu.SemaphoreType.DMA((len(xs),)),
        ],
        compiler_params=pltpu.CompilerParams(collective_id=cid, has_side_effects=True),
        cost_estimate=pl.CostEstimate(flops=0, transcendentals=0, bytes_accessed=nbytes),
        name="exchange_" + "_".join("".join(axes) for _, axes, _ in groups),
    )(*xs)
    return list(outs)


def gather(xs, groups, cid):
    return exchange(xs, [("gather", (axis,), (n,)) for axis, n in groups], cid)


def row_kernel(a_ref, b_ref, ao_ref, g_ref, *sems):
    xd_send, xd_recv, xr_send, xr_recv, z_send, z_recv, yd_send, yd_recv, yr_send, yr_recv, c_send, c_recv = sems[:12]
    local_sem, piece_send = sems[12], sems[13]
    nx, ny = COL_SPLIT[1], ROW_SPLIT[1]
    h, y, c = lax.axis_index("z_hi"), lax.axis_index("y"), lax.axis_index("core")
    xi = lax.axis_index("x")
    up_x, dn_x, far_x = lax.rem(xi + 1, nx), lax.rem(xi + nx - 1, nx), lax.rem(xi + 2, nx)
    up_y, dn_y, far_y = lax.rem(y + 1, ny), lax.rem(y + ny - 1, ny), lax.rem(y + 2, ny)
    core, zpeer = {"core": 1 - c}, {"z_hi": 1 - h}
    peers = [zpeer, core, {"y": up_y}, {"y": dn_y}, {"x": up_x}, {"x": dn_x}]
    barrier = pltpu.get_barrier_semaphore()
    for peer in peers:
        pl.semaphore_signal(barrier, inc=1, device_id=peer, device_id_type=MESH)
    pl.semaphore_wait(barrier, len(peers))
    own = [
        pltpu.make_async_copy(a_ref, ao_ref.at[xi], local_sem.at[0]),
        pltpu.make_async_copy(b_ref, g_ref.at[c, y, h], local_sem.at[1]),
    ]
    for copy in own:
        copy.start()
    sent = []
    half_a = a_ref.shape[0] // 2
    a_half = (pl.ds(0, half_a), pl.ds(half_a, half_a))

    def send(src, dst, ssem, rsem, peer):
        copy = pltpu.make_async_remote_copy(
            src_ref=src, dst_ref=dst, send_sem=ssem, recv_sem=rsem, device_id=peer, device_id_type=MESH
        )
        copy.start()
        sent.append(copy)

    def arrive(dst, rsem, like):
        pltpu.make_async_copy(like, dst, rsem).wait()

    def to_core(yy, hh):
        for half in range(2):
            block = g_ref.at[c, yy, hh, half]
            send(block, block, c_send.at[yy, hh, half], c_recv.at[yy, hh, half], core)

    send(a_ref, ao_ref.at[xi], xd_send.at[0], xd_recv.at[0], {"x": up_x})
    send(a_ref, ao_ref.at[xi], xd_send.at[1], xd_recv.at[1], {"x": dn_x})
    rows = b_ref.shape[1] // 2
    pieces = [(kk, pl.ds(part * rows, rows)) for kk in range(2) for part in range(2)]
    for p, (kk, span) in enumerate(pieces):
        send(b_ref.at[kk, span], g_ref.at[c, y, h, kk, span], z_send.at[p], z_recv.at[p], zpeer)
    send(b_ref, g_ref.at[c, y, h], yd_send.at[0, 0], yd_recv.at[0, 0], {"y": up_y})
    send(b_ref, g_ref.at[c, y, h], yd_send.at[1, 0], yd_recv.at[1, 0], {"y": dn_y})
    for half in range(2):
        send(b_ref.at[half], g_ref.at[c, y, h, half], c_send.at[y, h, half], c_recv.at[y, h, half], core)
    arrive(ao_ref.at[dn_x], xd_recv.at[0], a_ref)
    src = ao_ref.at[dn_x, a_half[0]]
    send(src, src, xr_send.at[0], xr_recv.at[0], {"x": up_x})
    arrive(ao_ref.at[up_x], xd_recv.at[1], a_ref)
    src = ao_ref.at[up_x, a_half[1]]
    send(src, src, xr_send.at[1], xr_recv.at[1], {"x": dn_x})
    for p, (kk, span) in enumerate(pieces):
        src = g_ref.at[c, y, 1 - h, kk, span]
        arrive(src, z_recv.at[p], b_ref.at[kk, span])
        send(src, src, yd_send.at[0, 1 + p], yd_recv.at[0, 1], {"y": up_y})
        send(src, src, yd_send.at[1, 1 + p], yd_recv.at[1, 1], {"y": dn_y})
        send(src, src, piece_send.at[p], c_recv.at[y, 1 - h, kk], core)
    for direction, origin, target in ((0, dn_y, up_y), (1, up_y, dn_y)):
        for k, hh in ((0, h), (1, 1 - h)):
            arrive(g_ref.at[c, origin, hh], yd_recv.at[direction, k], b_ref)
            src = g_ref.at[c, origin, hh, direction]
            send(src, src, yr_send.at[direction, k], yr_recv.at[direction, k], {"y": target})
            to_core(origin, hh)
    for k, hh in ((0, h), (1, 1 - h)):
        for direction in range(2):
            arrive(g_ref.at[c, far_y, hh, direction], yr_recv.at[direction, k], b_ref.at[0])
        to_core(far_y, hh)
    arrive(ao_ref.at[far_x, a_half[0]], xr_recv.at[0], a_ref.at[a_half[0]])
    arrive(ao_ref.at[far_x, a_half[1]], xr_recv.at[1], a_ref.at[a_half[1]])
    for yy in range(ny):
        for hh in range(ROW_SPLIT[0]):
            for half in range(2):
                arrive(g_ref.at[1 - c, yy, hh, half], c_recv.at[yy, hh, half], b_ref.at[0])
    for copy in sent:
        copy.wait_send()
    for copy in own:
        copy.wait()


def row_exchange(a, b):
    nx = COL_SPLIT[1]
    nh, ny, nc = ROW_SPLIT
    a_out = (nx,) + a.shape
    b_out = (nc, ny, nh) + b.shape
    nbytes = 2 * (math.prod(a_out) + math.prod(b_out)) * a.dtype.itemsize
    sem_shapes = [(2,), (2,), (4,), (2, 5), (2, 2), (ny, nh, 2)]
    ao, g = pl.pallas_call(
        row_kernel,
        out_shape=[jax.ShapeDtypeStruct(a_out, a.dtype), jax.ShapeDtypeStruct(b_out, b.dtype)],
        in_specs=[pl.BlockSpec(memory_space=pl.ANY)] * 2,
        out_specs=[pl.BlockSpec(memory_space=pl.ANY)] * 2,
        scratch_shapes=[pltpu.SemaphoreType.DMA(shape) for shape in sem_shapes for _ in range(2)]
        + [pltpu.SemaphoreType.DMA((2,)), pltpu.SemaphoreType.DMA((4,))],
        compiler_params=pltpu.CompilerParams(collective_id=7, has_side_effects=True),
        cost_estimate=pl.CostEstimate(flops=0, transcendentals=0, bytes_accessed=nbytes),
        name="row_exchange",
    )(a, b)
    return ao, g


def body(amplitudes, packed_tiles, tile_ids, residual_in):
    per_device = packed_tiles.shape[1]
    tile = packed_tiles.shape[2]
    col_count = COL_SPLIT[0] * COL_SPLIT[1]
    own_ids = tile_ids[0]
    target_col = own_ids // per_device
    chooser = (jnp.arange(col_count)[:, None] == target_col[None, :]).astype(jnp.bfloat16)
    outgoing = jnp.einsum("sl,lij->sij", chooser, packed_tiles[0], preferred_element_type=jnp.float32)
    outgoing = outgoing.astype(jnp.bfloat16)
    incoming, a, all_ids = exchange(
        [outgoing, amplitudes, tile_ids],
        [("a2a", COL_AXES, COL_SPLIT), ("line", ("z_lo",), (COL_SPLIT[0],)), ("gather", COL_AXES, COL_SPLIT)],
        3,
    )
    me = _index(COL_AXES, COL_SPLIT)
    all_ids = all_ids.reshape(col_count, per_device)
    mine = (all_ids // per_device) == me
    tags = jnp.sum(jnp.where(mine, all_ids % per_device + 1, 0), axis=1)
    unpack = (jnp.arange(per_device)[:, None] + 1 == tags[None, :]).astype(jnp.bfloat16)
    unpacked = jnp.einsum(
        "ps,sij->pij", unpack, incoming, preferred_element_type=jnp.float32
    ).astype(jnp.bfloat16)
    kt = 2
    qt = per_device // kt
    block = unpacked.reshape(kt, qt, tile, tile).transpose(0, 2, 1, 3).reshape(kt, tile, qt * tile)
    a, g = row_exchange(a, block)
    a = a.reshape(2, 2, 2, 4, a.shape[2], a.shape[3])
    product = jnp.einsum("ckhypj,cyhkjn->pn", a, g, preferred_element_type=jnp.float32)
    return residual_in + product


def solution(mesh):
    devices = mesh.devices.reshape(ROW_SPLIT + COL_SPLIT)
    fine = Mesh(devices, ROW_AXES + COL_AXES)
    row, col = ROW_AXES, COL_AXES
    in_specs = (P(row, col), P(row, col, None, None), P(row, col), P(row, col))
    out_specs = P(row, col)
    return jax.shard_map(body, mesh=fine, in_specs=in_specs, out_specs=out_specs, check_vma=False)
```

```python
import functools
import math

import jax
import jax.numpy as jnp
from jax import lax
from jax.experimental import pallas as pl
from jax.experimental.pallas import tpu as pltpu
from jax.sharding import Mesh
from jax.sharding import PartitionSpec as P

ROW_AXES = ("z_hi", "y", "core")
COL_AXES = ("z_lo", "x")
ROW_SPLIT = (2, 4, 2)
COL_SPLIT = (8, 4)
MESH = pl.DeviceIdType.MESH


def _index(axes, sizes):
    index = 0
    for axis, size in zip(axes, sizes):
        index = index * size + lax.axis_index(axis)
    return index


def _device(axes, sizes, flat):
    coords = {}
    for axis, size in reversed(list(zip(axes, sizes))):
        coords[axis] = lax.rem(flat, size)
        flat = flat // size
    return coords


def exchange_kernel(groups, *refs):
    count = len(groups)
    x_refs, o_refs = refs[:count], refs[count:2 * count]
    send_sem, recv_sem, line_send, line_recv, local_sem = refs[2 * count:]
    own = []
    for g, (kind, axes, sizes) in enumerate(groups):
        me = _index(axes, sizes)
        src = x_refs[g].at[me] if kind == "a2a" else x_refs[g]
        copy = pltpu.make_async_copy(src, o_refs[g].at[me], local_sem.at[g])
        copy.start()
        own.append(copy)
    barrier = pltpu.get_barrier_semaphore()
    total = 0
    for kind, axes, sizes in groups:
        n = math.prod(sizes)
        if kind == "line":
            axis = axes[0]
            i = lax.axis_index(axis)

            @pl.when(i > 0)
            def _():
                pl.semaphore_signal(barrier, inc=1, device_id={axis: i - 1}, device_id_type=MESH)

            @pl.when(i < n - 1)
            def _():
                pl.semaphore_signal(barrier, inc=1, device_id={axis: i + 1}, device_id_type=MESH)

            total = total + (i > 0).astype(jnp.int32) + (i < n - 1).astype(jnp.int32)
            continue
        me = _index(axes, sizes)
        for j in range(1, n):
            peer = _device(axes, sizes, lax.rem(me + j, n))
            pl.semaphore_signal(barrier, inc=1, device_id=peer, device_id_type=MESH)
        total = total + (n - 1)
    pl.semaphore_wait(barrier, total)
    copies = []
    slot = 0
    direct = [(g, grp) for g, grp in enumerate(groups) if grp[0] != "line"]
    longest = max([math.prod(sizes) for _, (_, _, sizes) in direct], default=1)
    for j in range(1, longest):
        for g, (kind, axes, sizes) in direct:
            n = math.prod(sizes)
            if j >= n:
                continue
            me = _index(axes, sizes)
            flat = lax.rem(me + j, n)
            src = x_refs[g] if kind == "gather" else x_refs[g].at[flat]
            copy = pltpu.make_async_remote_copy(
                src_ref=src,
                dst_ref=o_refs[g].at[me],
                send_sem=send_sem.at[slot],
                recv_sem=recv_sem.at[slot],
                device_id=_device(axes, sizes, flat),
                device_id_type=MESH,
            )
            copy.start()
            copies.append(copy)
            slot += 1
    for g, (kind, axes, sizes) in enumerate(groups):
        if kind == "line":
            _line_ring(axes[0], sizes[0], x_refs[g], o_refs[g], line_send, line_recv)
    for copy in copies + own:
        copy.wait()


def _line_ring(axis, n, x_ref, o_ref, send_sem, recv_sem):
    i = lax.axis_index(axis)

    def hop(step, direction):
        if direction == 0:
            origin, target, alive = i - step + 1, i + 1, (i + 1 <= n - 1) & (i - step + 1 >= 0)
        else:
            origin, target, alive = i + step - 1, i - 1, (i >= 1) & (i + step - 1 <= n - 1)
        origin = jnp.clip(origin, 0, n - 1)
        src = x_ref if step == 1 else o_ref.at[origin]
        copy = pltpu.make_async_remote_copy(
            src_ref=src,
            dst_ref=o_ref.at[origin],
            send_sem=send_sem.at[direction, step - 1],
            recv_sem=recv_sem.at[direction, step - 1],
            device_id={axis: jnp.clip(target, 0, n - 1)},
            device_id_type=MESH,
        )
        return copy, alive

    def arrival(step, direction):
        origin = i - step if direction == 0 else i + step
        alive = (origin >= 0) & (origin <= n - 1)
        copy = pltpu.make_async_copy(
            x_ref, o_ref.at[jnp.clip(origin, 0, n - 1)], recv_sem.at[direction, step - 1]
        )
        return copy, alive

    sent = []
    for step in range(1, n):
        for direction in (0, 1):
            copy, alive = hop(step, direction)
            pl.when(alive)(copy.start)
            sent.append((copy, alive))
        for direction in (0, 1):
            copy, alive = arrival(step, direction)
            pl.when(alive)(copy.wait)
    for copy, alive in sent:
        pl.when(alive)(copy.wait_send)


def exchange(xs, groups, cid):
    xs, groups = list(xs), list(groups)
    slots = max(1, sum(math.prod(sizes) - 1 for kind, _, sizes in groups if kind != "line"))
    line = max([sizes[0] for kind, _, sizes in groups if kind == "line"], default=2)
    shapes = []
    for x, (kind, _, sizes) in zip(xs, groups):
        shapes.append(x.shape if kind == "a2a" else (math.prod(sizes),) + x.shape)
    nbytes = sum(2 * math.prod(shape) * x.dtype.itemsize for x, shape in zip(xs, shapes))
    outs = pl.pallas_call(
        functools.partial(exchange_kernel, groups),
        out_shape=[jax.ShapeDtypeStruct(shape, x.dtype) for x, shape in zip(xs, shapes)],
        in_specs=[pl.BlockSpec(memory_space=pl.ANY)] * len(xs),
        out_specs=[pl.BlockSpec(memory_space=pl.ANY)] * len(xs),
        scratch_shapes=[
            pltpu.SemaphoreType.DMA((slots,)),
            pltpu.SemaphoreType.DMA((slots,)),
            pltpu.SemaphoreType.DMA((2, line - 1)),
            pltpu.SemaphoreType.DMA((2, line - 1)),
            pltpu.SemaphoreType.DMA((len(xs),)),
        ],
        compiler_params=pltpu.CompilerParams(collective_id=cid, has_side_effects=True),
        cost_estimate=pl.CostEstimate(flops=0, transcendentals=0, bytes_accessed=nbytes),
        name="exchange_" + "_".join("".join(axes) for _, axes, _ in groups),
    )(*xs)
    return list(outs)


def gather(xs, groups, cid):
    return exchange(xs, [("gather", (axis,), (n,)) for axis, n in groups], cid)


def row_kernel(a_ref, b_ref, ao_ref, g_ref, *sems):
    xd_send, xd_recv, xr_send, xr_recv, z_send, z_recv, yd_send, yd_recv, yr_send, yr_recv, c_send, c_recv = sems[:12]
    local_sem, piece_send, relay_send, forward_send = sems[12:16]
    nx, ny = COL_SPLIT[1], ROW_SPLIT[1]
    h, y, c = lax.axis_index("z_hi"), lax.axis_index("y"), lax.axis_index("core")
    xi = lax.axis_index("x")
    up_x, dn_x, far_x = lax.rem(xi + 1, nx), lax.rem(xi + nx - 1, nx), lax.rem(xi + 2, nx)
    up_y, dn_y, far_y = lax.rem(y + 1, ny), lax.rem(y + ny - 1, ny), lax.rem(y + 2, ny)
    core, zpeer = {"core": 1 - c}, {"z_hi": 1 - h}
    peers = [zpeer, core, {"y": up_y}, {"y": dn_y}, {"x": up_x}, {"x": dn_x}]
    barrier = pltpu.get_barrier_semaphore()
    for peer in peers:
        pl.semaphore_signal(barrier, inc=1, device_id=peer, device_id_type=MESH)
    pl.semaphore_wait(barrier, len(peers))
    own = [
        pltpu.make_async_copy(a_ref, ao_ref.at[xi], local_sem.at[0]),
        pltpu.make_async_copy(b_ref, g_ref.at[c, y, h], local_sem.at[1]),
    ]
    for copy in own:
        copy.start()
    sent = []
    half_a = a_ref.shape[0] // 2
    a_half = (pl.ds(0, half_a), pl.ds(half_a, half_a))

    def send(src, dst, ssem, rsem, peer):
        copy = pltpu.make_async_remote_copy(
            src_ref=src, dst_ref=dst, send_sem=ssem, recv_sem=rsem, device_id=peer, device_id_type=MESH
        )
        copy.start()
        sent.append(copy)

    def arrive(dst, rsem, like):
        pltpu.make_async_copy(like, dst, rsem).wait()

    def to_core(yy, hh):
        for half in range(2):
            block = g_ref.at[c, yy, hh, half]
            send(block, block, c_send.at[yy, hh, half], c_recv.at[yy, hh, half], core)

    send(a_ref, ao_ref.at[xi], xd_send.at[0], xd_recv.at[0], {"x": up_x})
    send(a_ref, ao_ref.at[xi], xd_send.at[1], xd_recv.at[1], {"x": dn_x})
    rows = b_ref.shape[1] // 2
    pieces = [(kk, pl.ds(part * rows, rows)) for kk in range(2) for part in range(2)]
    for p, (kk, span) in enumerate(pieces):
        send(b_ref.at[kk, span], g_ref.at[c, y, h, kk, span], z_send.at[p], z_recv.at[p], zpeer)
    send(b_ref, g_ref.at[c, y, h], yd_send.at[0, 0], yd_recv.at[0, 0], {"y": up_y})
    send(b_ref, g_ref.at[c, y, h], yd_send.at[1, 0], yd_recv.at[1, 0], {"y": dn_y})
    for half in range(2):
        send(b_ref.at[half], g_ref.at[c, y, h, half], c_send.at[y, h, half], c_recv.at[y, h, half], core)
    arrive(ao_ref.at[dn_x], xd_recv.at[0], a_ref)
    src = ao_ref.at[dn_x, a_half[0]]
    send(src, src, xr_send.at[0], xr_recv.at[0], {"x": up_x})
    arrive(ao_ref.at[up_x], xd_recv.at[1], a_ref)
    src = ao_ref.at[up_x, a_half[1]]
    send(src, src, xr_send.at[1], xr_recv.at[1], {"x": dn_x})
    for p, (kk, span) in enumerate(pieces):
        src = g_ref.at[c, y, 1 - h, kk, span]
        arrive(src, z_recv.at[p], b_ref.at[kk, span])
        send(src, src, yd_send.at[0, 1 + p], yd_recv.at[0, 1 + p], {"y": up_y})
        send(src, src, yd_send.at[1, 1 + p], yd_recv.at[1, 1 + p], {"y": dn_y})
        send(src, src, piece_send.at[p], c_recv.at[y, 1 - h, kk], core)
    for direction, origin, target in ((0, dn_y, up_y), (1, up_y, dn_y)):
        arrive(g_ref.at[c, origin, h], yd_recv.at[direction, 0], b_ref)
        src = g_ref.at[c, origin, h, direction]
        send(src, src, yr_send.at[direction, 0], yr_recv.at[direction, 0], {"y": target})
        to_core(origin, h)
        for p, (kk, span) in enumerate(pieces):
            blk = g_ref.at[c, origin, 1 - h, kk, span]
            arrive(blk, yd_recv.at[direction, 1 + p], b_ref.at[kk, span])
            if kk == direction:
                send(blk, blk, relay_send.at[direction, p % 2], yr_recv.at[direction, 1], {"y": target})
            send(blk, blk, forward_send.at[direction, p], c_recv.at[origin, 1 - h, kk], core)
    for k, hh in ((0, h), (1, 1 - h)):
        for direction in range(2):
            arrive(g_ref.at[c, far_y, hh, direction], yr_recv.at[direction, k], b_ref.at[0])
        to_core(far_y, hh)
    arrive(ao_ref.at[far_x, a_half[0]], xr_recv.at[0], a_ref.at[a_half[0]])
    arrive(ao_ref.at[far_x, a_half[1]], xr_recv.at[1], a_ref.at[a_half[1]])
    for yy in range(ny):
        for hh in range(ROW_SPLIT[0]):
            for half in range(2):
                arrive(g_ref.at[1 - c, yy, hh, half], c_recv.at[yy, hh, half], b_ref.at[0])
    for copy in sent:
        copy.wait_send()
    for copy in own:
        copy.wait()


def row_exchange(a, b):
    nx = COL_SPLIT[1]
    nh, ny, nc = ROW_SPLIT
    a_out = (nx,) + a.shape
    b_out = (nc, ny, nh) + b.shape
    nbytes = 2 * (math.prod(a_out) + math.prod(b_out)) * a.dtype.itemsize
    sem_shapes = [(2,), (2,), (4,), (2, 5), (2, 2), (ny, nh, 2)]
    ao, g = pl.pallas_call(
        row_kernel,
        out_shape=[jax.ShapeDtypeStruct(a_out, a.dtype), jax.ShapeDtypeStruct(b_out, b.dtype)],
        in_specs=[pl.BlockSpec(memory_space=pl.ANY)] * 2,
        out_specs=[pl.BlockSpec(memory_space=pl.ANY)] * 2,
        scratch_shapes=[pltpu.SemaphoreType.DMA(shape) for shape in sem_shapes for _ in range(2)]
        + [pltpu.SemaphoreType.DMA(shape) for shape in ((2,), (4,), (2, 2), (2, 4))],
        compiler_params=pltpu.CompilerParams(collective_id=7, has_side_effects=True),
        cost_estimate=pl.CostEstimate(flops=0, transcendentals=0, bytes_accessed=nbytes),
        name="row_exchange",
    )(a, b)
    return ao, g


def body(amplitudes, packed_tiles, tile_ids, residual_in):
    per_device = packed_tiles.shape[1]
    tile = packed_tiles.shape[2]
    col_count = COL_SPLIT[0] * COL_SPLIT[1]
    own_ids = tile_ids[0]
    target_col = own_ids // per_device
    chooser = (jnp.arange(col_count)[:, None] == target_col[None, :]).astype(jnp.bfloat16)
    outgoing = jnp.einsum("sl,lij->sij", chooser, packed_tiles[0], preferred_element_type=jnp.float32)
    outgoing = outgoing.astype(jnp.bfloat16)
    incoming, a, all_ids = exchange(
        [outgoing, amplitudes, tile_ids],
        [("a2a", COL_AXES, COL_SPLIT), ("line", ("z_lo",), (COL_SPLIT[0],)), ("gather", COL_AXES, COL_SPLIT)],
        3,
    )
    me = _index(COL_AXES, COL_SPLIT)
    all_ids = all_ids.reshape(col_count, per_device)
    mine = (all_ids // per_device) == me
    tags = jnp.sum(jnp.where(mine, all_ids % per_device + 1, 0), axis=1)
    unpack = (jnp.arange(per_device)[:, None] + 1 == tags[None, :]).astype(jnp.bfloat16)
    unpacked = jnp.einsum(
        "ps,sij->pij", unpack, incoming, preferred_element_type=jnp.float32
    ).astype(jnp.bfloat16)
    kt = 2
    qt = per_device // kt
    block = unpacked.reshape(kt, qt, tile, tile).transpose(0, 2, 1, 3).reshape(kt, tile, qt * tile)
    a, g = row_exchange(a, block)
    a = a.reshape(2, 2, 2, 4, a.shape[2], a.shape[3])
    product = jnp.einsum("ckhypj,cyhkjn->pn", a, g, preferred_element_type=jnp.float32)
    return residual_in + product


def solution(mesh):
    devices = mesh.devices.reshape(ROW_SPLIT + COL_SPLIT)
    fine = Mesh(devices, ROW_AXES + COL_AXES)
    row, col = ROW_AXES, COL_AXES
    in_specs = (P(row, col), P(row, col, None, None), P(row, col), P(row, col))
    out_specs = P(row, col)
    return jax.shard_map(body, mesh=fine, in_specs=in_specs, out_specs=out_specs, check_vma=False)
```

```python
import functools
import math

import jax
import jax.numpy as jnp
from jax import lax
from jax.experimental import pallas as pl
from jax.experimental.pallas import tpu as pltpu
from jax.sharding import Mesh
from jax.sharding import PartitionSpec as P

ROW_AXES = ("z_hi", "y", "core")
COL_AXES = ("z_lo", "x")
ROW_SPLIT = (2, 4, 2)
COL_SPLIT = (8, 4)
MESH = pl.DeviceIdType.MESH


def _index(axes, sizes):
    index = 0
    for axis, size in zip(axes, sizes):
        index = index * size + lax.axis_index(axis)
    return index


def _device(axes, sizes, flat):
    coords = {}
    for axis, size in reversed(list(zip(axes, sizes))):
        coords[axis] = lax.rem(flat, size)
        flat = flat // size
    return coords


def exchange_kernel(groups, *refs):
    count = len(groups)
    x_refs, o_refs = refs[:count], refs[count:2 * count]
    send_sem, recv_sem, line_send, line_recv, local_sem = refs[2 * count:]
    own = []
    for g, (kind, axes, sizes) in enumerate(groups):
        me = _index(axes, sizes)
        src = x_refs[g].at[me] if kind == "a2a" else x_refs[g]
        copy = pltpu.make_async_copy(src, o_refs[g].at[me], local_sem.at[g])
        copy.start()
        own.append(copy)
    barrier = pltpu.get_barrier_semaphore()
    total = 0
    for kind, axes, sizes in groups:
        n = math.prod(sizes)
        if kind == "line":
            axis = axes[0]
            i = lax.axis_index(axis)

            @pl.when(i > 0)
            def _():
                pl.semaphore_signal(barrier, inc=1, device_id={axis: i - 1}, device_id_type=MESH)

            @pl.when(i < n - 1)
            def _():
                pl.semaphore_signal(barrier, inc=1, device_id={axis: i + 1}, device_id_type=MESH)

            total = total + (i > 0).astype(jnp.int32) + (i < n - 1).astype(jnp.int32)
            continue
        me = _index(axes, sizes)
        for j in range(1, n):
            peer = _device(axes, sizes, lax.rem(me + j, n))
            pl.semaphore_signal(barrier, inc=1, device_id=peer, device_id_type=MESH)
        total = total + (n - 1)
    pl.semaphore_wait(barrier, total)
    copies = []
    slot = 0
    direct = [(g, grp) for g, grp in enumerate(groups) if grp[0] != "line"]
    longest = max([math.prod(sizes) for _, (_, _, sizes) in direct], default=1)
    for j in range(1, longest):
        for g, (kind, axes, sizes) in direct:
            n = math.prod(sizes)
            if j >= n:
                continue
            me = _index(axes, sizes)
            flat = lax.rem(me + j, n)
            src = x_refs[g] if kind == "gather" else x_refs[g].at[flat]
            copy = pltpu.make_async_remote_copy(
                src_ref=src,
                dst_ref=o_refs[g].at[me],
                send_sem=send_sem.at[slot],
                recv_sem=recv_sem.at[slot],
                device_id=_device(axes, sizes, flat),
                device_id_type=MESH,
            )
            copy.start()
            copies.append(copy)
            slot += 1
    for g, (kind, axes, sizes) in enumerate(groups):
        if kind == "line":
            _line_ring(axes[0], sizes[0], x_refs[g], o_refs[g], line_send, line_recv)
    for copy in copies + own:
        copy.wait()


def _line_ring(axis, n, x_ref, o_ref, send_sem, recv_sem):
    i = lax.axis_index(axis)

    def hop(step, direction):
        if direction == 0:
            origin, target, alive = i - step + 1, i + 1, (i + 1 <= n - 1) & (i - step + 1 >= 0)
        else:
            origin, target, alive = i + step - 1, i - 1, (i >= 1) & (i + step - 1 <= n - 1)
        origin = jnp.clip(origin, 0, n - 1)
        src = x_ref if step == 1 else o_ref.at[origin]
        copy = pltpu.make_async_remote_copy(
            src_ref=src,
            dst_ref=o_ref.at[origin],
            send_sem=send_sem.at[direction, step - 1],
            recv_sem=recv_sem.at[direction, step - 1],
            device_id={axis: jnp.clip(target, 0, n - 1)},
            device_id_type=MESH,
        )
        return copy, alive

    def arrival(step, direction):
        origin = i - step if direction == 0 else i + step
        alive = (origin >= 0) & (origin <= n - 1)
        copy = pltpu.make_async_copy(
            x_ref, o_ref.at[jnp.clip(origin, 0, n - 1)], recv_sem.at[direction, step - 1]
        )
        return copy, alive

    sent = []
    for step in range(1, n):
        for direction in (0, 1):
            copy, alive = hop(step, direction)
            pl.when(alive)(copy.start)
            sent.append((copy, alive))
        for direction in (0, 1):
            copy, alive = arrival(step, direction)
            pl.when(alive)(copy.wait)
    for copy, alive in sent:
        pl.when(alive)(copy.wait_send)


def exchange(xs, groups, cid):
    xs, groups = list(xs), list(groups)
    slots = max(1, sum(math.prod(sizes) - 1 for kind, _, sizes in groups if kind != "line"))
    line = max([sizes[0] for kind, _, sizes in groups if kind == "line"], default=2)
    shapes = []
    for x, (kind, _, sizes) in zip(xs, groups):
        shapes.append(x.shape if kind == "a2a" else (math.prod(sizes),) + x.shape)
    nbytes = sum(2 * math.prod(shape) * x.dtype.itemsize for x, shape in zip(xs, shapes))
    outs = pl.pallas_call(
        functools.partial(exchange_kernel, groups),
        out_shape=[jax.ShapeDtypeStruct(shape, x.dtype) for x, shape in zip(xs, shapes)],
        in_specs=[pl.BlockSpec(memory_space=pl.ANY)] * len(xs),
        out_specs=[pl.BlockSpec(memory_space=pl.ANY)] * len(xs),
        scratch_shapes=[
            pltpu.SemaphoreType.DMA((slots,)),
            pltpu.SemaphoreType.DMA((slots,)),
            pltpu.SemaphoreType.DMA((2, line - 1)),
            pltpu.SemaphoreType.DMA((2, line - 1)),
            pltpu.SemaphoreType.DMA((len(xs),)),
        ],
        compiler_params=pltpu.CompilerParams(collective_id=cid, has_side_effects=True),
        cost_estimate=pl.CostEstimate(flops=0, transcendentals=0, bytes_accessed=nbytes),
        name="exchange_" + "_".join("".join(axes) for _, axes, _ in groups),
    )(*xs)
    return list(outs)


def gather(xs, groups, cid):
    return exchange(xs, [("gather", (axis,), (n,)) for axis, n in groups], cid)


def row_kernel(a_ref, b_ref, ao_ref, g_ref, *sems):
    xd_send, xd_recv, xr_send, xr_recv, z_send, z_recv, yd_send, yd_recv, yr_send, yr_recv, c_send, c_recv = sems[:12]
    local_sem, piece_send = sems[12], sems[13]
    nx, ny = COL_SPLIT[1], ROW_SPLIT[1]
    h, y, c = lax.axis_index("z_hi"), lax.axis_index("y"), lax.axis_index("core")
    xi = lax.axis_index("x")
    up_x, dn_x, far_x = lax.rem(xi + 1, nx), lax.rem(xi + nx - 1, nx), lax.rem(xi + 2, nx)
    up_y, dn_y, far_y = lax.rem(y + 1, ny), lax.rem(y + ny - 1, ny), lax.rem(y + 2, ny)
    core, zpeer = {"core": 1 - c}, {"z_hi": 1 - h}
    peers = [zpeer, core, {"y": up_y}, {"y": dn_y}, {"x": up_x}, {"x": dn_x}]
    barrier = pltpu.get_barrier_semaphore()
    for peer in peers:
        pl.semaphore_signal(barrier, inc=1, device_id=peer, device_id_type=MESH)
    pl.semaphore_wait(barrier, len(peers))
    own = [
        pltpu.make_async_copy(a_ref, ao_ref.at[xi], local_sem.at[0]),
        pltpu.make_async_copy(b_ref, g_ref.at[c, y, h], local_sem.at[1]),
    ]
    for copy in own:
        copy.start()
    sent = []
    half_a = a_ref.shape[0] // 2
    a_half = (pl.ds(0, half_a), pl.ds(half_a, half_a))

    def send(src, dst, ssem, rsem, peer):
        copy = pltpu.make_async_remote_copy(
            src_ref=src, dst_ref=dst, send_sem=ssem, recv_sem=rsem, device_id=peer, device_id_type=MESH
        )
        copy.start()
        sent.append(copy)

    def arrive(dst, rsem, like):
        pltpu.make_async_copy(like, dst, rsem).wait()

    def to_core(yy, hh):
        for half in range(2):
            block = g_ref.at[c, yy, hh, half]
            send(block, block, c_send.at[yy, hh, half], c_recv.at[yy, hh, half], core)

    send(a_ref, ao_ref.at[xi], xd_send.at[0], xd_recv.at[0], {"x": up_x})
    send(a_ref, ao_ref.at[xi], xd_send.at[1], xd_recv.at[1], {"x": dn_x})
    rows = b_ref.shape[1] // 4
    pieces = [(kk, pl.ds(part * rows, rows)) for kk in range(2) for part in range(4)]
    for p, (kk, span) in enumerate(pieces):
        send(b_ref.at[kk, span], g_ref.at[c, y, h, kk, span], z_send.at[p], z_recv.at[p], zpeer)
    send(b_ref, g_ref.at[c, y, h], yd_send.at[0, 0], yd_recv.at[0, 0], {"y": up_y})
    send(b_ref, g_ref.at[c, y, h], yd_send.at[1, 0], yd_recv.at[1, 0], {"y": dn_y})
    for half in range(2):
        send(b_ref.at[half], g_ref.at[c, y, h, half], c_send.at[y, h, half], c_recv.at[y, h, half], core)
    arrive(ao_ref.at[dn_x], xd_recv.at[0], a_ref)
    src = ao_ref.at[dn_x, a_half[0]]
    send(src, src, xr_send.at[0], xr_recv.at[0], {"x": up_x})
    arrive(ao_ref.at[up_x], xd_recv.at[1], a_ref)
    src = ao_ref.at[up_x, a_half[1]]
    send(src, src, xr_send.at[1], xr_recv.at[1], {"x": dn_x})
    for p, (kk, span) in enumerate(pieces):
        src = g_ref.at[c, y, 1 - h, kk, span]
        arrive(src, z_recv.at[p], b_ref.at[kk, span])
        send(src, src, yd_send.at[0, 1 + p], yd_recv.at[0, 1], {"y": up_y})
        send(src, src, yd_send.at[1, 1 + p], yd_recv.at[1, 1], {"y": dn_y})
        send(src, src, piece_send.at[p], c_recv.at[y, 1 - h, kk], core)
    for direction, origin, target in ((0, dn_y, up_y), (1, up_y, dn_y)):
        for k, hh in ((0, h), (1, 1 - h)):
            arrive(g_ref.at[c, origin, hh], yd_recv.at[direction, k], b_ref)
            src = g_ref.at[c, origin, hh, direction]
            send(src, src, yr_send.at[direction, k], yr_recv.at[direction, k], {"y": target})
            to_core(origin, hh)
    for k, hh in ((0, h), (1, 1 - h)):
        for direction in range(2):
            arrive(g_ref.at[c, far_y, hh, direction], yr_recv.at[direction, k], b_ref.at[0])
        to_core(far_y, hh)
    arrive(ao_ref.at[far_x, a_half[0]], xr_recv.at[0], a_ref.at[a_half[0]])
    arrive(ao_ref.at[far_x, a_half[1]], xr_recv.at[1], a_ref.at[a_half[1]])
    for yy in range(ny):
        for hh in range(ROW_SPLIT[0]):
            for half in range(2):
                arrive(g_ref.at[1 - c, yy, hh, half], c_recv.at[yy, hh, half], b_ref.at[0])
    for copy in sent:
        copy.wait_send()
    for copy in own:
        copy.wait()


def row_exchange(a, b):
    nx = COL_SPLIT[1]
    nh, ny, nc = ROW_SPLIT
    a_out = (nx,) + a.shape
    b_out = (nc, ny, nh) + b.shape
    nbytes = 2 * (math.prod(a_out) + math.prod(b_out)) * a.dtype.itemsize
    sem_shapes = [(2,), (2,), (8,), (2, 9), (2, 2), (ny, nh, 2)]
    ao, g = pl.pallas_call(
        row_kernel,
        out_shape=[jax.ShapeDtypeStruct(a_out, a.dtype), jax.ShapeDtypeStruct(b_out, b.dtype)],
        in_specs=[pl.BlockSpec(memory_space=pl.ANY)] * 2,
        out_specs=[pl.BlockSpec(memory_space=pl.ANY)] * 2,
        scratch_shapes=[pltpu.SemaphoreType.DMA(shape) for shape in sem_shapes for _ in range(2)]
        + [pltpu.SemaphoreType.DMA((2,)), pltpu.SemaphoreType.DMA((8,))],
        compiler_params=pltpu.CompilerParams(collective_id=7, has_side_effects=True),
        cost_estimate=pl.CostEstimate(flops=0, transcendentals=0, bytes_accessed=nbytes),
        name="row_exchange",
    )(a, b)
    return ao, g


def body(amplitudes, packed_tiles, tile_ids, residual_in):
    per_device = packed_tiles.shape[1]
    tile = packed_tiles.shape[2]
    col_count = COL_SPLIT[0] * COL_SPLIT[1]
    own_ids = tile_ids[0]
    target_col = own_ids // per_device
    chooser = (jnp.arange(col_count)[:, None] == target_col[None, :]).astype(jnp.bfloat16)
    outgoing = jnp.einsum("sl,lij->sij", chooser, packed_tiles[0], preferred_element_type=jnp.float32)
    outgoing = outgoing.astype(jnp.bfloat16)
    incoming, a, all_ids = exchange(
        [outgoing, amplitudes, tile_ids],
        [("a2a", COL_AXES, COL_SPLIT), ("line", ("z_lo",), (COL_SPLIT[0],)), ("gather", COL_AXES, COL_SPLIT)],
        3,
    )
    me = _index(COL_AXES, COL_SPLIT)
    all_ids = all_ids.reshape(col_count, per_device)
    mine = (all_ids // per_device) == me
    tags = jnp.sum(jnp.where(mine, all_ids % per_device + 1, 0), axis=1)
    unpack = (jnp.arange(per_device)[:, None] + 1 == tags[None, :]).astype(jnp.bfloat16)
    unpacked = jnp.einsum(
        "ps,sij->pij", unpack, incoming, preferred_element_type=jnp.float32
    ).astype(jnp.bfloat16)
    kt = 2
    qt = per_device // kt
    block = unpacked.reshape(kt, qt, tile, tile).transpose(0, 2, 1, 3).reshape(kt, tile, qt * tile)
    a, g = row_exchange(a, block)
    a = a.reshape(2, 2, 2, 4, a.shape[2], a.shape[3])
    product = jnp.einsum("ckhypj,cyhkjn->pn", a, g, preferred_element_type=jnp.float32)
    return residual_in + product


def solution(mesh):
    devices = mesh.devices.reshape(ROW_SPLIT + COL_SPLIT)
    fine = Mesh(devices, ROW_AXES + COL_AXES)
    row, col = ROW_AXES, COL_AXES
    in_specs = (P(row, col), P(row, col, None, None), P(row, col), P(row, col))
    out_specs = P(row, col)
    return jax.shard_map(body, mesh=fine, in_specs=in_specs, out_specs=out_specs, check_vma=False)
```

```python
import functools
import math

import jax
import jax.numpy as jnp
from jax import lax
from jax.experimental import pallas as pl
from jax.experimental.pallas import tpu as pltpu
from jax.sharding import Mesh
from jax.sharding import PartitionSpec as P

ROW_AXES = ("z_hi", "y", "core")
COL_AXES = ("z_lo", "x")
ROW_SPLIT = (2, 4, 2)
COL_SPLIT = (8, 4)
MESH = pl.DeviceIdType.MESH


def _index(axes, sizes):
    index = 0
    for axis, size in zip(axes, sizes):
        index = index * size + lax.axis_index(axis)
    return index


def _device(axes, sizes, flat):
    coords = {}
    for axis, size in reversed(list(zip(axes, sizes))):
        coords[axis] = lax.rem(flat, size)
        flat = flat // size
    return coords


def exchange_kernel(groups, *refs):
    count = len(groups)
    x_refs, o_refs = refs[:count], refs[count:2 * count]
    send_sem, recv_sem, line_send, line_recv, local_sem = refs[2 * count:]
    own = []
    for g, (kind, axes, sizes) in enumerate(groups):
        me = _index(axes, sizes)
        src = x_refs[g].at[me] if kind == "a2a" else x_refs[g]
        copy = pltpu.make_async_copy(src, o_refs[g].at[me], local_sem.at[g])
        copy.start()
        own.append(copy)
    barrier = pltpu.get_barrier_semaphore()
    total = 0
    for kind, axes, sizes in groups:
        n = math.prod(sizes)
        if kind == "line":
            axis = axes[0]
            i = lax.axis_index(axis)

            @pl.when(i > 0)
            def _():
                pl.semaphore_signal(barrier, inc=1, device_id={axis: i - 1}, device_id_type=MESH)

            @pl.when(i < n - 1)
            def _():
                pl.semaphore_signal(barrier, inc=1, device_id={axis: i + 1}, device_id_type=MESH)

            total = total + (i > 0).astype(jnp.int32) + (i < n - 1).astype(jnp.int32)
            continue
        me = _index(axes, sizes)
        for j in range(1, n):
            peer = _device(axes, sizes, lax.rem(me + j, n))
            pl.semaphore_signal(barrier, inc=1, device_id=peer, device_id_type=MESH)
        total = total + (n - 1)
    pl.semaphore_wait(barrier, total)
    copies = []
    slot = 0
    direct = [(g, grp) for g, grp in enumerate(groups) if grp[0] != "line"]
    longest = max([math.prod(sizes) for _, (_, _, sizes) in direct], default=1)
    for j in range(1, longest):
        for g, (kind, axes, sizes) in direct:
            n = math.prod(sizes)
            if j >= n:
                continue
            me = _index(axes, sizes)
            flat = lax.rem(me + j, n)
            src = x_refs[g] if kind == "gather" else x_refs[g].at[flat]
            copy = pltpu.make_async_remote_copy(
                src_ref=src,
                dst_ref=o_refs[g].at[me],
                send_sem=send_sem.at[slot],
                recv_sem=recv_sem.at[slot],
                device_id=_device(axes, sizes, flat),
                device_id_type=MESH,
            )
            copy.start()
            copies.append(copy)
            slot += 1
    for g, (kind, axes, sizes) in enumerate(groups):
        if kind == "line":
            _line_ring(axes[0], sizes[0], x_refs[g], o_refs[g], line_send, line_recv)
    for copy in copies + own:
        copy.wait()


def _line_ring(axis, n, x_ref, o_ref, send_sem, recv_sem):
    i = lax.axis_index(axis)

    def hop(step, direction):
        if direction == 0:
            origin, target, alive = i - step + 1, i + 1, (i + 1 <= n - 1) & (i - step + 1 >= 0)
        else:
            origin, target, alive = i + step - 1, i - 1, (i >= 1) & (i + step - 1 <= n - 1)
        origin = jnp.clip(origin, 0, n - 1)
        src = x_ref if step == 1 else o_ref.at[origin]
        copy = pltpu.make_async_remote_copy(
            src_ref=src,
            dst_ref=o_ref.at[origin],
            send_sem=send_sem.at[direction, step - 1],
            recv_sem=recv_sem.at[direction, step - 1],
            device_id={axis: jnp.clip(target, 0, n - 1)},
            device_id_type=MESH,
        )
        return copy, alive

    def arrival(step, direction):
        origin = i - step if direction == 0 else i + step
        alive = (origin >= 0) & (origin <= n - 1)
        copy = pltpu.make_async_copy(
            x_ref, o_ref.at[jnp.clip(origin, 0, n - 1)], recv_sem.at[direction, step - 1]
        )
        return copy, alive

    sent = []
    for step in range(1, n):
        for direction in (0, 1):
            copy, alive = hop(step, direction)
            pl.when(alive)(copy.start)
            sent.append((copy, alive))
        for direction in (0, 1):
            copy, alive = arrival(step, direction)
            pl.when(alive)(copy.wait)
    for copy, alive in sent:
        pl.when(alive)(copy.wait_send)


def exchange(xs, groups, cid):
    xs, groups = list(xs), list(groups)
    slots = max(1, sum(math.prod(sizes) - 1 for kind, _, sizes in groups if kind != "line"))
    line = max([sizes[0] for kind, _, sizes in groups if kind == "line"], default=2)
    shapes = []
    for x, (kind, _, sizes) in zip(xs, groups):
        shapes.append(x.shape if kind == "a2a" else (math.prod(sizes),) + x.shape)
    nbytes = sum(2 * math.prod(shape) * x.dtype.itemsize for x, shape in zip(xs, shapes))
    outs = pl.pallas_call(
        functools.partial(exchange_kernel, groups),
        out_shape=[jax.ShapeDtypeStruct(shape, x.dtype) for x, shape in zip(xs, shapes)],
        in_specs=[pl.BlockSpec(memory_space=pl.ANY)] * len(xs),
        out_specs=[pl.BlockSpec(memory_space=pl.ANY)] * len(xs),
        scratch_shapes=[
            pltpu.SemaphoreType.DMA((slots,)),
            pltpu.SemaphoreType.DMA((slots,)),
            pltpu.SemaphoreType.DMA((2, line - 1)),
            pltpu.SemaphoreType.DMA((2, line - 1)),
            pltpu.SemaphoreType.DMA((len(xs),)),
        ],
        compiler_params=pltpu.CompilerParams(collective_id=cid, has_side_effects=True),
        cost_estimate=pl.CostEstimate(flops=0, transcendentals=0, bytes_accessed=nbytes),
        name="exchange_" + "_".join("".join(axes) for _, axes, _ in groups),
    )(*xs)
    return list(outs)


def gather(xs, groups, cid):
    return exchange(xs, [("gather", (axis,), (n,)) for axis, n in groups], cid)


def row_kernel(a_ref, b_ref, ao_ref, g_ref, *sems):
    xd_send, xd_recv, xr_send, xr_recv, z_send, z_recv, yd_send, yd_recv, yr_send, yr_recv, c_send, c_recv = sems[:12]
    local_sem, piece_send = sems[12], sems[13]
    nx, ny = COL_SPLIT[1], ROW_SPLIT[1]
    h, y, c = lax.axis_index("z_hi"), lax.axis_index("y"), lax.axis_index("core")
    xi = lax.axis_index("x")
    up_x, dn_x, far_x = lax.rem(xi + 1, nx), lax.rem(xi + nx - 1, nx), lax.rem(xi + 2, nx)
    up_y, dn_y, far_y = lax.rem(y + 1, ny), lax.rem(y + ny - 1, ny), lax.rem(y + 2, ny)
    core, zpeer = {"core": 1 - c}, {"z_hi": 1 - h}
    peers = [zpeer, core, {"y": up_y}, {"y": dn_y}, {"x": up_x}, {"x": dn_x}]
    barrier = pltpu.get_barrier_semaphore()
    for peer in peers:
        pl.semaphore_signal(barrier, inc=1, device_id=peer, device_id_type=MESH)
    pl.semaphore_wait(barrier, len(peers))
    own = [
        pltpu.make_async_copy(a_ref, ao_ref.at[xi], local_sem.at[0]),
        pltpu.make_async_copy(b_ref, g_ref.at[c, y, h], local_sem.at[1]),
    ]
    for copy in own:
        copy.start()
    sent = []
    half_a = a_ref.shape[0] // 2
    a_half = (pl.ds(0, half_a), pl.ds(half_a, half_a))

    def send(src, dst, ssem, rsem, peer):
        copy = pltpu.make_async_remote_copy(
            src_ref=src, dst_ref=dst, send_sem=ssem, recv_sem=rsem, device_id=peer, device_id_type=MESH
        )
        copy.start()
        sent.append(copy)

    def arrive(dst, rsem, like):
        pltpu.make_async_copy(like, dst, rsem).wait()

    def to_core(yy, hh):
        for half in range(2):
            block = g_ref.at[c, yy, hh, half]
            send(block, block, c_send.at[yy, hh, half], c_recv.at[yy, hh, half], core)

    send(a_ref, ao_ref.at[xi], xd_send.at[0], xd_recv.at[0], {"x": up_x})
    send(a_ref, ao_ref.at[xi], xd_send.at[1], xd_recv.at[1], {"x": dn_x})
    rows = b_ref.shape[1] // 4
    pieces = [(kk, pl.ds(part * rows, rows)) for kk in range(2) for part in range(4)]
    for p, (kk, span) in enumerate(pieces):
        send(b_ref.at[kk, span], g_ref.at[c, y, h, kk, span], z_send.at[p], z_recv.at[p], zpeer)
    send(b_ref, g_ref.at[c, y, h], yd_send.at[0, 0], yd_recv.at[0, 0], {"y": up_y})
    send(b_ref, g_ref.at[c, y, h], yd_send.at[1, 0], yd_recv.at[1, 0], {"y": dn_y})
    for half in range(2):
        send(b_ref.at[half], g_ref.at[c, y, h, half], c_send.at[y, h, half], c_recv.at[y, h, half], core)
    arrive(ao_ref.at[dn_x], xd_recv.at[0], a_ref)
    src = ao_ref.at[dn_x, a_half[0]]
    send(src, src, xr_send.at[0], xr_recv.at[0], {"x": up_x})
    arrive(ao_ref.at[up_x], xd_recv.at[1], a_ref)
    src = ao_ref.at[up_x, a_half[1]]
    send(src, src, xr_send.at[1], xr_recv.at[1], {"x": dn_x})
    for p, (kk, span) in enumerate(pieces):
        src = g_ref.at[c, y, 1 - h, kk, span]
        arrive(src, z_recv.at[p], b_ref.at[kk, span])
        send(src, src, yd_send.at[0, 1 + p], yd_recv.at[0, 1], {"y": up_y})
        send(src, src, yd_send.at[1, 1 + p], yd_recv.at[1, 1], {"y": dn_y})
        send(src, src, piece_send.at[p], c_recv.at[y, 1 - h, kk], core)
    for direction, origin, target in ((0, dn_y, up_y), (1, up_y, dn_y)):
        for k, hh in ((0, h), (1, 1 - h)):
            arrive(g_ref.at[c, origin, hh], yd_recv.at[direction, k], b_ref)
            src = g_ref.at[c, origin, hh, direction]
            send(src, src, yr_send.at[direction, k], yr_recv.at[direction, k], {"y": target})
            to_core(origin, hh)
    for k, hh in ((0, h), (1, 1 - h)):
        for direction in range(2):
            arrive(g_ref.at[c, far_y, hh, direction], yr_recv.at[direction, k], b_ref.at[0])
        to_core(far_y, hh)
    arrive(ao_ref.at[far_x, a_half[0]], xr_recv.at[0], a_ref.at[a_half[0]])
    arrive(ao_ref.at[far_x, a_half[1]], xr_recv.at[1], a_ref.at[a_half[1]])
    for yy in range(ny):
        for hh in range(ROW_SPLIT[0]):
            for half in range(2):
                arrive(g_ref.at[1 - c, yy, hh, half], c_recv.at[yy, hh, half], b_ref.at[0])
    for copy in sent:
        copy.wait_send()
    for copy in own:
        copy.wait()


def row_exchange(a, b):
    nx = COL_SPLIT[1]
    nh, ny, nc = ROW_SPLIT
    a_out = (nx,) + a.shape
    b_out = (nc, ny, nh) + b.shape
    nbytes = 2 * (math.prod(a_out) + math.prod(b_out)) * a.dtype.itemsize
    sem_shapes = [(2,), (2,), (8,), (2, 9), (2, 2), (ny, nh, 2)]
    ao, g = pl.pallas_call(
        row_kernel,
        out_shape=[jax.ShapeDtypeStruct(a_out, a.dtype), jax.ShapeDtypeStruct(b_out, b.dtype)],
        in_specs=[pl.BlockSpec(memory_space=pl.ANY)] * 2,
        out_specs=[pl.BlockSpec(memory_space=pl.ANY)] * 2,
        scratch_shapes=[pltpu.SemaphoreType.DMA(shape) for shape in sem_shapes for _ in range(2)]
        + [pltpu.SemaphoreType.DMA((2,)), pltpu.SemaphoreType.DMA((8,))],
        compiler_params=pltpu.CompilerParams(collective_id=7, has_side_effects=True),
        cost_estimate=pl.CostEstimate(flops=0, transcendentals=0, bytes_accessed=nbytes),
        name="row_exchange",
    )(a, b)
    return ao, g


def body(amplitudes, packed_tiles, tile_ids, residual_in):
    per_device = packed_tiles.shape[1]
    tile = packed_tiles.shape[2]
    col_count = COL_SPLIT[0] * COL_SPLIT[1]
    own_ids = tile_ids[0]
    target_col = own_ids // per_device
    chooser = jnp.arange(col_count)[:, None] == target_col[None, :]
    source = jnp.sum(jnp.where(chooser, jnp.arange(per_device)[None, :], 0), axis=1)
    outgoing = jnp.take(packed_tiles[0], source, axis=0)
    incoming, a, all_ids = exchange(
        [outgoing, amplitudes, tile_ids],
        [("a2a", COL_AXES, COL_SPLIT), ("line", ("z_lo",), (COL_SPLIT[0],)), ("gather", COL_AXES, COL_SPLIT)],
        3,
    )
    me = _index(COL_AXES, COL_SPLIT)
    all_ids = all_ids.reshape(col_count, per_device)
    mine = (all_ids // per_device) == me
    tags = jnp.sum(jnp.where(mine, all_ids % per_device + 1, 0), axis=1)
    holds = jnp.arange(per_device)[:, None] + 1 == tags[None, :]
    slot_of = jnp.sum(jnp.where(holds, jnp.arange(col_count)[None, :], 0), axis=1)
    unpacked = jnp.take(incoming, slot_of, axis=0)
    kt = 2
    qt = per_device // kt
    block = unpacked.reshape(kt, qt, tile, tile).transpose(0, 2, 1, 3).reshape(kt, tile, qt * tile)
    a, g = row_exchange(a, block)
    a = a.reshape(2, 2, 2, 4, a.shape[2], a.shape[3])
    product = jnp.einsum("ckhypj,cyhkjn->pn", a, g, preferred_element_type=jnp.float32)
    return residual_in + product


def solution(mesh):
    devices = mesh.devices.reshape(ROW_SPLIT + COL_SPLIT)
    fine = Mesh(devices, ROW_AXES + COL_AXES)
    row, col = ROW_AXES, COL_AXES
    in_specs = (P(row, col), P(row, col, None, None), P(row, col), P(row, col))
    out_specs = P(row, col)
    return jax.shard_map(body, mesh=fine, in_specs=in_specs, out_specs=out_specs, check_vma=False)
```

```python
import functools
import math

import jax
import jax.numpy as jnp
from jax import lax
from jax.experimental import pallas as pl
from jax.experimental.pallas import tpu as pltpu
from jax.sharding import Mesh
from jax.sharding import PartitionSpec as P

ROW_AXES = ("z_hi", "y", "core")
COL_AXES = ("z_lo", "x")
ROW_SPLIT = (2, 4, 2)
COL_SPLIT = (8, 4)
MESH = pl.DeviceIdType.MESH


def _index(axes, sizes):
    index = 0
    for axis, size in zip(axes, sizes):
        index = index * size + lax.axis_index(axis)
    return index


def _device(axes, sizes, flat):
    coords = {}
    for axis, size in reversed(list(zip(axes, sizes))):
        coords[axis] = lax.rem(flat, size)
        flat = flat // size
    return coords


def exchange_kernel(groups, *refs):
    count = len(groups)
    x_refs, o_refs = refs[:count], refs[count:2 * count]
    send_sem, recv_sem, line_send, line_recv, local_sem = refs[2 * count:]
    own = []
    for g, (kind, axes, sizes) in enumerate(groups):
        me = _index(axes, sizes)
        src = x_refs[g].at[me] if kind == "a2a" else x_refs[g]
        copy = pltpu.make_async_copy(src, o_refs[g].at[me], local_sem.at[g])
        copy.start()
        own.append(copy)
    barrier = pltpu.get_barrier_semaphore()
    total = 0
    for kind, axes, sizes in groups:
        n = math.prod(sizes)
        if kind == "line":
            axis = axes[0]
            i = lax.axis_index(axis)

            @pl.when(i > 0)
            def _():
                pl.semaphore_signal(barrier, inc=1, device_id={axis: i - 1}, device_id_type=MESH)

            @pl.when(i < n - 1)
            def _():
                pl.semaphore_signal(barrier, inc=1, device_id={axis: i + 1}, device_id_type=MESH)

            total = total + (i > 0).astype(jnp.int32) + (i < n - 1).astype(jnp.int32)
            continue
        me = _index(axes, sizes)
        for j in range(1, n):
            peer = _device(axes, sizes, lax.rem(me + j, n))
            pl.semaphore_signal(barrier, inc=1, device_id=peer, device_id_type=MESH)
        total = total + (n - 1)
    pl.semaphore_wait(barrier, total)
    copies = []
    slot = 0
    direct = [(g, grp) for g, grp in enumerate(groups) if grp[0] != "line"]
    longest = max([math.prod(sizes) for _, (_, _, sizes) in direct], default=1)
    for j in range(1, longest):
        for g, (kind, axes, sizes) in direct:
            n = math.prod(sizes)
            if j >= n:
                continue
            me = _index(axes, sizes)
            flat = lax.rem(me + j, n)
            src = x_refs[g] if kind == "gather" else x_refs[g].at[flat]
            copy = pltpu.make_async_remote_copy(
                src_ref=src,
                dst_ref=o_refs[g].at[me],
                send_sem=send_sem.at[slot],
                recv_sem=recv_sem.at[slot],
                device_id=_device(axes, sizes, flat),
                device_id_type=MESH,
            )
            copy.start()
            copies.append(copy)
            slot += 1
    for g, (kind, axes, sizes) in enumerate(groups):
        if kind == "line":
            _line_ring(axes[0], sizes[0], x_refs[g], o_refs[g], line_send, line_recv)
    for copy in copies + own:
        copy.wait()


def _line_ring(axis, n, x_ref, o_ref, send_sem, recv_sem):
    i = lax.axis_index(axis)

    def hop(step, direction):
        if direction == 0:
            origin, target, alive = i - step + 1, i + 1, (i + 1 <= n - 1) & (i - step + 1 >= 0)
        else:
            origin, target, alive = i + step - 1, i - 1, (i >= 1) & (i + step - 1 <= n - 1)
        origin = jnp.clip(origin, 0, n - 1)
        src = x_ref if step == 1 else o_ref.at[origin]
        copy = pltpu.make_async_remote_copy(
            src_ref=src,
            dst_ref=o_ref.at[origin],
            send_sem=send_sem.at[direction, step - 1],
            recv_sem=recv_sem.at[direction, step - 1],
            device_id={axis: jnp.clip(target, 0, n - 1)},
            device_id_type=MESH,
        )
        return copy, alive

    def arrival(step, direction):
        origin = i - step if direction == 0 else i + step
        alive = (origin >= 0) & (origin <= n - 1)
        copy = pltpu.make_async_copy(
            x_ref, o_ref.at[jnp.clip(origin, 0, n - 1)], recv_sem.at[direction, step - 1]
        )
        return copy, alive

    sent = []
    for step in range(1, n):
        for direction in (0, 1):
            copy, alive = hop(step, direction)
            pl.when(alive)(copy.start)
            sent.append((copy, alive))
        for direction in (0, 1):
            copy, alive = arrival(step, direction)
            pl.when(alive)(copy.wait)
    for copy, alive in sent:
        pl.when(alive)(copy.wait_send)


def exchange(xs, groups, cid):
    xs, groups = list(xs), list(groups)
    slots = max(1, sum(math.prod(sizes) - 1 for kind, _, sizes in groups if kind != "line"))
    line = max([sizes[0] for kind, _, sizes in groups if kind == "line"], default=2)
    shapes = []
    for x, (kind, _, sizes) in zip(xs, groups):
        shapes.append(x.shape if kind == "a2a" else (math.prod(sizes),) + x.shape)
    nbytes = sum(2 * math.prod(shape) * x.dtype.itemsize for x, shape in zip(xs, shapes))
    outs = pl.pallas_call(
        functools.partial(exchange_kernel, groups),
        out_shape=[jax.ShapeDtypeStruct(shape, x.dtype) for x, shape in zip(xs, shapes)],
        in_specs=[pl.BlockSpec(memory_space=pl.ANY)] * len(xs),
        out_specs=[pl.BlockSpec(memory_space=pl.ANY)] * len(xs),
        scratch_shapes=[
            pltpu.SemaphoreType.DMA((slots,)),
            pltpu.SemaphoreType.DMA((slots,)),
            pltpu.SemaphoreType.DMA((2, line - 1)),
            pltpu.SemaphoreType.DMA((2, line - 1)),
            pltpu.SemaphoreType.DMA((len(xs),)),
        ],
        compiler_params=pltpu.CompilerParams(collective_id=cid, has_side_effects=True),
        cost_estimate=pl.CostEstimate(flops=0, transcendentals=0, bytes_accessed=nbytes),
        name="exchange_" + "_".join("".join(axes) for _, axes, _ in groups),
    )(*xs)
    return list(outs)


def gather(xs, groups, cid):
    return exchange(xs, [("gather", (axis,), (n,)) for axis, n in groups], cid)


def row_kernel(a_ref, b_ref, ao_ref, g_ref, *sems):
    xd_send, xd_recv, xr_send, xr_recv, z_send, z_recv, yd_send, yd_recv, yr_send, yr_recv, c_send, c_recv = sems[:12]
    local_sem, piece_send = sems[12], sems[13]
    nx, ny = COL_SPLIT[1], ROW_SPLIT[1]
    h, y, c = lax.axis_index("z_hi"), lax.axis_index("y"), lax.axis_index("core")
    xi = lax.axis_index("x")
    up_x, dn_x, far_x = lax.rem(xi + 1, nx), lax.rem(xi + nx - 1, nx), lax.rem(xi + 2, nx)
    up_y, dn_y, far_y = lax.rem(y + 1, ny), lax.rem(y + ny - 1, ny), lax.rem(y + 2, ny)
    core, zpeer = {"core": 1 - c}, {"z_hi": 1 - h}
    peers = [zpeer, core, {"y": up_y}, {"y": dn_y}, {"x": up_x}, {"x": dn_x}]
    barrier = pltpu.get_barrier_semaphore()
    for peer in peers:
        pl.semaphore_signal(barrier, inc=1, device_id=peer, device_id_type=MESH)
    pl.semaphore_wait(barrier, len(peers))
    own = [
        pltpu.make_async_copy(a_ref, ao_ref.at[xi], local_sem.at[0]),
        pltpu.make_async_copy(b_ref, g_ref.at[c, y, h], local_sem.at[1]),
    ]
    for copy in own:
        copy.start()
    sent = []
    half_a = a_ref.shape[0] // 2
    a_half = (pl.ds(0, half_a), pl.ds(half_a, half_a))

    def send(src, dst, ssem, rsem, peer):
        copy = pltpu.make_async_remote_copy(
            src_ref=src, dst_ref=dst, send_sem=ssem, recv_sem=rsem, device_id=peer, device_id_type=MESH
        )
        copy.start()
        sent.append(copy)

    def arrive(dst, rsem, like):
        pltpu.make_async_copy(like, dst, rsem).wait()

    def to_core(yy, hh):
        for half in range(2):
            block = g_ref.at[c, yy, hh, half]
            send(block, block, c_send.at[yy, hh, half], c_recv.at[yy, hh, half], core)

    rows = b_ref.shape[1] // 4
    pieces = [(kk, pl.ds(part * rows, rows)) for kk in range(2) for part in range(4)]
    for p, (kk, span) in enumerate(pieces):
        send(b_ref.at[kk, span], g_ref.at[c, y, h, kk, span], z_send.at[p], z_recv.at[p], zpeer)
    send(a_ref, ao_ref.at[xi], xd_send.at[0], xd_recv.at[0], {"x": up_x})
    send(a_ref, ao_ref.at[xi], xd_send.at[1], xd_recv.at[1], {"x": dn_x})
    send(b_ref, g_ref.at[c, y, h], yd_send.at[0, 0], yd_recv.at[0, 0], {"y": up_y})
    send(b_ref, g_ref.at[c, y, h], yd_send.at[1, 0], yd_recv.at[1, 0], {"y": dn_y})
    for half in range(2):
        send(b_ref.at[half], g_ref.at[c, y, h, half], c_send.at[y, h, half], c_recv.at[y, h, half], core)
    arrive(ao_ref.at[dn_x], xd_recv.at[0], a_ref)
    src = ao_ref.at[dn_x, a_half[0]]
    send(src, src, xr_send.at[0], xr_recv.at[0], {"x": up_x})
    arrive(ao_ref.at[up_x], xd_recv.at[1], a_ref)
    src = ao_ref.at[up_x, a_half[1]]
    send(src, src, xr_send.at[1], xr_recv.at[1], {"x": dn_x})
    for p, (kk, span) in enumerate(pieces):
        src = g_ref.at[c, y, 1 - h, kk, span]
        arrive(src, z_recv.at[p], b_ref.at[kk, span])
        send(src, src, yd_send.at[0, 1 + p], yd_recv.at[0, 1], {"y": up_y})
        send(src, src, yd_send.at[1, 1 + p], yd_recv.at[1, 1], {"y": dn_y})
        send(src, src, piece_send.at[p], c_recv.at[y, 1 - h, kk], core)
    for direction, origin, target in ((0, dn_y, up_y), (1, up_y, dn_y)):
        for k, hh in ((0, h), (1, 1 - h)):
            arrive(g_ref.at[c, origin, hh], yd_recv.at[direction, k], b_ref)
            src = g_ref.at[c, origin, hh, direction]
            send(src, src, yr_send.at[direction, k], yr_recv.at[direction, k], {"y": target})
            to_core(origin, hh)
    for k, hh in ((0, h), (1, 1 - h)):
        for direction in range(2):
            arrive(g_ref.at[c, far_y, hh, direction], yr_recv.at[direction, k], b_ref.at[0])
        to_core(far_y, hh)
    arrive(ao_ref.at[far_x, a_half[0]], xr_recv.at[0], a_ref.at[a_half[0]])
    arrive(ao_ref.at[far_x, a_half[1]], xr_recv.at[1], a_ref.at[a_half[1]])
    for yy in range(ny):
        for hh in range(ROW_SPLIT[0]):
            for half in range(2):
                arrive(g_ref.at[1 - c, yy, hh, half], c_recv.at[yy, hh, half], b_ref.at[0])
    for copy in sent:
        copy.wait_send()
    for copy in own:
        copy.wait()


def row_exchange(a, b):
    nx = COL_SPLIT[1]
    nh, ny, nc = ROW_SPLIT
    a_out = (nx,) + a.shape
    b_out = (nc, ny, nh) + b.shape
    nbytes = 2 * (math.prod(a_out) + math.prod(b_out)) * a.dtype.itemsize
    sem_shapes = [(2,), (2,), (8,), (2, 9), (2, 2), (ny, nh, 2)]
    ao, g = pl.pallas_call(
        row_kernel,
        out_shape=[jax.ShapeDtypeStruct(a_out, a.dtype), jax.ShapeDtypeStruct(b_out, b.dtype)],
        in_specs=[pl.BlockSpec(memory_space=pl.ANY)] * 2,
        out_specs=[pl.BlockSpec(memory_space=pl.ANY)] * 2,
        scratch_shapes=[pltpu.SemaphoreType.DMA(shape) for shape in sem_shapes for _ in range(2)]
        + [pltpu.SemaphoreType.DMA((2,)), pltpu.SemaphoreType.DMA((8,))],
        compiler_params=pltpu.CompilerParams(collective_id=7, has_side_effects=True),
        cost_estimate=pl.CostEstimate(flops=0, transcendentals=0, bytes_accessed=nbytes),
        name="row_exchange",
    )(a, b)
    return ao, g


def body(amplitudes, packed_tiles, tile_ids, residual_in):
    per_device = packed_tiles.shape[1]
    tile = packed_tiles.shape[2]
    col_count = COL_SPLIT[0] * COL_SPLIT[1]
    own_ids = tile_ids[0]
    target_col = own_ids // per_device
    chooser = (jnp.arange(col_count)[:, None] == target_col[None, :]).astype(jnp.bfloat16)
    outgoing = jnp.einsum("sl,lij->sij", chooser, packed_tiles[0], preferred_element_type=jnp.float32)
    outgoing = outgoing.astype(jnp.bfloat16)
    incoming, a, all_ids = exchange(
        [outgoing, amplitudes, tile_ids],
        [("a2a", COL_AXES, COL_SPLIT), ("line", ("z_lo",), (COL_SPLIT[0],)), ("gather", COL_AXES, COL_SPLIT)],
        3,
    )
    me = _index(COL_AXES, COL_SPLIT)
    all_ids = all_ids.reshape(col_count, per_device)
    mine = (all_ids // per_device) == me
    tags = jnp.sum(jnp.where(mine, all_ids % per_device + 1, 0), axis=1)
    unpack = (jnp.arange(per_device)[:, None] + 1 == tags[None, :]).astype(jnp.bfloat16)
    unpacked = jnp.einsum(
        "ps,sij->pij", unpack, incoming, preferred_element_type=jnp.float32
    ).astype(jnp.bfloat16)
    kt = 2
    qt = per_device // kt
    block = unpacked.reshape(kt, qt, tile, tile).transpose(0, 2, 1, 3).reshape(kt, tile, qt * tile)
    a, g = row_exchange(a, block)
    a = a.reshape(2, 2, 2, 4, a.shape[2], a.shape[3])
    product = jnp.einsum("ckhypj,cyhkjn->pn", a, g, preferred_element_type=jnp.float32)
    return residual_in + product


def solution(mesh):
    devices = mesh.devices.reshape(ROW_SPLIT + COL_SPLIT)
    fine = Mesh(devices, ROW_AXES + COL_AXES)
    row, col = ROW_AXES, COL_AXES
    in_specs = (P(row, col), P(row, col, None, None), P(row, col), P(row, col))
    out_specs = P(row, col)
    return jax.shard_map(body, mesh=fine, in_specs=in_specs, out_specs=out_specs, check_vma=False)
```
